256 devices in a mesh: dp: 32 (over x, z), section: 8 (over y, core).
Axes of the slice: x: 4, y: 4, z: 8, core: 2. Of those that a mesh axis runs over, the one named last changes fastest.
Arguments:
- tap_maps: bfloat16 [4, 2, 4096, 3200], P(None, None, ('dp', 'section')), may hold values from -6 to 6
- lateral_weight: bfloat16 [8, 3200, 768], P('section', 'dp'), may hold values from -0.109375 to 0.109375
- conv_weight: bfloat16 [8, 6912, 768], P('section'), may hold values from -0.078125 to 0.078125
- classifier: bfloat16 [768, 150], replicated, may hold values from -0.875 to 0.875
- tile_counts: int32 [32, 2], P('dp'), may hold values from 1 to 2, as said below
- labels: int32 [2, 4096], P(None, 'dp'), may hold values from 0 to 149
Outputs:
- conv_grad: float32 [8, 6912, 768], P('section', 'dp')
- lateral_grad: float32 [8, 3200, 768], P('section', 'dp')
The draws below stay inside these ranges and needn't reach their ends.
Inputs may be any that keep to these rules, and one draw needn't show every extreme that they name: `tile_counts`: some entry equals 2.
All inputs are finite; a program needn't handle non-finite values.
Results may differ from the reference program's by a relative error of at most 0.035.
Values may be sent and summed in bfloat16 or wider, within the bound.
A program may use at most 128 MiB of HBM per device.

```python
import jax
import jax.numpy as jnp
from jax import lax

WIDTH = 3200
CHANNELS = 768
CLASSES = 150
TAPS = 4
MICRO = 2
TILE_CAP = 2
BAND_ROWS = 1
BAND_COLS = 64
PIXELS = 128
ALL_PIXELS = 4096
N_DP = 32
N_SECTION = 8


def draw_tile_counts(key, part):
    first_key, second_key = jax.random.split(key)
    counts = jax.random.randint(first_key, (N_DP * MICRO,), 1, TILE_CAP + 1)
    target = jax.random.randint(second_key, (), 0, N_DP * MICRO)
    counts = jnp.where(jnp.arange(N_DP * MICRO) == target, TILE_CAP, counts)
    return counts.reshape(N_DP, MICRO).astype(jnp.int32)


def plant(drawn, own_key, low, largest):
    longest = drawn.shape.index(max(drawn.shape))
    spots = []
    for shift in (0, 1):
        where = [jax.random.randint(jax.random.fold_in(own_key, axis), (), 0, length) for axis, length in enumerate(drawn.shape)]
        where[longest] = (where[longest] + shift) % drawn.shape[longest]
        spots.append(tuple(where))
    return drawn.at[spots[0]].set(low).at[spots[1]].set(largest)


def block_levels(key, shape, shards, least, largest):
    def one(dim, shards_of):
        heights = jax.random.uniform(jax.random.fold_in(jax.random.fold_in(key, 6), dim), (shards_of,), jnp.float32, least / len(shards), largest / len(shards))
        return jnp.repeat(jnp.exp(heights), shape[dim] // shards_of).reshape((-1,) + (1,) * (len(shape) - dim - 1))

    level = one(*shards[0])
    for cut in shards[1:]:
        level = level * one(*cut)
    return level


def noise(rng, dims, deviation, most, shards=(), kind=jnp.bfloat16):
    gain = block_levels(rng, dims, shards, -0.22, 0.18) if shards else 1.0
    values = jax.random.normal(rng, dims, jnp.float32) * deviation * gain
    return jnp.minimum(jnp.maximum(values, -most), most).astype(kind)


def setup_inputs(seed: int = 0) -> dict:
    streams_of = jax.random.split(jax.random.key(seed), 7)
    tap_maps = noise(streams_of[0], (TAPS, MICRO, ALL_PIXELS, WIDTH), 1.0, 6.0, ((2, 256),))
    lateral_weight = noise(streams_of[1], (N_SECTION, WIDTH, CHANNELS), WIDTH ** -0.5, 0.109375, ((0, 8), (1, 32)))
    conv_weight = noise(streams_of[2], (N_SECTION, 9 * CHANNELS, CHANNELS), (9 * CHANNELS) ** -0.5, 0.078125, ((0, 8),))
    classifier = noise(streams_of[3], (CHANNELS, CLASSES), (CHANNELS // 16) ** -0.5, 0.875)
    tile_counts = draw_tile_counts(jax.random.fold_in(streams_of[6], 71), 0)
    labels = plant(jax.random.randint(streams_of[5], (MICRO, ALL_PIXELS), 0, CLASSES), jax.random.fold_in(streams_of[5], 1), 0, CLASSES - 1).astype(jnp.int32)
    return {"tap_maps": tap_maps, "lateral_weight": lateral_weight, "conv_weight": conv_weight, "classifier": classifier, "tile_counts": tile_counts, "labels": labels}


def neighbour_shifts():
    return [(row_shift, col_shift) for row_shift in (-1, 0, 1) for col_shift in (-1, 0, 1)]


def to_tiles(field):
    micros = field.shape[0]
    chans = field.shape[-1]
    grid = field.reshape(micros, N_DP, TILE_CAP, BAND_ROWS, BAND_COLS, chans).transpose(0, 2, 1, 3, 4, 5)
    return grid.reshape(micros * TILE_CAP, N_DP * BAND_ROWS, BAND_COLS, chans)


def from_tiles(grid, micros):
    chans = grid.shape[-1]
    parts = grid.reshape(micros, TILE_CAP, N_DP, BAND_ROWS, BAND_COLS, chans).transpose(0, 2, 1, 3, 4, 5)
    return parts.reshape(micros, N_DP * PIXELS, chans)


def to_columns(field):
    micros = field.shape[0]
    grid = to_tiles(field)
    rows = grid.shape[1]
    padded = jnp.pad(grid, ((0, 0), (1, 1), (1, 1), (0, 0)))
    pieces = [padded[:, 1 + rs:1 + rs + rows, 1 + cs:1 + cs + BAND_COLS, :] for rs, cs in neighbour_shifts()]
    return from_tiles(jnp.concatenate(pieces, axis=-1), micros)


def from_columns(grads):
    micros = grads.shape[0]
    chans = grads.shape[-1] // 9
    grid = to_tiles(grads)
    rows = grid.shape[1]
    grid = grid.reshape(grid.shape[0], rows, BAND_COLS, 9, chans)
    total = jnp.zeros((grid.shape[0], rows + 2, BAND_COLS + 2, chans), jnp.float32)
    for offset, (rs, cs) in enumerate(neighbour_shifts()):
        total = total + jnp.pad(grid[:, :, :, offset, :].astype(jnp.float32), ((0, 0), (1 + rs, 1 - rs), (1 + cs, 1 - cs), (0, 0)))
    return from_tiles(total[:, 1:-1, 1:-1, :], micros)


def group_partials(left, right):
    depth = left.shape[-1]
    lefts = left.reshape(MICRO, N_DP, PIXELS, depth).transpose(1, 0, 2, 3).reshape(N_DP, MICRO * PIXELS, depth)
    rights = right.reshape(MICRO, N_DP, PIXELS, CHANNELS).transpose(1, 0, 2, 3).reshape(N_DP, MICRO * PIXELS, CHANNELS)

    def one_group(pair):
        return jnp.dot(pair[0].T, pair[1], preferred_element_type=jnp.float32).astype(jnp.bfloat16)

    rounded = lax.map(one_group, (lefts, rights))
    rounded = lax.optimization_barrier(rounded)
    return jnp.sum(rounded.astype(jnp.float32), axis=0)


def reference(tap_maps, lateral_weight, conv_weight, classifier, tile_counts, labels):
    band = BAND_ROWS * BAND_COLS
    npix = labels.shape[1]
    position = jnp.arange(npix)
    group = position // PIXELS
    slot = (position % PIXELS) // band
    per_count = tile_counts.T[:, group]
    valid = (slot[None, :] < per_count).astype(jnp.float32)
    pixel_weight = valid / (per_count.astype(jnp.float32) * band * N_DP * MICRO)
    activated = jnp.zeros((MICRO, npix, CHANNELS), jnp.bfloat16)
    summed_list = []
    preact_list = []
    for section in range(N_SECTION):
        level = section * TAPS // N_SECTION
        lateral = jnp.dot(tap_maps[level].reshape(-1, WIDTH), lateral_weight[section], preferred_element_type=jnp.float32).reshape(MICRO, npix, CHANNELS)
        summed = (activated.astype(jnp.float32) + lateral).astype(jnp.bfloat16)
        columns = to_columns(summed)
        preact = jnp.dot(columns.reshape(-1, 9 * CHANNELS), conv_weight[section], preferred_element_type=jnp.float32).reshape(MICRO, npix, CHANNELS)
        activated = jax.nn.silu(preact).astype(jnp.bfloat16)
        summed_list.append(summed)
        preact_list.append(preact)
    logits = jnp.dot(activated.reshape(-1, CHANNELS), classifier, preferred_element_type=jnp.float32).reshape(MICRO, npix, CLASSES)
    expo = jnp.exp(logits)
    probs = expo / jnp.sum(expo, axis=-1, keepdims=True)
    onehot = (labels[:, :, None] == jnp.arange(CLASSES)[None, None, :]).astype(jnp.float32)
    grad_logits = ((probs - onehot) * pixel_weight[:, :, None]).astype(jnp.bfloat16)
    grad_out = jnp.dot(grad_logits.reshape(-1, CLASSES), classifier.T, preferred_element_type=jnp.float32).reshape(MICRO, npix, CHANNELS)
    conv_grads = [None] * N_SECTION
    lateral_grads = [None] * N_SECTION
    for section in range(N_SECTION - 1, -1, -1):
        level = section * TAPS // N_SECTION
        preact = preact_list[section]
        sigma = jax.nn.sigmoid(preact)
        grad_pre = (grad_out * sigma * (1.0 + preact * (1.0 - sigma))).astype(jnp.bfloat16)
        columns = to_columns(summed_list[section])
        conv_grads[section] = group_partials(columns, grad_pre)
        grad_cols = jnp.dot(grad_pre.reshape(-1, CHANNELS), conv_weight[section].T, preferred_element_type=jnp.float32).reshape(MICRO, npix, 9 * CHANNELS)
        grad_in = from_columns(grad_cols).astype(jnp.bfloat16)
        lateral_grads[section] = group_partials(tap_maps[level], grad_in)
        grad_out = grad_in.astype(jnp.float32)
    return jnp.stack(conv_grads), jnp.stack(lateral_grads)
```

```python
import jax
import jax.numpy as jnp
from jax import lax
from jax.experimental import pallas as pl
from jax.experimental.pallas import tpu as pltpu
from jax.sharding import PartitionSpec as P

MESH = pl.DeviceIdType.MESH
F32 = jnp.float32
BF16 = jnp.bfloat16
NZ = 8
NX = 4
COLS = 64
ROWS = 4
PIX = ROWS * COLS
CH = 768
CK = 256
NCH = CH // CK
KPAD = 112
GROUPS = NX * NZ
KW = KPAD * GROUPS
SECTIONS = 8
CLASSES = 150
CPAD = 256


def nt(a, b):
    return lax.dot_general(a, b, (((1,), (1,)), ((), ())), preferred_element_type=F32)


def tn(a, b):
    return lax.dot_general(a, b, (((0,), (0,)), ((), ())), preferred_element_type=F32)


def nn(a, b):
    return jnp.dot(a, b, preferred_element_type=F32)


def head_kernel(
    taps_hbm, wl_hbm, w_hbm, cls_ref, oh_hbm, conv_out, lat_out,
    taps, wl, w, lateral, ext, xin, xout, gin, gsout, gx, dsilu, acc, gpv, rim_out, rim_in, oh, cg, lg,
    local_sem, tap_send, tap_recv, oh_send, oh_recv, x_send, x_recv, halo_send, halo_recv,
    g_send, g_recv, rim_send, rim_recv, out_sem,
):
    dp = lax.axis_index("dp")
    s = lax.axis_index("section")
    x, z = dp // NZ, dp % NZ
    odd = x % 2
    half = (z % 2 + odd) % 2
    image = z // 2
    has_up = jnp.logical_not(jnp.logical_and(half == 0, x == 0))
    has_down = jnp.logical_not(jnp.logical_and(half == 1, x == NX - 1))
    pair = dp + 1 - 2 * (z % 2)
    up = jnp.where(half == 1, pair, dp - NZ)
    down = jnp.where(half == 0, pair, dp + NZ)
    src_half = z // 4
    is_first, is_last = s == 0, s == SECTIONS - 1

    def home(img):
        return x * NZ + 2 * img + (src_half + odd) % 2

    my_tile = s // 4
    tap_slot = (z % 4) * 4 + s % 4

    wl_copy = pltpu.make_async_copy(wl_hbm, wl, local_sem.at[0])
    w_copy = pltpu.make_async_copy(w_hbm, w, local_sem.at[1])
    wl_copy.start()
    w_copy.start()

    barrier = pltpu.get_barrier_semaphore()

    def greet(d, sec):
        pl.semaphore_signal(barrier, inc=1, device_id={"dp": d, "section": sec}, device_id_type=MESH)

    def tap_source(j):
        return x * NZ + half * 4 + j // 4, (image % 2) * 4 + j % 4

    for j in range(16):
        d, sec = tap_source(j)

        @pl.when(jnp.logical_or(d != dp, sec != s))
        def _():
            greet(d, sec)

    @pl.when(has_up)
    def _():
        greet(up, s)

    @pl.when(has_down)
    def _():
        greet(down, s)

    @pl.when(s > 0)
    def _():
        greet(dp, s - 1)

    @pl.when(s < SECTIONS - 1)
    def _():
        greet(dp, s + 1)

    @pl.when(is_last)
    def _():
        for j in range(4):
            d = x * NZ + half * 4 + j

            @pl.when(d != dp)
            def _():
                greet(d, s)

    def tap_target(k):
        level, micro, core = k // 4, (k // 2) % 2, k % 2
        return home(2 * micro + my_tile), 2 * level + core

    need = jnp.int32(0)
    for k in range(16):
        d, sec = tap_target(k)
        need += jnp.logical_or(d != dp, sec != s).astype(jnp.int32)
    for flag in (has_up, has_down, s > 0, s < SECTIONS - 1):
        need += flag.astype(jnp.int32)
    for img in range(4):
        need += jnp.logical_and(is_last, home(img) != dp).astype(jnp.int32)
    pl.semaphore_wait(barrier, need)

    def tap_rows(j):
        return taps.at[pl.ds(pl.multiple_of((j // 4) * COLS + (j % 4) * 16, 16), 16), :]

    def tap_copy(k):
        d, sec = tap_target(k)
        return pltpu.make_async_remote_copy(
            src_ref=taps_hbm.at[k // 2], dst_ref=tap_rows(tap_slot),
            send_sem=tap_send.at[k], recv_sem=tap_recv.at[tap_slot],
            device_id={"dp": d, "section": sec}, device_id_type=MESH,
        )

    def tap_local(k):
        return pltpu.make_async_copy(taps_hbm.at[k // 2], tap_rows(tap_slot), tap_recv.at[tap_slot])

    for k in range(16):
        d, sec = tap_target(k)
        other = jnp.logical_or(d != dp, sec != s)

        @pl.when(other)
        def _():
            tap_copy(k).start()

        @pl.when(jnp.logical_not(other))
        def _():
            tap_local(k).start()

    def oh_rows(r):
        return oh.at[pl.ds(pl.multiple_of(r * COLS, COLS), COLS), :]

    def oh_src(img):
        return oh_hbm.at[img // 2, pl.ds((img % 2) * COLS, COLS), :]

    def oh_copy(img):
        return pltpu.make_async_remote_copy(
            src_ref=oh_src(img), dst_ref=oh_rows(z % 4),
            send_sem=oh_send.at[img], recv_sem=oh_recv.at[z % 4],
            device_id={"dp": home(img), "section": s}, device_id_type=MESH,
        )

    @pl.when(is_last)
    def _():
        for img in range(4):
            @pl.when(home(img) != dp)
            def _():
                oh_copy(img).start()

            @pl.when(home(img) == dp)
            def _():
                pltpu.make_async_copy(oh_src(img), oh_rows(z % 4), oh_recv.at[z % 4]).start()

    @pl.when(jnp.logical_not(has_up))
    def _():
        ext[0:COLS, :] = jnp.zeros((COLS, CH), BF16)

    @pl.when(jnp.logical_not(has_down))
    def _():
        ext[COLS + PIX:, :] = jnp.zeros((COLS, CH), BF16)

    for j in range(16):
        pltpu.make_async_copy(tap_rows(j), tap_rows(j), tap_recv.at[j]).wait()
    wl_copy.wait()

    for n in range(NCH):
        lateral[:, n * CK:(n + 1) * CK] = nn(taps[...], wl[:, n * CK:(n + 1) * CK])
    w_copy.wait()

    def lanes(c):
        return pl.ds(c * CK, CK)

    def x_copy(c):
        return pltpu.make_async_remote_copy(
            src_ref=xout.at[:, lanes(c)], dst_ref=xin.at[:, lanes(c)],
            send_sem=x_send.at[c], recv_sem=x_recv.at[c],
            device_id={"dp": dp, "section": s + 1}, device_id_type=MESH,
        )

    def halo_up(c):
        return pltpu.make_async_remote_copy(
            src_ref=ext.at[pl.ds(COLS, COLS), lanes(c)], dst_ref=ext.at[pl.ds(COLS + PIX, COLS), lanes(c)],
            send_sem=halo_send.at[0, c], recv_sem=halo_recv.at[1, c],
            device_id={"dp": up, "section": s}, device_id_type=MESH,
        )

    def halo_down(c):
        return pltpu.make_async_remote_copy(
            src_ref=ext.at[pl.ds(PIX, COLS), lanes(c)], dst_ref=ext.at[pl.ds(0, COLS), lanes(c)],
            send_sem=halo_send.at[1, c], recv_sem=halo_recv.at[0, c],
            device_id={"dp": down, "section": s}, device_id_type=MESH,
        )

    def local_wait(ref, sem):
        pltpu.make_async_copy(ref, ref, sem).wait()

    def take_x(c):
        cols = slice(c * CK, (c + 1) * CK)

        @pl.when(is_first)
        def _():
            ext[COLS:COLS + PIX, cols] = lateral[:, cols].astype(BF16)

        @pl.when(s > 0)
        def _():
            local_wait(xin.at[:, lanes(c)], x_recv.at[c])
            ext[COLS:COLS + PIX, cols] = (xin[:, cols].astype(F32) + lateral[:, cols]).astype(BF16)

        @pl.when(has_up)
        def _():
            halo_up(c).start()

        @pl.when(has_down)
        def _():
            halo_down(c).start()

    def wait_halo(c):
        @pl.when(has_up)
        def _():
            local_wait(ext.at[pl.ds(0, COLS), lanes(c)], halo_recv.at[0, c])

        @pl.when(has_down)
        def _():
            local_wait(ext.at[pl.ds(COLS + PIX, COLS), lanes(c)], halo_recv.at[1, c])

    def conv_part(c, dr, dc, ncols):
        rows = (1 + dr) * COLS
        return nn(
            ext[rows:rows + PIX, c * CK:(c + 1) * CK],
            w[(dr + 1) * 3 + dc + 1, c * CK:(c + 1) * CK, ncols],
        )

    every = slice(0, CH)

    def conv_inner(c, start):
        for dc in (-1, 0, 1):
            term = conv_part(c, 0, dc, every)
            if start:
                acc[dc + 1] = term
            else:
                acc[dc + 1] += term

    def conv_outer(c):
        for dc in (-1, 0, 1):
            acc[dc + 1] += conv_part(c, -1, dc, every) + conv_part(c, 1, dc, every)

    col = lax.broadcasted_iota(jnp.int32, (PIX, CK), 0) % COLS

    def before(v):
        return jnp.where(col == 0, 0.0, pltpu.roll(v, 1, 0))

    def after(v):
        return jnp.where(col == COLS - 1, 0.0, pltpu.roll(v, PIX - 1, 0))

    take_x(0)
    take_x(1)
    conv_inner(0, True)
    wait_halo(0)
    conv_outer(0)
    take_x(2)
    conv_inner(1, False)
    conv_inner(2, False)
    wait_halo(1)
    conv_outer(1)
    wait_halo(2)
    for n in range(NCH):
        ncols = slice(n * CK, (n + 1) * CK)
        parts = [
            acc[dc + 1, :, ncols] + conv_part(2, -1, dc, ncols) + conv_part(2, 1, dc, ncols)
            for dc in (-1, 0, 1)
        ]
        pre = before(parts[0]) + parts[1] + after(parts[2])
        sig = 1.0 / (1.0 + jnp.exp(-pre))
        xout[:, ncols] = (pre * sig).astype(BF16)

        @pl.when(s < SECTIONS - 1)
        def _():
            x_copy(n).start()

        dsilu[:, ncols] = sig * (1.0 + pre * (1.0 - sig))

    @pl.when(is_last)
    def _():
        for r in range(4):
            local_wait(oh_rows(r), oh_recv.at[r])
        logits = nn(xout[...], cls_ref[...])
        lane = lax.broadcasted_iota(jnp.int32, (PIX, CPAD), 1)
        real = lane < CLASSES
        expo = jnp.where(real, jnp.exp(logits), 0.0)
        probs = expo / jnp.sum(expo, axis=-1, keepdims=True)
        marks = oh[...].astype(F32)
        weight = jnp.sum(jnp.where(lane == CPAD - 1, marks, 0.0), axis=-1, keepdims=True)
        hot = jnp.where(real, marks, 0.0)
        grad_logits = ((probs - hot) * weight).astype(BF16)
        gx[...] = nt(grad_logits, cls_ref[...])

    def g_copy(c):
        return pltpu.make_async_remote_copy(
            src_ref=gsout.at[:, lanes(c)], dst_ref=gin.at[:, lanes(c)],
            send_sem=g_send.at[c], recv_sem=g_recv.at[c],
            device_id={"dp": dp, "section": s - 1}, device_id_type=MESH,
        )

    def rim_up(c):
        return pltpu.make_async_remote_copy(
            src_ref=rim_out.at[0, :, lanes(c)], dst_ref=rim_in.at[1, :, lanes(c)],
            send_sem=rim_send.at[0, c], recv_sem=rim_recv.at[1, c],
            device_id={"dp": up, "section": s}, device_id_type=MESH,
        )

    def rim_down(c):
        return pltpu.make_async_remote_copy(
            src_ref=rim_out.at[1, :, lanes(c)], dst_ref=rim_in.at[0, :, lanes(c)],
            send_sem=rim_send.at[1, c], recv_sem=rim_recv.at[0, c],
            device_id={"dp": down, "section": s}, device_id_type=MESH,
        )

    def take_g(c):
        cols = slice(c * CK, (c + 1) * CK)

        @pl.when(s < SECTIONS - 1)
        def _():
            local_wait(gin.at[:, lanes(c)], g_recv.at[c])
            gx[:, cols] = gin[:, cols].astype(F32)

        grad_pre = (gx[:, cols] * dsilu[:, cols]).astype(BF16).astype(F32)
        gpv[0, :, cols] = after(grad_pre).astype(BF16)
        gpv[1, :, cols] = grad_pre.astype(BF16)
        gpv[2, :, cols] = before(grad_pre).astype(BF16)

    def back_part(c, dr, krows):
        total = None
        for dc in (-1, 0, 1):
            term = nt(
                gpv[dc + 1, :, c * CK:(c + 1) * CK],
                w[(dr + 1) * 3 + dc + 1, krows, c * CK:(c + 1) * CK],
            )
            total = term if total is None else total + term
        return total

    take_g(0)
    for dr in (-1, 0, 1):
        acc[dr + 1] = back_part(0, dr, every)
    take_g(1)
    for dr in (-1, 0, 1):
        acc[dr + 1] += back_part(1, dr, every)
    take_g(2)
    for n in range(NCH):
        ncols = slice(n * CK, (n + 1) * CK)
        upper = acc[0, :, ncols] + back_part(2, -1, ncols)
        acc[0, :, ncols] = upper
        rim_out[0, :, ncols] = upper[0:COLS].astype(BF16)
        lower = acc[2, :, ncols] + back_part(2, 1, ncols)
        acc[2, :, ncols] = lower
        rim_out[1, :, ncols] = lower[PIX - COLS:].astype(BF16)

        @pl.when(has_up)
        def _():
            rim_up(n).start()

        @pl.when(has_down)
        def _():
            rim_down(n).start()

    acc[1] += back_part(2, 0, every)
    for n in range(NCH):
        ncols = slice(n * CK, (n + 1) * CK)
        acc[1, 0:PIX - COLS, ncols] += acc[0, COLS:, ncols]
        acc[1, COLS:, ncols] += acc[2, 0:PIX - COLS, ncols]

        @pl.when(has_up)
        def _():
            local_wait(rim_in.at[0, :, lanes(n)], rim_recv.at[0, n])
            acc[1, 0:COLS, ncols] += rim_in[0, :, ncols].astype(F32)

        @pl.when(has_down)
        def _():
            local_wait(rim_in.at[1, :, lanes(n)], rim_recv.at[1, n])
            acc[1, PIX - COLS:, ncols] += rim_in[1, :, ncols].astype(F32)

        gsout[:, ncols] = acc[1, :, ncols].astype(BF16)

        @pl.when(s > 0)
        def _():
            g_copy(n).start()

    def conv_grad_copy(o):
        return pltpu.make_async_copy(cg.at[o], conv_out.at[o], out_sem.at[o])

    for dr in (-1, 0, 1):
        rows = (1 + dr) * COLS
        flipped = ext[rows:rows + PIX, :].T
        for dc in (-1, 0, 1):
            o = (dr + 1) * 3 + dc + 1
            cg[o] = nn(flipped, gpv[dc + 1]).astype(BF16)
            conv_grad_copy(o).start()

    lat_copy = pltpu.make_async_copy(lg, lat_out, out_sem.at[9])

    @pl.loop(0, KW // 512)
    def _(b):
        at = pl.ds(pl.multiple_of(b * 512, 512), 512)
        lg[at, :] = nn(taps[:, at].T, gsout[...]).astype(BF16)

    lat_copy.start()

    for k in range(16):
        d, sec = tap_target(k)

        @pl.when(jnp.logical_or(d != dp, sec != s))
        def _():
            tap_copy(k).wait_send()

    @pl.when(is_last)
    def _():
        for img in range(4):
            @pl.when(home(img) != dp)
            def _():
                oh_copy(img).wait_send()

    for c in range(NCH):
        @pl.when(s < SECTIONS - 1)
        def _():
            x_copy(c).wait_send()

        @pl.when(s > 0)
        def _():
            g_copy(c).wait_send()

        @pl.when(has_up)
        def _():
            halo_up(c).wait_send()
            rim_up(c).wait_send()

        @pl.when(has_down)
        def _():
            halo_down(c).wait_send()
            rim_down(c).wait_send()

    for o in range(9):
        conv_grad_copy(o).wait()
    lat_copy.wait()


def head_call(taps, wl, w, cls, oh):
    dma = pltpu.SemaphoreType.DMA
    hbm = pl.BlockSpec(memory_space=pl.ANY)
    vmem = pl.BlockSpec(memory_space=pltpu.VMEM)
    return pl.pallas_call(
        head_kernel,
        out_shape=(
            jax.ShapeDtypeStruct((9, CH, CH), BF16),
            jax.ShapeDtypeStruct((KW, CH), BF16),
        ),
        in_specs=[hbm, hbm, hbm, vmem, hbm],
        out_specs=(hbm, hbm),
        scratch_shapes=[
            pltpu.VMEM((PIX, KW), BF16),
            pltpu.VMEM((KW, CH), BF16),
            pltpu.VMEM((9, CH, CH), BF16),
            pltpu.VMEM((PIX, CH), F32),
            pltpu.VMEM((PIX + 2 * COLS, CH), BF16),
            pltpu.VMEM((PIX, CH), BF16),
            pltpu.VMEM((PIX, CH), BF16),
            pltpu.VMEM((PIX, CH), BF16),
            pltpu.VMEM((PIX, CH), BF16),
            pltpu.VMEM((PIX, CH), F32),
            pltpu.VMEM((PIX, CH), F32),
            pltpu.VMEM((3, PIX, CH), F32),
            pltpu.VMEM((3, PIX, CH), BF16),
            pltpu.VMEM((2, COLS, CH), BF16),
            pltpu.VMEM((2, COLS, CH), BF16),
            pltpu.VMEM((PIX, CPAD), BF16),
            pltpu.VMEM((9, CH, CH), BF16),
            pltpu.VMEM((KW, CH), BF16),
            dma((2,)),
            dma((16,)),
            dma((16,)),
            dma((4,)),
            dma((4,)),
            dma((NCH,)),
            dma((NCH,)),
            dma((2, NCH)),
            dma((2, NCH)),
            dma((NCH,)),
            dma((NCH,)),
            dma((2, NCH)),
            dma((2, NCH)),
            dma((10,)),
        ],
        compiler_params=pltpu.CompilerParams(
            collective_id=0, has_side_effects=True, vmem_limit_bytes=56 << 20
        ),
    )(taps, wl, w, cls, oh)


def on_device(tap_maps, lateral_weight, conv_weight, classifier, tile_counts, labels):
    levels, micros, here, width = tap_maps.shape
    per = width // GROUPS
    classes = classifier.shape[1]
    pixels = labels.shape[1]
    grouped = tap_maps.reshape(levels * micros, here, GROUPS, per)
    taps = jnp.pad(grouped, ((0, 0), (0, 0), (0, 0), (0, KPAD - per))).reshape(levels * micros, here, KW)
    own = jnp.pad(lateral_weight[0], ((0, KPAD - per), (0, 0)))
    wl = lax.all_gather(own, "dp", axis=0, tiled=True)
    cls = jnp.pad(classifier, ((0, 0), (0, CPAD - classes)))
    counts = tile_counts[0][:, None]
    valid = (jnp.arange(pixels)[None, :] // COLS < counts).astype(F32)
    weight = valid / (counts.astype(F32) * COLS * GROUPS * micros)
    lane = jnp.arange(CPAD)
    hot = (labels[:, :, None] == lane).astype(F32)
    oh = jnp.where(lane == CPAD - 1, weight[:, :, None], hot).astype(BF16)
    conv_part, lat_part = head_call(taps, wl, conv_weight.reshape(9, CH, CH), cls, oh)
    conv_grad = lax.psum_scatter(
        conv_part.reshape(9 * CH, CH), "dp", scatter_dimension=0, tiled=True
    ).astype(F32)
    lateral_grad = lax.psum_scatter(lat_part, "dp", scatter_dimension=0, tiled=True)[:per].astype(F32)
    return (conv_grad[None], lateral_grad[None])


def solution(mesh):
    placed = (
        P(None, None, ("dp", "section"), None),
        P("section", "dp", None),
        P("section", None, None),
        P(),
        P("dp", None),
        P(None, "dp"),
    )
    return jax.shard_map(
        on_device,
        mesh=mesh,
        in_specs=placed,
        out_specs=(P("section", "dp", None), P("section", "dp", None)),
        check_vma=False,
    )
```

```python
import jax
import jax.numpy as jnp
from jax import lax
from jax.experimental import pallas as pl
from jax.experimental.pallas import tpu as pltpu
from jax.sharding import PartitionSpec as P

MESH = pl.DeviceIdType.MESH
F32 = jnp.float32
BF16 = jnp.bfloat16
NZ = 8
NX = 4
COLS = 64
ROWS = 4
PIX = ROWS * COLS
CH = 768
CK = 256
NCH = CH // CK
KPAD = 112
GROUPS = NX * NZ
KW = KPAD * GROUPS
SECTIONS = 8
WIDE = NX * PIX
CROWS = 9 * CH // GROUPS
XC, XL = CROWS * NZ, KPAD * NZ
UNIT = XC // 9
HALF = CH // 2
CLASSES = 150
CPAD = 256


def nt(a, b):
    return lax.dot_general(a, b, (((1,), (1,)), ((), ())), preferred_element_type=F32)


def tn(a, b):
    return lax.dot_general(a, b, (((0,), (0,)), ((), ())), preferred_element_type=F32)


def nn(a, b):
    return jnp.dot(a, b, preferred_element_type=F32)


def head_kernel(
    taps_hbm, wl_hbm, w_hbm, cls_ref, oh_hbm, conv_out, lat_out,
    taps, wl, w, lateral, ext, xin, xout, gin, dsilu, acc, gpv, rim_out, rim_in, oh,
    ext_all, taps_all, gp_all, gs_all, gpv_all, cols_t, taps_t, part_c, part_l, ring_c, ring_l,
    local_sem, tap_send, tap_recv, oh_send, oh_recv, x_send, x_recv, halo_send, halo_recv,
    g_send, g_recv, rim_send, rim_recv, early_sem, e_send, e_recv, a_send, a_recv, rc_send, rc_recv, rl_send, rl_recv,
):
    dp = lax.axis_index("dp")
    s = lax.axis_index("section")
    x, z = dp // NZ, dp % NZ
    odd = x % 2
    half = (z % 2 + odd) % 2
    image = z // 2
    has_up = jnp.logical_not(jnp.logical_and(half == 0, x == 0))
    has_down = jnp.logical_not(jnp.logical_and(half == 1, x == NX - 1))
    pair = dp + 1 - 2 * (z % 2)
    up = jnp.where(half == 1, pair, dp - NZ)
    down = jnp.where(half == 0, pair, dp + NZ)
    src_half = z // 4
    is_first, is_last = s == 0, s == SECTIONS - 1

    def home(img):
        return x * NZ + 2 * img + (src_half + odd) % 2

    gx = lateral
    early = s < 4
    z_next, z_prev = x * NZ + (z + 1) % NZ, x * NZ + (z + NZ - 1) % NZ

    my_tile = s // 4
    tap_slot = (z % 4) * 4 + s % 4

    wl_copy = pltpu.make_async_copy(wl_hbm, wl, local_sem.at[0])
    w_copy = pltpu.make_async_copy(w_hbm, w, local_sem.at[1])
    wl_copy.start()
    w_copy.start()

    barrier = pltpu.get_barrier_semaphore()

    def greet(d, sec):
        pl.semaphore_signal(barrier, inc=1, device_id={"dp": d, "section": sec}, device_id_type=MESH)

    def tap_source(j):
        return x * NZ + half * 4 + j // 4, (image % 2) * 4 + j % 4

    for j in range(16):
        d, sec = tap_source(j)

        @pl.when(jnp.logical_or(d != dp, sec != s))
        def _():
            greet(d, sec)

    for k in range(1, NX):
        greet((x + k) % NX * NZ + z, s)
    greet(z_next, s)
    greet(z_prev, s)

    @pl.when(has_up)
    def _():
        greet(up, s)

    @pl.when(has_down)
    def _():
        greet(down, s)

    @pl.when(s > 0)
    def _():
        greet(dp, s - 1)

    @pl.when(s < SECTIONS - 1)
    def _():
        greet(dp, s + 1)

    @pl.when(is_last)
    def _():
        for j in range(4):
            d = x * NZ + half * 4 + j

            @pl.when(d != dp)
            def _():
                greet(d, s)

    def tap_target(k):
        level, micro, core = k // 4, (k // 2) % 2, k % 2
        return home(2 * micro + my_tile), 2 * level + core

    need = jnp.int32(NX - 1 + 2)
    for k in range(16):
        d, sec = tap_target(k)
        need += jnp.logical_or(d != dp, sec != s).astype(jnp.int32)
    for flag in (has_up, has_down, s > 0, s < SECTIONS - 1):
        need += flag.astype(jnp.int32)
    for img in range(4):
        need += jnp.logical_and(is_last, home(img) != dp).astype(jnp.int32)
    pl.semaphore_wait(barrier, need)

    def tap_rows(j):
        return taps.at[pl.ds(pl.multiple_of((j // 4) * COLS + (j % 4) * 16, 16), 16), :]

    def tap_copy(k):
        d, sec = tap_target(k)
        return pltpu.make_async_remote_copy(
            src_ref=taps_hbm.at[k // 2], dst_ref=tap_rows(tap_slot),
            send_sem=tap_send.at[k], recv_sem=tap_recv.at[tap_slot],
            device_id={"dp": d, "section": sec}, device_id_type=MESH,
        )

    def tap_local(k):
        return pltpu.make_async_copy(taps_hbm.at[k // 2], tap_rows(tap_slot), tap_recv.at[tap_slot])

    for k in range(16):
        d, sec = tap_target(k)
        other = jnp.logical_or(d != dp, sec != s)

        @pl.when(other)
        def _():
            tap_copy(k).start()

        @pl.when(jnp.logical_not(other))
        def _():
            tap_local(k).start()

    def oh_rows(r):
        return oh.at[pl.ds(pl.multiple_of(r * COLS, COLS), COLS), :]

    def oh_src(img):
        return oh_hbm.at[img // 2, pl.ds((img % 2) * COLS, COLS), :]

    def oh_copy(img):
        return pltpu.make_async_remote_copy(
            src_ref=oh_src(img), dst_ref=oh_rows(z % 4),
            send_sem=oh_send.at[img], recv_sem=oh_recv.at[z % 4],
            device_id={"dp": home(img), "section": s}, device_id_type=MESH,
        )

    @pl.when(is_last)
    def _():
        for img in range(4):
            @pl.when(home(img) != dp)
            def _():
                oh_copy(img).start()

            @pl.when(home(img) == dp)
            def _():
                pltpu.make_async_copy(oh_src(img), oh_rows(z % 4), oh_recv.at[z % 4]).start()

    @pl.when(jnp.logical_not(has_up))
    def _():
        ext[0:COLS, :] = jnp.zeros((COLS, CH), BF16)

    @pl.when(jnp.logical_not(has_down))
    def _():
        ext[COLS + PIX:, :] = jnp.zeros((COLS, CH), BF16)

    for j in range(16):
        pltpu.make_async_copy(tap_rows(j), tap_rows(j), tap_recv.at[j]).wait()
    wl_copy.wait()

    for n in range(NCH):
        lateral[:, n * CK:(n + 1) * CK] = nn(taps[...], wl[:, n * CK:(n + 1) * CK])
    w_copy.wait()

    def lanes(c):
        return pl.ds(c * CK, CK)

    def x_copy(c):
        return pltpu.make_async_remote_copy(
            src_ref=xout.at[:, lanes(c)], dst_ref=xin.at[:, lanes(c)],
            send_sem=x_send.at[c], recv_sem=x_recv.at[c],
            device_id={"dp": dp, "section": s + 1}, device_id_type=MESH,
        )

    def halo_up(c):
        return pltpu.make_async_remote_copy(
            src_ref=ext.at[pl.ds(COLS, COLS), lanes(c)], dst_ref=ext.at[pl.ds(COLS + PIX, COLS), lanes(c)],
            send_sem=halo_send.at[0, c], recv_sem=halo_recv.at[1, c],
            device_id={"dp": up, "section": s}, device_id_type=MESH,
        )

    def halo_down(c):
        return pltpu.make_async_remote_copy(
            src_ref=ext.at[pl.ds(PIX, COLS), lanes(c)], dst_ref=ext.at[pl.ds(0, COLS), lanes(c)],
            send_sem=halo_send.at[1, c], recv_sem=halo_recv.at[0, c],
            device_id={"dp": down, "section": s}, device_id_type=MESH,
        )

    def local_wait(ref, sem):
        pltpu.make_async_copy(ref, ref, sem).wait()

    def take_x(c):
        cols = slice(c * CK, (c + 1) * CK)

        @pl.when(is_first)
        def _():
            ext[COLS:COLS + PIX, cols] = lateral[:, cols].astype(BF16)

        @pl.when(s > 0)
        def _():
            local_wait(xin.at[:, lanes(c)], x_recv.at[c])
            ext[COLS:COLS + PIX, cols] = (xin[:, cols].astype(F32) + lateral[:, cols]).astype(BF16)

        @pl.when(has_up)
        def _():
            halo_up(c).start()

        @pl.when(has_down)
        def _():
            halo_down(c).start()

    def wait_halo(c):
        @pl.when(has_up)
        def _():
            local_wait(ext.at[pl.ds(0, COLS), lanes(c)], halo_recv.at[0, c])

        @pl.when(has_down)
        def _():
            local_wait(ext.at[pl.ds(COLS + PIX, COLS), lanes(c)], halo_recv.at[1, c])

    def conv_part(c, dr, dc, ncols):
        rows = (1 + dr) * COLS
        return nn(
            ext[rows:rows + PIX, c * CK:(c + 1) * CK],
            w[(dr + 1) * 3 + dc + 1, c * CK:(c + 1) * CK, ncols],
        )

    every = slice(0, CH)

    def conv_inner(c, start):
        for dc in (-1, 0, 1):
            term = conv_part(c, 0, dc, every)
            if start:
                acc[dc + 1] = term
            else:
                acc[dc + 1] += term

    def conv_outer(c):
        for dc in (-1, 0, 1):
            acc[dc + 1] += conv_part(c, -1, dc, every) + conv_part(c, 1, dc, every)

    col = lax.broadcasted_iota(jnp.int32, (PIX, CK), 0) % COLS

    def before(v):
        return jnp.where(col == 0, 0.0, pltpu.roll(v, 1, 0))

    def after(v):
        return jnp.where(col == COLS - 1, 0.0, pltpu.roll(v, PIX - 1, 0))

    take_x(0)
    take_x(1)
    conv_inner(0, True)
    wait_halo(0)
    conv_outer(0)
    take_x(2)
    conv_inner(1, False)
    conv_inner(2, False)
    wait_halo(1)
    conv_outer(1)
    wait_halo(2)
    for n in range(NCH):
        ncols = slice(n * CK, (n + 1) * CK)
        parts = [
            acc[dc + 1, :, ncols] + conv_part(2, -1, dc, ncols) + conv_part(2, 1, dc, ncols)
            for dc in (-1, 0, 1)
        ]
        pre = before(parts[0]) + parts[1] + after(parts[2])
        sig = 1.0 / (1.0 + jnp.exp(-pre))
        xout[:, ncols] = (pre * sig).astype(BF16)

        @pl.when(s < SECTIONS - 1)
        def _():
            x_copy(n).start()

        dsilu[:, ncols] = sig * (1.0 + pre * (1.0 - sig))

    def early_copies(k):
        peer = (x + k) % NX
        to = {"dp": peer * NZ + z, "section": s}
        at = pl.ds(pl.multiple_of(peer * XL, 128), XL)
        return (
            pltpu.make_async_remote_copy(
                src_ref=ext, dst_ref=ext_all.at[x], send_sem=e_send.at[0, k], recv_sem=e_recv.at[0, x],
                device_id=to, device_id_type=MESH,
            ),
            pltpu.make_async_remote_copy(
                src_ref=taps.at[:, at], dst_ref=taps_all.at[x], send_sem=e_send.at[1, k], recv_sem=e_recv.at[1, x],
                device_id=to, device_id_type=MESH,
            ),
        )

    def exchange_early():
        at = pl.ds(pl.multiple_of(x * XL, 128), XL)
        pltpu.make_async_copy(ext, ext_all.at[x], e_recv.at[0, x]).start()
        pltpu.make_async_copy(taps.at[:, at], taps_all.at[x], e_recv.at[1, x]).start()
        for k in range(1, NX):
            for copy in early_copies(k):
                copy.start()
        for src in range(NX):
            local_wait(ext_all.at[src], e_recv.at[0, src])
            local_wait(taps_all.at[src], e_recv.at[1, src])
            lanes_of = slice(src * PIX, (src + 1) * PIX)
            for dr in range(3):
                cols_t[dr, :, lanes_of] = ext_all[src, dr * COLS:dr * COLS + PIX, :].T
            taps_t[:, lanes_of] = taps_all[src].T

    @pl.when(jnp.logical_and(early, s % 2 == 1))
    def _():
        pl.semaphore_signal(early_sem, inc=1, device_id={"dp": dp, "section": s - 1}, device_id_type=MESH)

    @pl.when(jnp.logical_and(early, s % 2 == 0))
    def _():
        pl.semaphore_wait(early_sem, 1)

    @pl.when(early)
    def _():
        exchange_early()

    @pl.when(is_last)
    def _():
        for r in range(4):
            local_wait(oh_rows(r), oh_recv.at[r])
        logits = nn(xout[...], cls_ref[...])
        lane = lax.broadcasted_iota(jnp.int32, (PIX, CPAD), 1)
        real = lane < CLASSES
        expo = jnp.where(real, jnp.exp(logits), 0.0)
        probs = expo / jnp.sum(expo, axis=-1, keepdims=True)
        marks = oh[...].astype(F32)
        weight = jnp.sum(jnp.where(lane == CPAD - 1, marks, 0.0), axis=-1, keepdims=True)
        hot = jnp.where(real, marks, 0.0)
        grad_logits = ((probs - hot) * weight).astype(BF16)
        gx[...] = nt(grad_logits, cls_ref[...])

    def g_copy(c):
        return pltpu.make_async_remote_copy(
            src_ref=gs_all.at[x, :, lanes(c)], dst_ref=gin.at[:, lanes(c)],
            send_sem=g_send.at[c], recv_sem=g_recv.at[c],
            device_id={"dp": dp, "section": s - 1}, device_id_type=MESH,
        )

    def rim_up(c):
        return pltpu.make_async_remote_copy(
            src_ref=rim_out.at[0, :, lanes(c)], dst_ref=rim_in.at[1, :, lanes(c)],
            send_sem=rim_send.at[0, c], recv_sem=rim_recv.at[1, c],
            device_id={"dp": up, "section": s}, device_id_type=MESH,
        )

    def rim_down(c):
        return pltpu.make_async_remote_copy(
            src_ref=rim_out.at[1, :, lanes(c)], dst_ref=rim_in.at[0, :, lanes(c)],
            send_sem=rim_send.at[1, c], recv_sem=rim_recv.at[0, c],
            device_id={"dp": down, "section": s}, device_id_type=MESH,
        )

    def take_g(c):
        cols = slice(c * CK, (c + 1) * CK)

        @pl.when(s < SECTIONS - 1)
        def _():
            local_wait(gin.at[:, lanes(c)], g_recv.at[c])
            gx[:, cols] = gin[:, cols].astype(F32)

        grad_pre = (gx[:, cols] * dsilu[:, cols]).astype(BF16).astype(F32)
        gpv[0, :, cols] = after(grad_pre).astype(BF16)
        gpv[1, :, cols] = grad_pre.astype(BF16)
        gp_all[x, :, cols] = grad_pre.astype(BF16)
        gpv[2, :, cols] = before(grad_pre).astype(BF16)

    def back_part(c, dr, krows):
        total = None
        for dc in (-1, 0, 1):
            term = nt(
                gpv[dc + 1, :, c * CK:(c + 1) * CK],
                w[(dr + 1) * 3 + dc + 1, krows, c * CK:(c + 1) * CK],
            )
            total = term if total is None else total + term
        return total

    take_g(0)
    for dr in (-1, 0, 1):
        acc[dr + 1] = back_part(0, dr, every)
    take_g(1)
    for dr in (-1, 0, 1):
        acc[dr + 1] += back_part(1, dr, every)
    take_g(2)
    for n in range(NCH):
        ncols = slice(n * CK, (n + 1) * CK)
        upper = acc[0, :, ncols] + back_part(2, -1, ncols)
        acc[0, :, ncols] = upper
        rim_out[0, :, ncols] = upper[0:COLS].astype(BF16)
        lower = acc[2, :, ncols] + back_part(2, 1, ncols)
        acc[2, :, ncols] = lower
        rim_out[1, :, ncols] = lower[PIX - COLS:].astype(BF16)

        @pl.when(has_up)
        def _():
            rim_up(n).start()

        @pl.when(has_down)
        def _():
            rim_down(n).start()

    acc[1] += back_part(2, 0, every)
    for n in range(NCH):
        ncols = slice(n * CK, (n + 1) * CK)
        acc[1, 0:PIX - COLS, ncols] += acc[0, COLS:, ncols]
        acc[1, COLS:, ncols] += acc[2, 0:PIX - COLS, ncols]

        @pl.when(has_up)
        def _():
            local_wait(rim_in.at[0, :, lanes(n)], rim_recv.at[0, n])
            acc[1, 0:COLS, ncols] += rim_in[0, :, ncols].astype(F32)

        @pl.when(has_down)
        def _():
            local_wait(rim_in.at[1, :, lanes(n)], rim_recv.at[1, n])
            acc[1, PIX - COLS:, ncols] += rim_in[1, :, ncols].astype(F32)

        gs_all[x, :, ncols] = acc[1, :, ncols].astype(BF16)

        @pl.when(s > 0)
        def _():
            g_copy(n).start()

    def ring_copy(kind, k):
        ref = (gp_all, gs_all)[kind]
        return pltpu.make_async_remote_copy(
            src_ref=ref.at[x], dst_ref=ref.at[x], send_sem=a_send.at[kind, k], recv_sem=a_recv.at[kind, x],
            device_id={"dp": (x + k) % NX * NZ + z, "section": s}, device_id_type=MESH,
        )

    for kind in range(2):
        for k in range(1, NX):
            ring_copy(kind, k).start()

    @pl.when(jnp.logical_not(early))
    def _():
        exchange_early()

    def wait_ring(kind, src):
        @pl.when(src != x)
        def _():
            local_wait((gp_all, gs_all)[kind].at[src], a_recv.at[kind, src])

    whole_col = lax.broadcasted_iota(jnp.int32, (PIX, CH), 0) % COLS
    for src in range(NX):
        wait_ring(0, src)
        rows = slice(src * PIX, (src + 1) * PIX)
        value = gp_all[src].astype(F32)
        gpv_all[0, rows, :] = jnp.where(whole_col == COLS - 1, 0.0, pltpu.roll(value, PIX - 1, 0)).astype(BF16)
        gpv_all[1, rows, :] = gp_all[src]
        gpv_all[2, rows, :] = jnp.where(whole_col == 0, 0.0, pltpu.roll(value, 1, 0)).astype(BF16)

    @pl.loop(0, 9)
    def _(u):
        unit = 9 * x + u
        o = unit // 4
        chans = pl.ds(pl.multiple_of((unit % 4) * UNIT, UNIT), UNIT)
        part_c[pl.ds(pl.multiple_of(u * UNIT, UNIT), UNIT), :] = nn(cols_t[o // 3, chans, :], gpv_all[o % 3])

    def slice_at(way, t):
        return (z + NZ - 1 - t) % NZ if way == 0 else (z + 1 + t) % NZ

    def own_rows(part, rows, way, t):
        at = pl.ds(pl.multiple_of(slice_at(way, t) * rows, 8), rows)
        return part[at, way * HALF:(way + 1) * HALF]

    def hop(ring, send, recv, way, t):
        return pltpu.make_async_remote_copy(
            src_ref=ring.at[way, t], dst_ref=ring.at[way, t + 1],
            send_sem=send.at[way, t], recv_sem=recv.at[way, t],
            device_id={"dp": z_next if way == 0 else z_prev, "section": s}, device_id_type=MESH,
        )

    conv_ring = (ring_c, rc_send, rc_recv)
    lat_ring = (ring_l, rl_send, rl_recv)
    for way in range(2):
        ring_c[way, 0] = own_rows(part_c, CROWS, way, 0).astype(BF16)
        hop(*conv_ring, way, 0).start()

    for src in range(NX):
        wait_ring(1, src)
    spread = gs_all[...].reshape(WIDE, CH)

    part_l[...] = nn(taps_t[...], spread)

    for way in range(2):
        ring_l[way, 0] = own_rows(part_l, KPAD, way, 0).astype(BF16)
        hop(*lat_ring, way, 0).start()

    for t in range(NZ - 1):
        for ring, part, rows, out in ((conv_ring, part_c, CROWS, conv_out), (lat_ring, part_l, KPAD, lat_out)):
            for way in range(2):
                buf = ring[0]
                local_wait(buf.at[way, t + 1], ring[2].at[way, t])
                total = buf[way, t + 1].astype(F32) + own_rows(part, rows, way, t + 1)
                if t < NZ - 2:
                    buf[way, t + 1] = total.astype(BF16)
                    hop(*ring, way, t + 1).start()
                else:
                    out[:, way * HALF:(way + 1) * HALF] = total

    for k in range(16):
        d, sec = tap_target(k)

        @pl.when(jnp.logical_or(d != dp, sec != s))
        def _():
            tap_copy(k).wait_send()

    @pl.when(is_last)
    def _():
        for img in range(4):
            @pl.when(home(img) != dp)
            def _():
                oh_copy(img).wait_send()

    for c in range(NCH):
        @pl.when(s < SECTIONS - 1)
        def _():
            x_copy(c).wait_send()

        @pl.when(s > 0)
        def _():
            g_copy(c).wait_send()

        @pl.when(has_up)
        def _():
            halo_up(c).wait_send()
            rim_up(c).wait_send()

        @pl.when(has_down)
        def _():
            halo_down(c).wait_send()
            rim_down(c).wait_send()

    for k in range(1, NX):
        for copy in early_copies(k):
            copy.wait_send()
        for kind in range(2):
            ring_copy(kind, k).wait_send()
    for way in range(2):
        for t in range(NZ - 1):
            hop(*conv_ring, way, t).wait_send()
            hop(*lat_ring, way, t).wait_send()


def head_call(taps, wl, w, cls, oh):
    dma = pltpu.SemaphoreType.DMA
    hbm = pl.BlockSpec(memory_space=pl.ANY)
    vmem = pl.BlockSpec(memory_space=pltpu.VMEM)
    return pl.pallas_call(
        head_kernel,
        out_shape=(
            jax.ShapeDtypeStruct((CROWS, CH), F32),
            jax.ShapeDtypeStruct((KPAD, CH), F32),
        ),
        in_specs=[hbm, hbm, hbm, vmem, hbm],
        out_specs=(vmem, vmem),
        scratch_shapes=[
            pltpu.VMEM((PIX, KW), BF16),
            pltpu.VMEM((KW, CH), BF16),
            pltpu.VMEM((9, CH, CH), BF16),
            pltpu.VMEM((PIX, CH), F32),
            pltpu.VMEM((PIX + 2 * COLS, CH), BF16),
            pltpu.VMEM((PIX, CH), BF16),
            pltpu.VMEM((PIX, CH), BF16),
            pltpu.VMEM((PIX, CH), BF16),
            pltpu.VMEM((PIX, CH), F32),
            pltpu.VMEM((3, PIX, CH), F32),
            pltpu.VMEM((3, PIX, CH), BF16),
            pltpu.VMEM((2, COLS, CH), BF16),
            pltpu.VMEM((2, COLS, CH), BF16),
            pltpu.VMEM((PIX, CPAD), BF16),
            pltpu.VMEM((NX, PIX + 2 * COLS, CH), BF16),
            pltpu.VMEM((NX, PIX, XL), BF16),
            pltpu.VMEM((NX, PIX, CH), BF16),
            pltpu.VMEM((NX, PIX, CH), BF16),
            pltpu.VMEM((3, WIDE, CH), BF16),
            pltpu.VMEM((3, CH, WIDE), BF16),
            pltpu.VMEM((XL, WIDE), BF16),
            pltpu.VMEM((XC, CH), F32),
            pltpu.VMEM((XL, CH), F32),
            pltpu.VMEM((2, NZ, CROWS, HALF), BF16),
            pltpu.VMEM((2, NZ, KPAD, HALF), BF16),
            dma((2,)),
            dma((16,)),
            dma((16,)),
            dma((4,)),
            dma((4,)),
            dma((NCH,)),
            dma((NCH,)),
            dma((2, NCH)),
            dma((2, NCH)),
            dma((NCH,)),
            dma((NCH,)),
            dma((2, NCH)),
            dma((2, NCH)),
            pltpu.SemaphoreType.REGULAR,
            dma((2, NX)),
            dma((2, NX)),
            dma((2, NX)),
            dma((2, NX)),
            dma((2, NZ - 1)),
            dma((2, NZ - 1)),
            dma((2, NZ - 1)),
            dma((2, NZ - 1)),
        ],
        compiler_params=pltpu.CompilerParams(
            collective_id=0, has_side_effects=True, vmem_limit_bytes=60 << 20
        ),
    )(taps, wl, w, cls, oh)


def on_device(tap_maps, lateral_weight, conv_weight, classifier, tile_counts, labels):
    levels, micros, here, width = tap_maps.shape
    per = width // GROUPS
    classes = classifier.shape[1]
    pixels = labels.shape[1]
    grouped = tap_maps.reshape(levels * micros, here, GROUPS, per)
    taps = jnp.pad(grouped, ((0, 0), (0, 0), (0, 0), (0, KPAD - per))).reshape(levels * micros, here, KW)
    own = jnp.pad(lateral_weight[0], ((0, KPAD - per), (0, 0)))
    wl = lax.all_gather(own, "dp", axis=0, tiled=True)
    cls = jnp.pad(classifier, ((0, 0), (0, CPAD - classes)))
    counts = tile_counts[0][:, None]
    valid = (jnp.arange(pixels)[None, :] // COLS < counts).astype(F32)
    weight = valid / (counts.astype(F32) * COLS * GROUPS * micros)
    lane = jnp.arange(CPAD)
    hot = (labels[:, :, None] == lane).astype(F32)
    oh = jnp.where(lane == CPAD - 1, weight[:, :, None], hot).astype(BF16)
    conv_grad, lateral_grad = head_call(taps, wl, conv_weight.reshape(9, CH, CH), cls, oh)
    return (conv_grad[None], lateral_grad[None, :per])


def solution(mesh):
    placed = (
        P(None, None, ("dp", "section"), None),
        P("section", "dp", None),
        P("section", None, None),
        P(),
        P("dp", None),
        P(None, "dp"),
    )
    return jax.shard_map(
        on_device,
        mesh=mesh,
        in_specs=placed,
        out_specs=(P("section", "dp", None), P("section", "dp", None)),
        check_vma=False,
    )
```

```python
import jax
import jax.numpy as jnp
from jax import lax
from jax.experimental import pallas as pl
from jax.experimental.pallas import tpu as pltpu
from jax.sharding import PartitionSpec as P

MESH = pl.DeviceIdType.MESH
F32 = jnp.float32
BF16 = jnp.bfloat16
NZ = 8
NX = 4
COLS = 64
ROWS = 4
PIX = ROWS * COLS
CH = 768
CK = 256
NCH = CH // CK
KROWS = 100
KPAD = 112
GROUPS = NX * NZ
KW = KPAD * GROUPS
SECTIONS = 8
WIDE = NX * PIX
CROWS = 9 * CH // GROUPS
XC, XL = CROWS * NZ, KPAD * NZ
UNIT = XC // 9
HALF = CH // 2
FARROWS = PIX // 2
CLASSES = 150
CPAD = 256


def nt(a, b):
    return lax.dot_general(a, b, (((1,), (1,)), ((), ())), preferred_element_type=F32)


def tn(a, b):
    return lax.dot_general(a, b, (((0,), (0,)), ((), ())), preferred_element_type=F32)


def nn(a, b):
    return jnp.dot(a, b, preferred_element_type=F32)


def head_kernel(
    tap_ref, lat_ref, w_hbm, cls_ref, counts_ref, labels_ref, conv_out, lat_out,
    tap_pad, taps, wl, w, lateral, ext, xin, xout, gin, dsilu, acc, gpv, rim_out, rim_in, oh_own, oh,
    ext_all, taps_all, transit, gp_all, gs_all, gpv_all, cols_t, taps_t, part_c, part_l, ring_c, ring_l,
    local_sem, tap_send, tap_recv, pass_send, wz_send, wx_send, wf_send, w_recv, oh_send, oh_recv,
    x_send, x_recv, halo_send, halo_recv, g_send, g_recv, rim_send, rim_recv,
    early_sem, t_send, t_recv, a_send, a_recv, rc_send, rc_recv, rl_send, rl_recv,
):
    dp = lax.axis_index("dp")
    s = lax.axis_index("section")
    x, z = dp // NZ, dp % NZ
    odd = x % 2
    half = (z % 2 + odd) % 2
    image = z // 2
    has_up = jnp.logical_not(jnp.logical_and(half == 0, x == 0))
    has_down = jnp.logical_not(jnp.logical_and(half == 1, x == NX - 1))
    pair = dp + 1 - 2 * (z % 2)
    up = jnp.where(half == 1, pair, dp - NZ)
    down = jnp.where(half == 0, pair, dp + NZ)
    src_half = z // 4
    is_first, is_last = s == 0, s == SECTIONS - 1
    even = s % 2 == 0
    gx = lateral
    z_next, z_prev = x * NZ + (z + 1) % NZ, x * NZ + (z + NZ - 1) % NZ
    x_left, x_right, x_far = (x + NX - 1) % NX, (x + 1) % NX, (x + 2) % NX
    left, right = x_left * NZ + z, x_right * NZ + z

    def home(img):
        return x * NZ + 2 * img + (src_half + odd) % 2

    def remote(src, dst, send, recv, d, sec):
        return pltpu.make_async_remote_copy(
            src_ref=src, dst_ref=dst, send_sem=send, recv_sem=recv,
            device_id={"dp": d, "section": sec}, device_id_type=MESH,
        )

    def local_wait(ref, sem):
        pltpu.make_async_copy(ref, ref, sem).wait()

    my_tile = s // 4
    tap_slot = (z % 4) * 4 + s % 4
    w_copy = pltpu.make_async_copy(w_hbm, w, local_sem.at[0])
    w_copy.start()

    barrier = pltpu.get_barrier_semaphore()

    def greet(d, sec):
        pl.semaphore_signal(barrier, inc=1, device_id={"dp": d, "section": sec}, device_id_type=MESH)

    @pl.when(even)
    def _():
        for j in range(16):
            d, sec = x * NZ + half * 4 + j // 4, (image % 2) * 4 + j % 4

            @pl.when(jnp.logical_or(d != dp, sec != s))
            def _():
                greet(d, sec)

    for d in (left, right, z_next, z_prev):
        greet(d, s)

    @pl.when(has_up)
    def _():
        greet(up, s)

    @pl.when(has_down)
    def _():
        greet(down, s)

    @pl.when(s > 0)
    def _():
        greet(dp, s - 1)

    @pl.when(s < SECTIONS - 1)
    def _():
        greet(dp, s + 1)

    @pl.when(is_last)
    def _():
        for j in range(4):
            d = x * NZ + half * 4 + j

            @pl.when(d != dp)
            def _():
                greet(d, s)

    flat = tap_ref[...].reshape(8 * 16, GROUPS * KROWS).astype(F32)
    lane = lax.broadcasted_iota(jnp.int32, (8 * 16, 128), 1)
    for tile in range(KW // 128):
        first = tile * 128
        total = jnp.zeros((8 * 16, 128), F32)
        for g in range(first // KPAD, min((first + 127) // KPAD + 1, GROUPS)):
            lo = first - (KPAD - KROWS) * g
            start = min(max(lo // 128 * 128, 0), GROUPS * KROWS - 256)
            moved = pltpu.roll(flat[:, start:start + 256], (start - lo) % 256, 1)[:, :128]
            inside = jnp.logical_and(lane + first >= KPAD * g, lane + first < KPAD * g + KROWS)
            total = jnp.where(inside, moved, total)
        tap_pad[:, :, first:first + 128] = total.astype(BF16).reshape(8, 16, 128)

    def w_rows(xx, zz):
        return wl.at[pl.ds(pl.multiple_of((xx * NZ + zz) * KPAD, 16), KPAD), :]

    wl[pl.ds(pl.multiple_of(dp * KPAD, 16), KPAD), :] = lat_ref[...]

    def tap_target(k):
        level, micro = k // 2, k % 2
        return home(2 * micro + my_tile), 2 * level

    need = jnp.int32(4)
    for k in range(8):
        d, sec = tap_target(k)
        need += jnp.logical_or(d != dp, sec != s).astype(jnp.int32)
    for flag in (has_up, has_down, s > 0, s < SECTIONS - 1):
        need += flag.astype(jnp.int32)
    for img in range(4):
        need += jnp.logical_and(is_last, home(img) != dp).astype(jnp.int32)
    pl.semaphore_wait(barrier, need)

    def tap_rows(j):
        return taps.at[pl.ds(pl.multiple_of((j // 4) * COLS + (j % 4) * 16, 16), 16), :]

    def tap_copy(k):
        d, sec = tap_target(k)
        return remote(tap_pad.at[k], tap_rows(tap_slot), tap_send.at[k], tap_recv.at[tap_slot], d, sec)

    def tap_pass(j):
        return remote(tap_rows(j), tap_rows(j), pass_send.at[j], tap_recv.at[j], dp, s + 1)

    for k in range(8):
        d, sec = tap_target(k)
        other = jnp.logical_or(d != dp, sec != s)

        @pl.when(other)
        def _():
            tap_copy(k).start()

        @pl.when(jnp.logical_not(other))
        def _():
            pltpu.make_async_copy(tap_pad.at[k], tap_rows(tap_slot), tap_recv.at[tap_slot]).start()

    order = (0, -1, 1, -2, 2, -3, 3, -4)

    def ring_z(i):
        return (z + NZ + order[i]) % NZ

    def w_send_z(i, way):
        block = w_rows(x, ring_z(i))
        return remote(
            block, block, wz_send.at[way, i], w_recv.at[x * NZ + ring_z(i)], z_next if way == 0 else z_prev, s
        )

    def w_send_x(i, way):
        block = w_rows(x, ring_z(i))
        return remote(
            block, block, wx_send.at[way, i], w_recv.at[x * NZ + ring_z(i)], right if way == 0 else left, s
        )

    def w_send_far(i):
        xx = x_left if i % 2 == 0 else x_right
        block = w_rows(xx, ring_z(i))
        return remote(
            block, block, wf_send.at[i], w_recv.at[xx * NZ + ring_z(i)], right if i % 2 == 0 else left, s
        )

    def w_wait(xx, i):
        local_wait(w_rows(xx, ring_z(i)), w_recv.at[xx * NZ + ring_z(i)])

    def z_ways(i):
        ways = []
        if order[i] <= 0 and order[i] > -4:
            ways.append(0)
        if order[i] >= 0 and order[i] < 3:
            ways.append(1)
        return ways

    def far_step(i):
        for xx, forwards in ((x_left, i % 2 == 0), (x_right, i % 2 == 1)):
            w_wait(xx, i)
            if forwards:
                w_send_far(i).start()

    for i in range(NZ):
        if i > 0:
            w_wait(x, i)
        for way in z_ways(i):
            w_send_z(i, way).start()
        for way in range(2):
            w_send_x(i, way).start()
        if i > 0:
            far_step(i - 1)

        @pl.when(even)
        def _():
            for j in (2 * i, 2 * i + 1):
                local_wait(tap_rows(j), tap_recv.at[j])
                tap_pass(j).start()

    far_step(NZ - 1)

    def oh_rows(r):
        return oh.at[pl.ds(pl.multiple_of(r * COLS, COLS), COLS), :]

    def oh_src(img):
        return oh_own.at[img // 2, pl.ds((img % 2) * COLS, COLS), :]

    def oh_copy(img):
        return remote(oh_src(img), oh_rows(z % 4), oh_send.at[img], oh_recv.at[z % 4], home(img), s)

    @pl.when(is_last)
    def _():
        sub = lax.broadcasted_iota(jnp.int32, (CPAD, 2 * COLS), 0)
        tile_of = lax.broadcasted_iota(jnp.int32, (CPAD, 2 * COLS), 1) // COLS
        for micro in range(2):
            count = counts_ref[0, micro]
            share = 1.0 / (count.astype(F32) * (COLS * GROUPS * 2))
            weight = jnp.where(tile_of < count, share, 0.0)
            hot = jnp.where(sub == labels_ref[micro:micro + 1, :], 1.0, 0.0)
            oh_own[micro] = jnp.where(sub == CPAD - 1, weight, hot).T.astype(BF16)
        for img in range(4):
            @pl.when(home(img) != dp)
            def _():
                oh_copy(img).start()

            @pl.when(home(img) == dp)
            def _():
                pltpu.make_async_copy(oh_src(img), oh_rows(z % 4), oh_recv.at[z % 4]).start()

    @pl.when(jnp.logical_not(has_up))
    def _():
        ext[0:COLS, :] = jnp.zeros((COLS, CH), BF16)

    @pl.when(jnp.logical_not(has_down))
    def _():
        ext[COLS + PIX:, :] = jnp.zeros((COLS, CH), BF16)

    @pl.when(jnp.logical_not(even))
    def _():
        for j in range(16):
            local_wait(tap_rows(j), tap_recv.at[j])

    for i in range(NZ):
        w_wait(x_far, i)

    for n in range(NCH):
        lateral[:, n * CK:(n + 1) * CK] = nn(taps[...], wl[:, n * CK:(n + 1) * CK])
    w_copy.wait()

    def lanes(c):
        return pl.ds(c * CK, CK)

    def x_copy(c):
        return pltpu.make_async_remote_copy(
            src_ref=xout.at[:, lanes(c)], dst_ref=xin.at[:, lanes(c)],
            send_sem=x_send.at[c], recv_sem=x_recv.at[c],
            device_id={"dp": dp, "section": s + 1}, device_id_type=MESH,
        )

    def halo_up(c):
        return pltpu.make_async_remote_copy(
            src_ref=ext.at[pl.ds(COLS, COLS), lanes(c)], dst_ref=ext.at[pl.ds(COLS + PIX, COLS), lanes(c)],
            send_sem=halo_send.at[0, c], recv_sem=halo_recv.at[1, c],
            device_id={"dp": up, "section": s}, device_id_type=MESH,
        )

    def halo_down(c):
        return pltpu.make_async_remote_copy(
            src_ref=ext.at[pl.ds(PIX, COLS), lanes(c)], dst_ref=ext.at[pl.ds(0, COLS), lanes(c)],
            send_sem=halo_send.at[1, c], recv_sem=halo_recv.at[0, c],
            device_id={"dp": down, "section": s}, device_id_type=MESH,
        )

    def take_x(c):
        cols = slice(c * CK, (c + 1) * CK)

        @pl.when(is_first)
        def _():
            ext[COLS:COLS + PIX, cols] = lateral[:, cols].astype(BF16)

        @pl.when(s > 0)
        def _():
            local_wait(xin.at[:, lanes(c)], x_recv.at[c])
            ext[COLS:COLS + PIX, cols] = (xin[:, cols].astype(F32) + lateral[:, cols]).astype(BF16)

        @pl.when(has_up)
        def _():
            halo_up(c).start()

        @pl.when(has_down)
        def _():
            halo_down(c).start()

    def wait_halo(c):
        @pl.when(has_up)
        def _():
            local_wait(ext.at[pl.ds(0, COLS), lanes(c)], halo_recv.at[0, c])

        @pl.when(has_down)
        def _():
            local_wait(ext.at[pl.ds(COLS + PIX, COLS), lanes(c)], halo_recv.at[1, c])

    def conv_part(c, dr, dc, ncols):
        rows = (1 + dr) * COLS
        return nn(
            ext[rows:rows + PIX, c * CK:(c + 1) * CK],
            w[(dr + 1) * 3 + dc + 1, c * CK:(c + 1) * CK, ncols],
        )

    every = slice(0, CH)

    def conv_inner(c, start):
        for dc in (-1, 0, 1):
            term = conv_part(c, 0, dc, every)
            if start:
                acc[dc + 1] = term
            else:
                acc[dc + 1] += term

    def conv_outer(c):
        for dc in (-1, 0, 1):
            acc[dc + 1] += conv_part(c, -1, dc, every) + conv_part(c, 1, dc, every)

    col = lax.broadcasted_iota(jnp.int32, (PIX, CK), 0) % COLS

    def before(v):
        return jnp.where(col == 0, 0.0, pltpu.roll(v, 1, 0))

    def after(v):
        return jnp.where(col == COLS - 1, 0.0, pltpu.roll(v, PIX - 1, 0))

    take_x(0)
    take_x(1)
    conv_inner(0, True)
    wait_halo(0)
    conv_outer(0)
    take_x(2)
    conv_inner(1, False)
    conv_inner(2, False)
    wait_halo(1)
    conv_outer(1)
    wait_halo(2)
    for n in range(NCH):
        ncols = slice(n * CK, (n + 1) * CK)
        parts = [
            acc[dc + 1, :, ncols] + conv_part(2, -1, dc, ncols) + conv_part(2, 1, dc, ncols)
            for dc in (-1, 0, 1)
        ]
        pre = before(parts[0]) + parts[1] + after(parts[2])
        sig = 1.0 / (1.0 + jnp.exp(-pre))
        xout[:, ncols] = (pre * sig).astype(BF16)

        @pl.when(s < SECTIONS - 1)
        def _():
            x_copy(n).start()

        dsilu[:, ncols] = sig * (1.0 + pre * (1.0 - sig))

    def gather_copy(buf, kind, way):
        return remote(
            buf.at[x], buf.at[x], a_send.at[kind, way], a_recv.at[kind, way], right if way == 0 else left, s
        )

    def gather_far(buf, kind, way):
        rows = buf.shape[1] // 2
        block = buf.at[x_left if way == 0 else x_right, pl.ds(way * rows, rows), :]
        return remote(
            block, block, a_send.at[kind, 2 + way], a_recv.at[kind, 2 + way], right if way == 0 else left, s
        )

    def gather_start(buf, kind):
        for way in range(2):
            gather_copy(buf, kind, way).start()

    def gather_forward(buf, kind):
        for way in range(2):
            local_wait(buf.at[x_left if way == 0 else x_right], a_recv.at[kind, way])
            gather_far(buf, kind, way).start()

    def gather_finish(buf, kind):
        rows = buf.shape[1] // 2
        for way in range(2):
            local_wait(buf.at[x_far, pl.ds(way * rows, rows), :], a_recv.at[kind, 2 + way])

    def gather_sent(buf, kind):
        for way in range(2):
            gather_copy(buf, kind, way).wait_send()
            gather_far(buf, kind, way).wait_send()

    def tap_part(xx):
        return pl.ds(pl.multiple_of(xx * XL, 128), XL)

    def slice_copies(way):
        to = right if way == 0 else left
        near = x_right if way == 0 else x_left
        return (
            remote(taps.at[:, tap_part(near)], taps_all.at[x], t_send.at[way], t_recv.at[way], to, s),
            remote(
                taps.at[pl.ds(way * FARROWS, FARROWS), tap_part(x_far)], transit.at[way],
                t_send.at[2 + way], t_recv.at[2 + way], to, s,
            ),
        )

    def slice_far(way):
        source = x_left if way == 0 else x_right
        return remote(
            transit.at[way], taps_all.at[source, pl.ds(way * FARROWS, FARROWS), :],
            t_send.at[4 + way], t_recv.at[4 + way], right if way == 0 else left, s,
        )

    def early_start():
        ext_all[x] = ext[...]
        taps_all[x] = taps[:, tap_part(x)]
        for way in range(2):
            for copy in slice_copies(way):
                copy.start()
        gather_start(ext_all, 2)

    def early_forward():
        for way in range(2):
            local_wait(transit.at[way], t_recv.at[2 + way])
            slice_far(way).start()
        gather_forward(ext_all, 2)

    def turn(src):
        lanes_of = pl.ds(pl.multiple_of(src * PIX, PIX), PIX)
        for dr in range(3):
            cols_t[dr, :, lanes_of] = ext_all[src, dr * COLS:dr * COLS + PIX, :].T
        taps_t[:, lanes_of] = taps_all[src].T

    def early_finish():
        for way in range(2):
            local_wait(taps_all.at[x_left if way == 0 else x_right], t_recv.at[way])
            local_wait(taps_all.at[x_far, pl.ds(way * FARROWS, FARROWS), :], t_recv.at[4 + way])
        gather_finish(ext_all, 2)

        @pl.loop(0, NX)
        def _(src):
            turn(src)

    @pl.when(jnp.logical_and(s < 6, s % 2 == 1))
    def _():
        pl.semaphore_signal(early_sem, inc=1, device_id={"dp": dp, "section": s - 1}, device_id_type=MESH)

    @pl.when(jnp.logical_and(s < 6, s % 2 == 0))
    def _():
        pl.semaphore_wait(early_sem, 1)

    @pl.when(s < 6)
    def _():
        early_start()

    @pl.when(s < 4)
    def _():
        early_forward()
        early_finish()

    @pl.when(is_last)
    def _():
        for r in range(4):
            local_wait(oh_rows(r), oh_recv.at[r])
        logits = nn(xout[...], cls_ref[...])
        spot = lax.broadcasted_iota(jnp.int32, (PIX, CPAD), 1)
        expo = jnp.exp(logits)
        probs = expo / jnp.sum(expo, axis=-1, keepdims=True)
        marks = oh[...].astype(F32)
        weight = jnp.sum(jnp.where(spot == CPAD - 1, marks, 0.0), axis=-1, keepdims=True)
        grad_logits = ((probs - marks[:, :CLASSES]) * weight).astype(BF16)
        gx[...] = nt(grad_logits, cls_ref[...])

    def g_copy(c):
        return pltpu.make_async_remote_copy(
            src_ref=gs_all.at[x, :, lanes(c)], dst_ref=gin.at[:, lanes(c)],
            send_sem=g_send.at[c], recv_sem=g_recv.at[c],
            device_id={"dp": dp, "section": s - 1}, device_id_type=MESH,
        )

    def rim_up(c):
        return pltpu.make_async_remote_copy(
            src_ref=rim_out.at[0, :, lanes(c)], dst_ref=rim_in.at[1, :, lanes(c)],
            send_sem=rim_send.at[0, c], recv_sem=rim_recv.at[1, c],
            device_id={"dp": up, "section": s}, device_id_type=MESH,
        )

    def rim_down(c):
        return pltpu.make_async_remote_copy(
            src_ref=rim_out.at[1, :, lanes(c)], dst_ref=rim_in.at[0, :, lanes(c)],
            send_sem=rim_send.at[1, c], recv_sem=rim_recv.at[0, c],
            device_id={"dp": down, "section": s}, device_id_type=MESH,
        )

    def take_g(c):
        cols = slice(c * CK, (c + 1) * CK)

        @pl.when(s < SECTIONS - 1)
        def _():
            local_wait(gin.at[:, lanes(c)], g_recv.at[c])
            gx[:, cols] = gin[:, cols].astype(F32)

        grad_pre = (gx[:, cols] * dsilu[:, cols]).astype(BF16).astype(F32)
        gpv[0, :, cols] = after(grad_pre).astype(BF16)
        gpv[1, :, cols] = grad_pre.astype(BF16)
        gp_all[x, :, cols] = grad_pre.astype(BF16)
        gpv[2, :, cols] = before(grad_pre).astype(BF16)

    def back_part(c, dr, krows):
        total = None
        for dc in (-1, 0, 1):
            term = nt(
                gpv[dc + 1, :, c * CK:(c + 1) * CK],
                w[(dr + 1) * 3 + dc + 1, krows, c * CK:(c + 1) * CK],
            )
            total = term if total is None else total + term
        return total

    take_g(0)
    for dr in (-1, 0, 1):
        acc[dr + 1] = back_part(0, dr, every)
    take_g(1)
    for dr in (-1, 0, 1):
        acc[dr + 1] += back_part(1, dr, every)
    take_g(2)
    for n in range(NCH):
        ncols = slice(n * CK, (n + 1) * CK)
        upper = acc[0, :, ncols] + back_part(2, -1, ncols)
        acc[0, :, ncols] = upper
        rim_out[0, :, ncols] = upper[0:COLS].astype(BF16)
        lower = acc[2, :, ncols] + back_part(2, 1, ncols)
        acc[2, :, ncols] = lower
        rim_out[1, :, ncols] = lower[PIX - COLS:].astype(BF16)

        @pl.when(has_up)
        def _():
            rim_up(n).start()

        @pl.when(has_down)
        def _():
            rim_down(n).start()

    acc[1] += back_part(2, 0, every)
    for n in range(NCH):
        ncols = slice(n * CK, (n + 1) * CK)
        acc[1, 0:PIX - COLS, ncols] += acc[0, COLS:, ncols]
        acc[1, COLS:, ncols] += acc[2, 0:PIX - COLS, ncols]

        @pl.when(has_up)
        def _():
            local_wait(rim_in.at[0, :, lanes(n)], rim_recv.at[0, n])
            acc[1, 0:COLS, ncols] += rim_in[0, :, ncols].astype(F32)

        @pl.when(has_down)
        def _():
            local_wait(rim_in.at[1, :, lanes(n)], rim_recv.at[1, n])
            acc[1, PIX - COLS:, ncols] += rim_in[1, :, ncols].astype(F32)

        gs_all[x, :, ncols] = acc[1, :, ncols].astype(BF16)

        @pl.when(s > 0)
        def _():
            g_copy(n).start()

    gather_start(gp_all, 0)
    gather_start(gs_all, 1)

    @pl.when(s >= 6)
    def _():
        early_start()

    gather_forward(gp_all, 0)
    gather_forward(gs_all, 1)

    @pl.when(s >= 4)
    def _():
        early_forward()

    whole_col = lax.broadcasted_iota(jnp.int32, (PIX, CH), 0) % COLS

    def spread(src):
        rows = pl.ds(pl.multiple_of(src * PIX, PIX), PIX)
        value = gp_all[src].astype(F32)
        gpv_all[0, rows, :] = jnp.where(whole_col == COLS - 1, 0.0, pltpu.roll(value, PIX - 1, 0)).astype(BF16)
        gpv_all[1, rows, :] = gp_all[src]
        gpv_all[2, rows, :] = jnp.where(whole_col == 0, 0.0, pltpu.roll(value, 1, 0)).astype(BF16)

    spread(x)
    spread(x_left)
    spread(x_right)
    gather_finish(gp_all, 0)
    spread(x_far)

    @pl.when(s >= 4)
    def _():
        early_finish()

    @pl.loop(0, 9)
    def _(u):
        unit = 9 * x + u
        o = unit // 4
        chans = pl.ds(pl.multiple_of((unit % 4) * UNIT, UNIT), UNIT)
        part_c[pl.ds(pl.multiple_of(u * UNIT, UNIT), UNIT), :] = nn(cols_t[o // 3, chans, :], gpv_all[o % 3])

    def slice_at(way, t):
        return (z + NZ - 1 - t) % NZ if way == 0 else (z + 1 + t) % NZ

    def own_rows(part, rows, way, t):
        at = pl.ds(pl.multiple_of(slice_at(way, t) * rows, 8), rows)
        return part[at, way * HALF:(way + 1) * HALF]

    def hop(ring, send, recv, way, t):
        return pltpu.make_async_remote_copy(
            src_ref=ring.at[way, t], dst_ref=ring.at[way, t + 1],
            send_sem=send.at[way, t], recv_sem=recv.at[way, t],
            device_id={"dp": z_next if way == 0 else z_prev, "section": s}, device_id_type=MESH,
        )

    conv_ring = (ring_c, rc_send, rc_recv)
    lat_ring = (ring_l, rl_send, rl_recv)
    for way in range(2):
        ring_c[way, 0] = own_rows(part_c, CROWS, way, 0).astype(BF16)
        hop(*conv_ring, way, 0).start()

    gather_finish(gs_all, 1)
    part_l[...] = nn(taps_t[...], gs_all[...].reshape(WIDE, CH))

    for way in range(2):
        ring_l[way, 0] = own_rows(part_l, KPAD, way, 0).astype(BF16)
        hop(*lat_ring, way, 0).start()

    for t in range(NZ - 1):
        for ring, part, rows, out in ((conv_ring, part_c, CROWS, conv_out), (lat_ring, part_l, KPAD, lat_out)):
            for way in range(2):
                buf = ring[0]
                local_wait(buf.at[way, t + 1], ring[2].at[way, t])
                total = buf[way, t + 1].astype(F32) + own_rows(part, rows, way, t + 1)
                if t < NZ - 2:
                    buf[way, t + 1] = total.astype(BF16)
                    hop(*ring, way, t + 1).start()
                else:
                    out[:, way * HALF:(way + 1) * HALF] = total

    for k in range(8):
        d, sec = tap_target(k)

        @pl.when(jnp.logical_or(d != dp, sec != s))
        def _():
            tap_copy(k).wait_send()

    @pl.when(even)
    def _():
        for j in range(16):
            tap_pass(j).wait_send()

    for i in range(NZ):
        for way in z_ways(i):
            w_send_z(i, way).wait_send()
        for way in range(2):
            w_send_x(i, way).wait_send()
        w_send_far(i).wait_send()

    @pl.when(is_last)
    def _():
        for img in range(4):
            @pl.when(home(img) != dp)
            def _():
                oh_copy(img).wait_send()

    for c in range(NCH):
        @pl.when(s < SECTIONS - 1)
        def _():
            x_copy(c).wait_send()

        @pl.when(s > 0)
        def _():
            g_copy(c).wait_send()

        @pl.when(has_up)
        def _():
            halo_up(c).wait_send()
            rim_up(c).wait_send()

        @pl.when(has_down)
        def _():
            halo_down(c).wait_send()
            rim_down(c).wait_send()

    for kind, buf in enumerate((gp_all, gs_all, ext_all)):
        gather_sent(buf, kind)
    for way in range(2):
        for copy in slice_copies(way):
            copy.wait_send()
        slice_far(way).wait_send()
    for way in range(2):
        for t in range(NZ - 1):
            hop(*conv_ring, way, t).wait_send()
            hop(*lat_ring, way, t).wait_send()


def head_call(taps, lat, w, cls, counts, labels):
    dma = pltpu.SemaphoreType.DMA
    hbm = pl.BlockSpec(memory_space=pl.ANY)
    vmem = pl.BlockSpec(memory_space=pltpu.VMEM)
    smem = pl.BlockSpec(memory_space=pltpu.SMEM)
    return pl.pallas_call(
        head_kernel,
        out_shape=(
            jax.ShapeDtypeStruct((CROWS, CH), F32),
            jax.ShapeDtypeStruct((KPAD, CH), F32),
        ),
        in_specs=[vmem, vmem, hbm, vmem, smem, vmem],
        out_specs=(vmem, vmem),
        scratch_shapes=[
            pltpu.VMEM((8, 16, KW), BF16),
            pltpu.VMEM((PIX, KW), BF16),
            pltpu.VMEM((KW, CH), BF16),
            pltpu.VMEM((9, CH, CH), BF16),
            pltpu.VMEM((PIX, CH), F32),
            pltpu.VMEM((PIX + 2 * COLS, CH), BF16),
            pltpu.VMEM((PIX, CH), BF16),
            pltpu.VMEM((PIX, CH), BF16),
            pltpu.VMEM((PIX, CH), BF16),
            pltpu.VMEM((PIX, CH), F32),
            pltpu.VMEM((3, PIX, CH), F32),
            pltpu.VMEM((3, PIX, CH), BF16),
            pltpu.VMEM((2, COLS, CH), BF16),
            pltpu.VMEM((2, COLS, CH), BF16),
            pltpu.VMEM((2, 2 * COLS, CPAD), BF16),
            pltpu.VMEM((PIX, CPAD), BF16),
            pltpu.VMEM((NX, PIX + 2 * COLS, CH), BF16),
            pltpu.VMEM((NX, PIX, XL), BF16),
            pltpu.VMEM((2, FARROWS, XL), BF16),
            pltpu.VMEM((NX, PIX, CH), BF16),
            pltpu.VMEM((NX, PIX, CH), BF16),
            pltpu.VMEM((3, WIDE, CH), BF16),
            pltpu.VMEM((3, CH, WIDE), BF16),
            pltpu.VMEM((XL, WIDE), BF16),
            pltpu.VMEM((XC, CH), F32),
            pltpu.VMEM((XL, CH), F32),
            pltpu.VMEM((2, NZ, CROWS, HALF), BF16),
            pltpu.VMEM((2, NZ, KPAD, HALF), BF16),
            dma((1,)),
            dma((8,)),
            dma((16,)),
            dma((16,)),
            dma((2, NZ)),
            dma((2, NZ)),
            dma((NZ,)),
            dma((GROUPS,)),
            dma((4,)),
            dma((4,)),
            dma((NCH,)),
            dma((NCH,)),
            dma((2, NCH)),
            dma((2, NCH)),
            dma((NCH,)),
            dma((NCH,)),
            dma((2, NCH)),
            dma((2, NCH)),
            pltpu.SemaphoreType.REGULAR,
            dma((6,)),
            dma((6,)),
            dma((3, 4)),
            dma((3, 4)),
            dma((2, NZ - 1)),
            dma((2, NZ - 1)),
            dma((2, NZ - 1)),
            dma((2, NZ - 1)),
        ],
        compiler_params=pltpu.CompilerParams(
            collective_id=0, has_side_effects=True, vmem_limit_bytes=62 << 20
        ),
    )(taps, lat, w, cls, counts, labels)


def on_device(tap_maps, lateral_weight, conv_weight, classifier, tile_counts, labels):
    levels, micros, here, width = tap_maps.shape
    taps = tap_maps.reshape(levels * micros, here, width)
    lat = jnp.pad(lateral_weight[0], ((0, KPAD - KROWS), (0, 0)))
    conv_grad, lateral_grad = head_call(
        taps, lat, conv_weight.reshape(9, CH, CH), classifier, tile_counts, labels
    )
    return (conv_grad[None], lateral_grad[None, :KROWS])


def solution(mesh):
    placed = (
        P(None, None, ("dp", "section"), None),
        P("section", "dp", None),
        P("section", None, None),
        P(),
        P("dp", None),
        P(None, "dp"),
    )
    return jax.shard_map(
        on_device,
        mesh=mesh,
        in_specs=placed,
        out_specs=(P("section", "dp", None), P("section", "dp", None)),
        check_vma=False,
    )
```

```python
import jax
import jax.numpy as jnp
from jax import lax
from jax.experimental import pallas as pl
from jax.experimental.pallas import tpu as pltpu
from jax.sharding import PartitionSpec as P

MESH = pl.DeviceIdType.MESH
F32 = jnp.float32
BF16 = jnp.bfloat16
NZ = 8
NX = 4
COLS = 64
ROWS = 4
PIX = ROWS * COLS
CH = 768
CK = 256
NCH = CH // CK
KROWS = 100
KPAD = 112
GROUPS = NX * NZ
KW = KPAD * GROUPS
SECTIONS = 8
WIDE = NX * PIX
CROWS = 9 * CH // GROUPS
XC, XL = CROWS * NZ, KPAD * NZ
UNIT = XC // 9
HALF = CH // 2
FARROWS = PIX // 2
CLASSES = 150
CPAD = 256


def nt(a, b):
    return lax.dot_general(a, b, (((1,), (1,)), ((), ())), preferred_element_type=F32)


def tn(a, b):
    return lax.dot_general(a, b, (((0,), (0,)), ((), ())), preferred_element_type=F32)


def nn(a, b):
    return jnp.dot(a, b, preferred_element_type=F32)


def head_kernel(
    tap_ref, lat_ref, w_hbm, cls_ref, counts_ref, labels_ref, conv_out, lat_out,
    tap_pad, wl, w, gx, lat_send, lat_far, lat_near, lat_nat, lat_img,
    ext, xin, xout, gin, dsilu, acc, gpv, rim_out, rim_in, oh_own, oh,
    ext_all, taps_all, gs_img, gp_all, gs_all, gpv_all, cols_t, taps_t, part_c, part_l, ring_c, ring_l,
    local_sem, tap_send, tap_recv, pass_send, pass_recv, wz_send, w_recv,
    lf_send, lf_recv, ln_send, ln_recv, lz_send, lz_recv, oh_send, oh_recv,
    x_send, x_recv, halo_send, halo_recv, g_send, g_recv, rim_send, rim_recv,
    early_sem, gz_send, gz_recv, a_send, a_recv, rc_send, rc_recv, rl_send, rl_recv,
):
    dp = lax.axis_index("dp")
    s = lax.axis_index("section")
    x, z = dp // NZ, dp % NZ
    odd = x % 2
    half = (z % 2 + odd) % 2
    image = z // 2
    has_up = jnp.logical_not(jnp.logical_and(half == 0, x == 0))
    has_down = jnp.logical_not(jnp.logical_and(half == 1, x == NX - 1))
    pair = dp + 1 - 2 * (z % 2)
    up = jnp.where(half == 1, pair, dp - NZ)
    down = jnp.where(half == 0, pair, dp + NZ)
    src_half = z // 4
    is_first, is_last = s == 0, s == SECTIONS - 1
    even = s % 2 == 0
    z_next, z_prev = x * NZ + (z + 1) % NZ, x * NZ + (z + NZ - 1) % NZ
    x_left, x_right, x_far = (x + NX - 1) % NX, (x + 1) % NX, (x + 2) % NX
    left, right = x_left * NZ + z, x_right * NZ + z

    def home(img):
        return x * NZ + 2 * img + (src_half + odd) % 2

    def remote(src, dst, send, recv, d, sec):
        return pltpu.make_async_remote_copy(
            src_ref=src, dst_ref=dst, send_sem=send, recv_sem=recv,
            device_id={"dp": d, "section": sec}, device_id_type=MESH,
        )

    def local_wait(ref, sem):
        pltpu.make_async_copy(ref, ref, sem).wait()

    w_copy = pltpu.make_async_copy(w_hbm, w, local_sem.at[0])
    w_copy.start()

    barrier = pltpu.get_barrier_semaphore()

    def greet(d, sec):
        pl.semaphore_signal(barrier, inc=1, device_id={"dp": d, "section": sec}, device_id_type=MESH)

    @pl.when(even)
    def _():
        for xx in range(NX):
            for sec in range(SECTIONS):
                @pl.when(jnp.logical_or(xx != x, sec != s))
                def _():
                    greet(xx * NZ + z, sec)

    for d in (left, right, z_next, z_prev):
        greet(d, s)

    @pl.when(has_up)
    def _():
        greet(up, s)

    @pl.when(has_down)
    def _():
        greet(down, s)

    @pl.when(s > 0)
    def _():
        greet(dp, s - 1)

    @pl.when(s < SECTIONS - 1)
    def _():
        greet(dp, s + 1)

    def native(r):
        return x * NZ + half * 4 + r

    for r in range(4):
        for d in (native(r), home(r)):
            @pl.when(d != dp)
            def _():
                greet(d, s)

    flat = tap_ref[...].reshape(8 * 16, GROUPS * KROWS).astype(F32)
    lane = lax.broadcasted_iota(jnp.int32, (8 * 16, 128), 1)
    for tile in range(KW // 128):
        first = tile * 128
        total = jnp.zeros((8 * 16, 128), F32)
        for g in range(first // KPAD, min((first + 127) // KPAD + 1, GROUPS)):
            lo = first - (KPAD - KROWS) * g
            start = min(max(lo // 128 * 128, 0), GROUPS * KROWS - 256)
            moved = pltpu.roll(flat[:, start:start + 256], (start - lo) % 256, 1)[:, :128]
            inside = jnp.logical_and(lane + first >= KPAD * g, lane + first < KPAD * g + KROWS)
            total = jnp.where(inside, moved, total)
        tap_pad[:, :, first:first + 128] = total.astype(BF16).reshape(8, 16, 128)

    def w_rows(zz):
        return wl.at[pl.ds(pl.multiple_of(zz * KPAD, 16), KPAD), :]

    wl[pl.ds(pl.multiple_of(z * KPAD, 16), KPAD), :] = lat_ref[...]

    need = jnp.where(even, 4 + 15, 4 + 16)
    for flag in (has_up, has_down, s > 0, s < SECTIONS - 1):
        need += flag.astype(jnp.int32)
    for r in range(4):
        need += (native(r) != dp).astype(jnp.int32) + (home(r) != dp).astype(jnp.int32)
    pl.semaphore_wait(barrier, need)

    def tap_cell(xx, j):
        return taps_all.at[xx, pl.ds(pl.multiple_of(j * 16, 16), 16), :]

    def tap_src(k, xx):
        return tap_pad.at[k, :, pl.ds(xx * XL, XL)]

    def tap_copy(k, xx):
        slot = (k % 2) * SECTIONS + s
        return remote(
            tap_src(k, xx), tap_cell(x, slot), tap_send.at[k, xx], tap_recv.at[x, slot], xx * NZ + z, k // 2 * 2
        )

    def tap_pass(xx):
        return remote(taps_all.at[xx], taps_all.at[xx], pass_send.at[xx], pass_recv.at[xx], dp, s + 1)

    def elsewhere(k, xx):
        return jnp.logical_or(xx != x, k // 2 * 2 != s)

    for k in range(8):
        for xx in range(NX):
            @pl.when(elsewhere(k, xx))
            def _():
                tap_copy(k, xx).start()

            @pl.when(jnp.logical_not(elsewhere(k, xx)))
            def _():
                slot = (k % 2) * SECTIONS + s
                pltpu.make_async_copy(tap_src(k, xx), tap_cell(x, slot), tap_recv.at[x, slot]).start()

    order = (0, -1, 1, -2, 2, -3, 3, -4)

    def ring_z(i):
        return (z + NZ + order[i]) % NZ

    def w_send_z(i, way):
        block = w_rows(ring_z(i))
        return remote(block, block, wz_send.at[way, i], w_recv.at[ring_z(i)], z_next if way == 0 else z_prev, s)

    def z_ways(i):
        ways = []
        if order[i] <= 0 and order[i] > -4:
            ways.append(0)
        if order[i] >= 0 and order[i] < 3:
            ways.append(1)
        return ways

    for i in range(NZ):
        if i > 0:
            local_wait(w_rows(ring_z(i)), w_recv.at[ring_z(i)])
        for way in z_ways(i):
            w_send_z(i, way).start()

    def oh_rows(r):
        return oh.at[pl.ds(pl.multiple_of(r * COLS, COLS), COLS), :]

    def oh_src(img):
        return oh_own.at[img // 2, pl.ds((img % 2) * COLS, COLS), :]

    def oh_copy(img):
        return remote(oh_src(img), oh_rows(z % 4), oh_send.at[img], oh_recv.at[z % 4], home(img), s)

    @pl.when(is_last)
    def _():
        sub = lax.broadcasted_iota(jnp.int32, (CPAD, 2 * COLS), 0)
        tile_of = lax.broadcasted_iota(jnp.int32, (CPAD, 2 * COLS), 1) // COLS
        for micro in range(2):
            count = counts_ref[0, micro]
            share = 1.0 / (count.astype(F32) * (COLS * GROUPS * 2))
            weight = jnp.where(tile_of < count, share, 0.0)
            hot = jnp.where(sub == labels_ref[micro:micro + 1, :], 1.0, 0.0)
            oh_own[micro] = jnp.where(sub == CPAD - 1, weight, hot).T.astype(BF16)
        for img in range(4):
            @pl.when(home(img) != dp)
            def _():
                oh_copy(img).start()

            @pl.when(home(img) == dp)
            def _():
                pltpu.make_async_copy(oh_src(img), oh_rows(z % 4), oh_recv.at[z % 4]).start()

    @pl.when(jnp.logical_not(has_up))
    def _():
        ext[0:COLS, :] = jnp.zeros((COLS, CH), BF16)

    @pl.when(jnp.logical_not(has_down))
    def _():
        ext[COLS + PIX:, :] = jnp.zeros((COLS, CH), BF16)

    @pl.when(even)
    def _():
        for xx in range(NX):
            for j in range(2 * SECTIONS):
                local_wait(tap_cell(xx, j), tap_recv.at[xx, j])
            tap_pass(xx).start()

    @pl.when(jnp.logical_not(even))
    def _():
        for xx in range(NX):
            local_wait(taps_all.at[xx], pass_recv.at[xx])

    first_rows, last_rows = pl.ds(0, FARROWS), pl.ds(FARROWS, FARROWS)
    half_rows = (first_rows, last_rows)

    def far_copy(way):
        return remote(
            lat_send.at[2, half_rows[way]], lat_far.at[way], lf_send.at[way], lf_recv.at[way],
            right if way == 0 else left, s,
        )

    def near_copy(way, part):
        return remote(
            lat_send.at[way, half_rows[part]], lat_near.at[way, half_rows[part]],
            ln_send.at[way, part], ln_recv.at[way, part], right if way == 0 else left, s,
        )

    lat_send[2] = nn(taps_all[x_far], wl[...]).astype(BF16)
    for way in range(2):
        far_copy(way).start()
    for way in range(2):
        acc[way] = nn(taps_all[x_right if way == 0 else x_left], wl[...])
        rows = half_rows[1 - way]
        lat_send[way, rows] = acc[way, rows].astype(BF16)
        near_copy(way, 1 - way).start()
    acc[2] = nn(taps_all[x], wl[...])
    for way in range(2):
        rows = half_rows[way]
        local_wait(lat_far.at[way], lf_recv.at[way])
        lat_send[way, rows] = (acc[way, rows] + lat_far[way].astype(F32)).astype(BF16)
        near_copy(way, way).start()
    for part in range(2):
        rows = half_rows[part]
        for way in (1 - part, part):
            local_wait(lat_near.at[way, rows], ln_recv.at[way, part])
        lat_nat[rows] = (
            acc[2, rows] + lat_near[0, rows].astype(F32) + lat_near[1, rows].astype(F32)
        ).astype(BF16)

    def band(ref, j):
        return ref.at[pl.ds(pl.multiple_of(j * COLS, COLS), COLS), :]

    def lat_copy(img):
        return remote(band(lat_nat, img), band(lat_img, z % 4), lz_send.at[img], lz_recv.at[z % 4], home(img), s)

    for img in range(4):
        @pl.when(home(img) != dp)
        def _():
            lat_copy(img).start()

        @pl.when(home(img) == dp)
        def _():
            pltpu.make_async_copy(band(lat_nat, img), band(lat_img, z % 4), lz_recv.at[z % 4]).start()

    for r in range(4):
        local_wait(band(lat_img, r), lz_recv.at[r])
    w_copy.wait()

    def lanes(c):
        return pl.ds(c * CK, CK)

    def x_copy(c):
        return pltpu.make_async_remote_copy(
            src_ref=xout.at[:, lanes(c)], dst_ref=xin.at[:, lanes(c)],
            send_sem=x_send.at[c], recv_sem=x_recv.at[c],
            device_id={"dp": dp, "section": s + 1}, device_id_type=MESH,
        )

    def halo_up(c):
        return pltpu.make_async_remote_copy(
            src_ref=ext.at[pl.ds(COLS, COLS), lanes(c)], dst_ref=ext.at[pl.ds(COLS + PIX, COLS), lanes(c)],
            send_sem=halo_send.at[0, c], recv_sem=halo_recv.at[1, c],
            device_id={"dp": up, "section": s}, device_id_type=MESH,
        )

    def halo_down(c):
        return pltpu.make_async_remote_copy(
            src_ref=ext.at[pl.ds(PIX, COLS), lanes(c)], dst_ref=ext.at[pl.ds(0, COLS), lanes(c)],
            send_sem=halo_send.at[1, c], recv_sem=halo_recv.at[0, c],
            device_id={"dp": down, "section": s}, device_id_type=MESH,
        )

    def take_x(c):
        cols = slice(c * CK, (c + 1) * CK)

        @pl.when(is_first)
        def _():
            ext[COLS:COLS + PIX, cols] = lat_img[:, cols]

        @pl.when(s > 0)
        def _():
            local_wait(xin.at[:, lanes(c)], x_recv.at[c])
            ext[COLS:COLS + PIX, cols] = (xin[:, cols].astype(F32) + lat_img[:, cols].astype(F32)).astype(BF16)

        @pl.when(has_up)
        def _():
            halo_up(c).start()

        @pl.when(has_down)
        def _():
            halo_down(c).start()

    def wait_halo(c):
        @pl.when(has_up)
        def _():
            local_wait(ext.at[pl.ds(0, COLS), lanes(c)], halo_recv.at[0, c])

        @pl.when(has_down)
        def _():
            local_wait(ext.at[pl.ds(COLS + PIX, COLS), lanes(c)], halo_recv.at[1, c])

    def conv_part(c, dr, dc, ncols):
        rows = (1 + dr) * COLS
        return nn(
            ext[rows:rows + PIX, c * CK:(c + 1) * CK],
            w[(dr + 1) * 3 + dc + 1, c * CK:(c + 1) * CK, ncols],
        )

    every = slice(0, CH)

    def conv_inner(c, start):
        for dc in (-1, 0, 1):
            term = conv_part(c, 0, dc, every)
            if start:
                acc[dc + 1] = term
            else:
                acc[dc + 1] += term

    def conv_outer(c):
        for dc in (-1, 0, 1):
            acc[dc + 1] += conv_part(c, -1, dc, every) + conv_part(c, 1, dc, every)

    col = lax.broadcasted_iota(jnp.int32, (PIX, CK), 0) % COLS

    def before(v):
        return jnp.where(col == 0, 0.0, pltpu.roll(v, 1, 0))

    def after(v):
        return jnp.where(col == COLS - 1, 0.0, pltpu.roll(v, PIX - 1, 0))

    take_x(0)
    take_x(1)
    conv_inner(0, True)
    wait_halo(0)
    conv_outer(0)
    take_x(2)
    conv_inner(1, False)
    conv_inner(2, False)
    wait_halo(1)
    conv_outer(1)
    wait_halo(2)
    for n in range(NCH):
        ncols = slice(n * CK, (n + 1) * CK)
        parts = [
            acc[dc + 1, :, ncols] + conv_part(2, -1, dc, ncols) + conv_part(2, 1, dc, ncols)
            for dc in (-1, 0, 1)
        ]
        pre = before(parts[0]) + parts[1] + after(parts[2])
        sig = 1.0 / (1.0 + jnp.exp(-pre))
        xout[:, ncols] = (pre * sig).astype(BF16)

        @pl.when(s < SECTIONS - 1)
        def _():
            x_copy(n).start()

        dsilu[:, ncols] = sig * (1.0 + pre * (1.0 - sig))

    def gather_copy(buf, kind, way):
        return remote(
            buf.at[x], buf.at[x], a_send.at[kind, way], a_recv.at[kind, way], right if way == 0 else left, s
        )

    def gather_far(buf, kind, way):
        rows = buf.shape[1] // 2
        block = buf.at[x_left if way == 0 else x_right, pl.ds(way * rows, rows), :]
        return remote(
            block, block, a_send.at[kind, 2 + way], a_recv.at[kind, 2 + way], right if way == 0 else left, s
        )

    def gather_start(buf, kind):
        for way in range(2):
            gather_copy(buf, kind, way).start()

    def gather_forward(buf, kind):
        for way in range(2):
            local_wait(buf.at[x_left if way == 0 else x_right], a_recv.at[kind, way])
            gather_far(buf, kind, way).start()

    def gather_finish(buf, kind):
        rows = buf.shape[1] // 2
        for way in range(2):
            local_wait(buf.at[x_far, pl.ds(way * rows, rows), :], a_recv.at[kind, 2 + way])

    def gather_sent(buf, kind):
        for way in range(2):
            gather_copy(buf, kind, way).wait_send()
            gather_far(buf, kind, way).wait_send()

    def early_start():
        ext_all[x] = ext[...]
        gather_start(ext_all, 2)

    def early_finish():
        gather_finish(ext_all, 2)

        @pl.loop(0, NX)
        def _(src):
            lanes_of = pl.ds(pl.multiple_of(src * PIX, PIX), PIX)
            for dr in range(3):
                cols_t[dr, :, lanes_of] = ext_all[src, dr * COLS:dr * COLS + PIX, :].T
            taps_t[:, lanes_of] = taps_all[src].T

    @pl.when(jnp.logical_and(s < 6, s % 2 == 1))
    def _():
        pl.semaphore_signal(early_sem, inc=1, device_id={"dp": dp, "section": s - 1}, device_id_type=MESH)

    @pl.when(jnp.logical_and(s < 6, s % 2 == 0))
    def _():
        pl.semaphore_wait(early_sem, 1)

    @pl.when(s < 6)
    def _():
        early_start()

    @pl.when(s < 4)
    def _():
        gather_forward(ext_all, 2)
        early_finish()

    @pl.when(is_last)
    def _():
        for r in range(4):
            local_wait(oh_rows(r), oh_recv.at[r])
        logits = nn(xout[...], cls_ref[...])
        spot = lax.broadcasted_iota(jnp.int32, (PIX, CPAD), 1)
        expo = jnp.exp(logits)
        probs = expo / jnp.sum(expo, axis=-1, keepdims=True)
        marks = oh[...].astype(F32)
        weight = jnp.sum(jnp.where(spot == CPAD - 1, marks, 0.0), axis=-1, keepdims=True)
        grad_logits = ((probs - marks[:, :CLASSES]) * weight).astype(BF16)
        gx[...] = nt(grad_logits, cls_ref[...])

    def g_copy(c):
        return pltpu.make_async_remote_copy(
            src_ref=gs_img.at[:, lanes(c)], dst_ref=gin.at[:, lanes(c)],
            send_sem=g_send.at[c], recv_sem=g_recv.at[c],
            device_id={"dp": dp, "section": s - 1}, device_id_type=MESH,
        )

    def rim_up(c):
        return pltpu.make_async_remote_copy(
            src_ref=rim_out.at[0, :, lanes(c)], dst_ref=rim_in.at[1, :, lanes(c)],
            send_sem=rim_send.at[0, c], recv_sem=rim_recv.at[1, c],
            device_id={"dp": up, "section": s}, device_id_type=MESH,
        )

    def rim_down(c):
        return pltpu.make_async_remote_copy(
            src_ref=rim_out.at[1, :, lanes(c)], dst_ref=rim_in.at[0, :, lanes(c)],
            send_sem=rim_send.at[1, c], recv_sem=rim_recv.at[0, c],
            device_id={"dp": down, "section": s}, device_id_type=MESH,
        )

    def take_g(c):
        cols = slice(c * CK, (c + 1) * CK)

        @pl.when(s < SECTIONS - 1)
        def _():
            local_wait(gin.at[:, lanes(c)], g_recv.at[c])
            gx[:, cols] = gin[:, cols].astype(F32)

        grad_pre = (gx[:, cols] * dsilu[:, cols]).astype(BF16).astype(F32)
        gpv[0, :, cols] = after(grad_pre).astype(BF16)
        gpv[1, :, cols] = grad_pre.astype(BF16)
        gp_all[x, :, cols] = grad_pre.astype(BF16)
        gpv[2, :, cols] = before(grad_pre).astype(BF16)

    def back_part(c, dr, krows):
        total = None
        for dc in (-1, 0, 1):
            term = nt(
                gpv[dc + 1, :, c * CK:(c + 1) * CK],
                w[(dr + 1) * 3 + dc + 1, krows, c * CK:(c + 1) * CK],
            )
            total = term if total is None else total + term
        return total

    take_g(0)
    for dr in (-1, 0, 1):
        acc[dr + 1] = back_part(0, dr, every)
    take_g(1)
    for dr in (-1, 0, 1):
        acc[dr + 1] += back_part(1, dr, every)
    take_g(2)
    for n in range(NCH):
        ncols = slice(n * CK, (n + 1) * CK)
        upper = acc[0, :, ncols] + back_part(2, -1, ncols)
        acc[0, :, ncols] = upper
        rim_out[0, :, ncols] = upper[0:COLS].astype(BF16)
        lower = acc[2, :, ncols] + back_part(2, 1, ncols)
        acc[2, :, ncols] = lower
        rim_out[1, :, ncols] = lower[PIX - COLS:].astype(BF16)

        @pl.when(has_up)
        def _():
            rim_up(n).start()

        @pl.when(has_down)
        def _():
            rim_down(n).start()

    acc[1] += back_part(2, 0, every)
    for n in range(NCH):
        ncols = slice(n * CK, (n + 1) * CK)
        acc[1, 0:PIX - COLS, ncols] += acc[0, COLS:, ncols]
        acc[1, COLS:, ncols] += acc[2, 0:PIX - COLS, ncols]

        @pl.when(has_up)
        def _():
            local_wait(rim_in.at[0, :, lanes(n)], rim_recv.at[0, n])
            acc[1, 0:COLS, ncols] += rim_in[0, :, ncols].astype(F32)

        @pl.when(has_down)
        def _():
            local_wait(rim_in.at[1, :, lanes(n)], rim_recv.at[1, n])
            acc[1, PIX - COLS:, ncols] += rim_in[1, :, ncols].astype(F32)

        gs_img[:, ncols] = acc[1, :, ncols].astype(BF16)

        @pl.when(s > 0)
        def _():
            g_copy(n).start()

    def gz_copy(r):
        return remote(
            band(gs_img, r), band(gs_all.at[x], image), gz_send.at[r], gz_recv.at[image], native(r), s
        )

    for r in range(4):
        @pl.when(native(r) != dp)
        def _():
            gz_copy(r).start()

        @pl.when(native(r) == dp)
        def _():
            pltpu.make_async_copy(band(gs_img, r), band(gs_all.at[x], image), gz_recv.at[image]).start()

    gather_start(gp_all, 0)

    @pl.when(s >= 6)
    def _():
        early_start()

    gather_forward(gp_all, 0)
    for img in range(4):
        local_wait(band(gs_all.at[x], img), gz_recv.at[img])
    gather_start(gs_all, 1)

    @pl.when(s >= 4)
    def _():
        gather_forward(ext_all, 2)

    whole_col = lax.broadcasted_iota(jnp.int32, (PIX, CH), 0) % COLS

    def spread(src):
        rows = pl.ds(pl.multiple_of(src * PIX, PIX), PIX)
        value = gp_all[src].astype(F32)
        gpv_all[0, rows, :] = jnp.where(whole_col == COLS - 1, 0.0, pltpu.roll(value, PIX - 1, 0)).astype(BF16)
        gpv_all[1, rows, :] = gp_all[src]
        gpv_all[2, rows, :] = jnp.where(whole_col == 0, 0.0, pltpu.roll(value, 1, 0)).astype(BF16)

    spread(x)
    spread(x_left)
    spread(x_right)
    gather_forward(gs_all, 1)
    gather_finish(gp_all, 0)
    spread(x_far)

    @pl.when(s >= 4)
    def _():
        early_finish()

    @pl.loop(0, 9)
    def _(u):
        unit = 9 * x + u
        o = unit // 4
        chans = pl.ds(pl.multiple_of((unit % 4) * UNIT, UNIT), UNIT)
        part_c[pl.ds(pl.multiple_of(u * UNIT, UNIT), UNIT), :] = nn(cols_t[o // 3, chans, :], gpv_all[o % 3])

    def slice_at(way, t):
        return (z + NZ - 1 - t) % NZ if way == 0 else (z + 1 + t) % NZ

    def own_rows(part, rows, way, t):
        at = pl.ds(pl.multiple_of(slice_at(way, t) * rows, 8), rows)
        return part[at, way * HALF:(way + 1) * HALF]

    def hop(ring, send, recv, way, t):
        return pltpu.make_async_remote_copy(
            src_ref=ring.at[way, t], dst_ref=ring.at[way, t + 1],
            send_sem=send.at[way, t], recv_sem=recv.at[way, t],
            device_id={"dp": z_next if way == 0 else z_prev, "section": s}, device_id_type=MESH,
        )

    conv_ring = (ring_c, rc_send, rc_recv)
    lat_ring = (ring_l, rl_send, rl_recv)
    for way in range(2):
        ring_c[way, 0] = own_rows(part_c, CROWS, way, 0).astype(BF16)
        hop(*conv_ring, way, 0).start()

    gather_finish(gs_all, 1)
    part_l[...] = nn(taps_t[...], gs_all[...].reshape(WIDE, CH))

    for way in range(2):
        ring_l[way, 0] = own_rows(part_l, KPAD, way, 0).astype(BF16)
        hop(*lat_ring, way, 0).start()

    for t in range(NZ - 1):
        for ring, part, rows, out in ((conv_ring, part_c, CROWS, conv_out), (lat_ring, part_l, KPAD, lat_out)):
            for way in range(2):
                buf = ring[0]
                local_wait(buf.at[way, t + 1], ring[2].at[way, t])
                total = buf[way, t + 1].astype(F32) + own_rows(part, rows, way, t + 1)
                if t < NZ - 2:
                    buf[way, t + 1] = total.astype(BF16)
                    hop(*ring, way, t + 1).start()
                else:
                    out[:, way * HALF:(way + 1) * HALF] = total

    for k in range(8):
        for xx in range(NX):
            @pl.when(elsewhere(k, xx))
            def _():
                tap_copy(k, xx).wait_send()

    @pl.when(even)
    def _():
        for xx in range(NX):
            tap_pass(xx).wait_send()

    for i in range(NZ):
        for way in z_ways(i):
            w_send_z(i, way).wait_send()
    for way in range(2):
        far_copy(way).wait_send()
        for part in range(2):
            near_copy(way, part).wait_send()
    for r in range(4):
        @pl.when(home(r) != dp)
        def _():
            lat_copy(r).wait_send()

    @pl.when(is_last)
    def _():
        for img in range(4):
            @pl.when(home(img) != dp)
            def _():
                oh_copy(img).wait_send()

    for c in range(NCH):
        @pl.when(s < SECTIONS - 1)
        def _():
            x_copy(c).wait_send()

        @pl.when(s > 0)
        def _():
            g_copy(c).wait_send()

        @pl.when(has_up)
        def _():
            halo_up(c).wait_send()
            rim_up(c).wait_send()

        @pl.when(has_down)
        def _():
            halo_down(c).wait_send()
            rim_down(c).wait_send()

    for kind, buf in enumerate((gp_all, gs_all, ext_all)):
        gather_sent(buf, kind)
    for r in range(4):
        @pl.when(native(r) != dp)
        def _():
            gz_copy(r).wait_send()

    for way in range(2):
        for t in range(NZ - 1):
            hop(*conv_ring, way, t).wait_send()
            hop(*lat_ring, way, t).wait_send()


def head_call(taps, lat, w, cls, counts, labels):
    dma = pltpu.SemaphoreType.DMA
    hbm = pl.BlockSpec(memory_space=pl.ANY)
    vmem = pl.BlockSpec(memory_space=pltpu.VMEM)
    smem = pl.BlockSpec(memory_space=pltpu.SMEM)
    return pl.pallas_call(
        head_kernel,
        out_shape=(
            jax.ShapeDtypeStruct((CROWS, CH), F32),
            jax.ShapeDtypeStruct((KPAD, CH), F32),
        ),
        in_specs=[vmem, vmem, hbm, vmem, smem, vmem],
        out_specs=(vmem, vmem),
        scratch_shapes=[
            pltpu.VMEM((8, 16, KW), BF16),
            pltpu.VMEM((XL, CH), BF16),
            pltpu.VMEM((9, CH, CH), BF16),
            pltpu.VMEM((PIX, CH), F32),
            pltpu.VMEM((3, PIX, CH), BF16),
            pltpu.VMEM((2, FARROWS, CH), BF16),
            pltpu.VMEM((2, PIX, CH), BF16),
            pltpu.VMEM((PIX, CH), BF16),
            pltpu.VMEM((PIX, CH), BF16),
            pltpu.VMEM((PIX + 2 * COLS, CH), BF16),
            pltpu.VMEM((PIX, CH), BF16),
            pltpu.VMEM((PIX, CH), BF16),
            pltpu.VMEM((PIX, CH), BF16),
            pltpu.VMEM((PIX, CH), F32),
            pltpu.VMEM((3, PIX, CH), F32),
            pltpu.VMEM((3, PIX, CH), BF16),
            pltpu.VMEM((2, COLS, CH), BF16),
            pltpu.VMEM((2, COLS, CH), BF16),
            pltpu.VMEM((2, 2 * COLS, CPAD), BF16),
            pltpu.VMEM((PIX, CPAD), BF16),
            pltpu.VMEM((NX, PIX + 2 * COLS, CH), BF16),
            pltpu.VMEM((NX, PIX, XL), BF16),
            pltpu.VMEM((PIX, CH), BF16),
            pltpu.VMEM((NX, PIX, CH), BF16),
            pltpu.VMEM((NX, PIX, CH), BF16),
            pltpu.VMEM((3, WIDE, CH), BF16),
            pltpu.VMEM((3, CH, WIDE), BF16),
            pltpu.VMEM((XL, WIDE), BF16),
            pltpu.VMEM((XC, CH), F32),
            pltpu.VMEM((XL, CH), F32),
            pltpu.VMEM((2, NZ, CROWS, HALF), BF16),
            pltpu.VMEM((2, NZ, KPAD, HALF), BF16),
            dma((1,)),
            dma((8, NX)),
            dma((NX, 2 * SECTIONS)),
            dma((NX,)),
            dma((NX,)),
            dma((2, NZ)),
            dma((NZ,)),
            dma((2,)),
            dma((2,)),
            dma((2, 2)),
            dma((2, 2)),
            dma((4,)),
            dma((4,)),
            dma((4,)),
            dma((4,)),
            dma((NCH,)),
            dma((NCH,)),
            dma((2, NCH)),
            dma((2, NCH)),
            dma((NCH,)),
            dma((NCH,)),
            dma((2, NCH)),
            dma((2, NCH)),
            pltpu.SemaphoreType.REGULAR,
            dma((4,)),
            dma((4,)),
            dma((3, 4)),
            dma((3, 4)),
            dma((2, NZ - 1)),
            dma((2, NZ - 1)),
            dma((2, NZ - 1)),
            dma((2, NZ - 1)),
        ],
        compiler_params=pltpu.CompilerParams(
            collective_id=0, has_side_effects=True, vmem_limit_bytes=62 << 20
        ),
    )(taps, lat, w, cls, counts, labels)


def on_device(tap_maps, lateral_weight, conv_weight, classifier, tile_counts, labels):
    levels, micros, here, width = tap_maps.shape
    taps = tap_maps.reshape(levels * micros, here, width)
    lat = jnp.pad(lateral_weight[0], ((0, KPAD - KROWS), (0, 0)))
    conv_grad, lateral_grad = head_call(
        taps, lat, conv_weight.reshape(9, CH, CH), classifier, tile_counts, labels
    )
    return (conv_grad[None], lateral_grad[None, :KROWS])


def solution(mesh):
    placed = (
        P(None, None, ("dp", "section"), None),
        P("section", "dp", None),
        P("section", None, None),
        P(),
        P("dp", None),
        P(None, "dp"),
    )
    return jax.shard_map(
        on_device,
        mesh=mesh,
        in_specs=placed,
        out_specs=(P("section", "dp", None), P("section", "dp", None)),
        check_vma=False,
    )
```

```python
import jax
import jax.numpy as jnp
from jax import lax
from jax.experimental import pallas as pl
from jax.experimental.pallas import tpu as pltpu
from jax.sharding import PartitionSpec as P

MESH = pl.DeviceIdType.MESH
F32 = jnp.float32
BF16 = jnp.bfloat16
NZ = 8
NX = 4
COLS = 64
ROWS = 4
PIX = ROWS * COLS
CH = 768
CK = 256
NCH = CH // CK
KROWS = 100
KPAD = 112
GROUPS = NX * NZ
KW = KPAD * GROUPS
SECTIONS = 8
WIDE = NX * PIX
CROWS = 9 * CH // GROUPS
XC, XL = CROWS * NZ, KPAD * NZ
UNIT = XC // 9
HALF = CH // 2
FARROWS = PIX // 2
CLASSES = 150
CPAD = 256


def nt(a, b):
    return lax.dot_general(a, b, (((1,), (1,)), ((), ())), preferred_element_type=F32)


def tn(a, b):
    return lax.dot_general(a, b, (((0,), (0,)), ((), ())), preferred_element_type=F32)


def nn(a, b):
    return jnp.dot(a, b, preferred_element_type=F32)


def head_kernel(
    tap_ref, lat_ref, w_hbm, cls_ref, counts_ref, labels_ref, conv_out, lat_out,
    tap_pad, wl, w, gx, lat_send, lat_far, lat_near, lat_nat, lat_img,
    ext, xin, xout, gin, dsilu, acc, gpv, rim_out, rim_in, oh_own, oh,
    lat_halo, x_halo, g_out, g_rim,
    ext_all, taps_all, gs_img, gp_all, gs_all, gpv_all, cols_t, taps_t, part_c, part_l, ring_c, ring_l,
    local_sem, tap_send, tap_recv, pass_send, pass_recv, wz_send, w_recv,
    lf_send, lf_recv, ln_send, ln_recv, lz_send, lz_recv, oh_send, oh_recv,
    x_send, x_recv, halo_send, halo_recv, g_send, g_recv, rim_send, rim_recv,
    lh_send, lh_recv, xh_send, xh_recv, gr_send, gr_recv,
    early_sem, gz_send, gz_recv, a_send, a_recv, rc_send, rc_recv, rl_send, rl_recv,
):
    dp = lax.axis_index("dp")
    s = lax.axis_index("section")
    x, z = dp // NZ, dp % NZ
    odd = x % 2
    half = (z % 2 + odd) % 2
    image = z // 2
    has_up = jnp.logical_not(jnp.logical_and(half == 0, x == 0))
    has_down = jnp.logical_not(jnp.logical_and(half == 1, x == NX - 1))
    pair = dp + 1 - 2 * (z % 2)
    up = jnp.where(half == 1, pair, dp - NZ)
    down = jnp.where(half == 0, pair, dp + NZ)
    src_half = z // 4
    is_first, is_last = s == 0, s == SECTIONS - 1
    even = s % 2 == 0
    sibling = s + 1 - 2 * (s % 2)
    z_next, z_prev = x * NZ + (z + 1) % NZ, x * NZ + (z + NZ - 1) % NZ
    x_left, x_right, x_far = (x + NX - 1) % NX, (x + 1) % NX, (x + 2) % NX
    left, right = x_left * NZ + z, x_right * NZ + z

    def home(img):
        return x * NZ + 2 * img + (src_half + odd) % 2

    def remote(src, dst, send, recv, d, sec):
        return pltpu.make_async_remote_copy(
            src_ref=src, dst_ref=dst, send_sem=send, recv_sem=recv,
            device_id={"dp": d, "section": sec}, device_id_type=MESH,
        )

    def local_wait(ref, sem):
        pltpu.make_async_copy(ref, ref, sem).wait()

    w_copy = pltpu.make_async_copy(w_hbm, w, local_sem.at[0])
    w_copy.start()

    barrier = pltpu.get_barrier_semaphore()

    def greet(d, sec):
        pl.semaphore_signal(barrier, inc=1, device_id={"dp": d, "section": sec}, device_id_type=MESH)

    @pl.when(even)
    def _():
        for xx in range(NX):
            for sec in range(SECTIONS):
                @pl.when(jnp.logical_or(xx != x, sec != s))
                def _():
                    greet(xx * NZ + z, sec)

    for d in (left, right, z_next, z_prev):
        greet(d, s)

    @pl.when(has_up)
    def _():
        greet(up, s)
        greet(up, sibling)

    @pl.when(has_down)
    def _():
        greet(down, s)
        greet(down, sibling)

    @pl.when(s > 0)
    def _():
        greet(dp, s - 1)

    @pl.when(s < SECTIONS - 1)
    def _():
        greet(dp, s + 1)

    def native(r):
        return x * NZ + half * 4 + r

    for r in range(4):
        for d in (native(r), home(r)):
            @pl.when(d != dp)
            def _():
                greet(d, s)

    flat = tap_ref[...].reshape(8 * 16, GROUPS * KROWS).astype(F32)
    lane = lax.broadcasted_iota(jnp.int32, (8 * 16, 128), 1)
    for tile in range(KW // 128):
        first = tile * 128
        total = jnp.zeros((8 * 16, 128), F32)
        for g in range(first // KPAD, min((first + 127) // KPAD + 1, GROUPS)):
            lo = first - (KPAD - KROWS) * g
            start = min(max(lo // 128 * 128, 0), GROUPS * KROWS - 256)
            moved = pltpu.roll(flat[:, start:start + 256], (start - lo) % 256, 1)[:, :128]
            inside = jnp.logical_and(lane + first >= KPAD * g, lane + first < KPAD * g + KROWS)
            total = jnp.where(inside, moved, total)
        tap_pad[:, :, first:first + 128] = total.astype(BF16).reshape(8, 16, 128)

    def w_rows(zz):
        return wl.at[pl.ds(pl.multiple_of(zz * KPAD, 16), KPAD), :]

    wl[pl.ds(pl.multiple_of(z * KPAD, 16), KPAD), :] = lat_ref[...]

    need = jnp.where(even, 4 + 15, 4 + 16)
    for flag in (has_up, has_down, has_up, has_down, s > 0, s < SECTIONS - 1):
        need += flag.astype(jnp.int32)
    for r in range(4):
        need += (native(r) != dp).astype(jnp.int32) + (home(r) != dp).astype(jnp.int32)
    pl.semaphore_wait(barrier, need)

    def tap_cell(xx, j):
        return taps_all.at[xx, pl.ds(pl.multiple_of(j * 16, 16), 16), :]

    def tap_src(k, xx):
        return tap_pad.at[k, :, pl.ds(xx * XL, XL)]

    def tap_copy(k, xx):
        slot = (k % 2) * SECTIONS + s
        return remote(
            tap_src(k, xx), tap_cell(x, slot), tap_send.at[k, xx], tap_recv.at[x, slot], xx * NZ + z, k // 2 * 2
        )

    def tap_pass(xx):
        return remote(taps_all.at[xx], taps_all.at[xx], pass_send.at[xx], pass_recv.at[xx], dp, s + 1)

    def elsewhere(k, xx):
        return jnp.logical_or(xx != x, k // 2 * 2 != s)

    for k in range(8):
        for xx in range(NX):
            @pl.when(elsewhere(k, xx))
            def _():
                tap_copy(k, xx).start()

            @pl.when(jnp.logical_not(elsewhere(k, xx)))
            def _():
                slot = (k % 2) * SECTIONS + s
                pltpu.make_async_copy(tap_src(k, xx), tap_cell(x, slot), tap_recv.at[x, slot]).start()

    order = (0, -1, 1, -2, 2, -3, 3, -4)

    def ring_z(i):
        return (z + NZ + order[i]) % NZ

    def w_send_z(i, way):
        block = w_rows(ring_z(i))
        return remote(block, block, wz_send.at[way, i], w_recv.at[ring_z(i)], z_next if way == 0 else z_prev, s)

    def z_ways(i):
        ways = []
        if order[i] <= 0 and order[i] > -4:
            ways.append(0)
        if order[i] >= 0 and order[i] < 3:
            ways.append(1)
        return ways

    for i in range(NZ):
        if i > 0:
            local_wait(w_rows(ring_z(i)), w_recv.at[ring_z(i)])
        for way in z_ways(i):
            w_send_z(i, way).start()

    def oh_rows(r):
        return oh.at[pl.ds(pl.multiple_of(r * COLS, COLS), COLS), :]

    def oh_src(img):
        return oh_own.at[img // 2, pl.ds((img % 2) * COLS, COLS), :]

    def oh_copy(img):
        return remote(oh_src(img), oh_rows(z % 4), oh_send.at[img], oh_recv.at[z % 4], home(img), s)

    @pl.when(is_last)
    def _():
        sub = lax.broadcasted_iota(jnp.int32, (CPAD, 2 * COLS), 0)
        tile_of = lax.broadcasted_iota(jnp.int32, (CPAD, 2 * COLS), 1) // COLS
        for micro in range(2):
            count = counts_ref[0, micro]
            share = 1.0 / (count.astype(F32) * (COLS * GROUPS * 2))
            weight = jnp.where(tile_of < count, share, 0.0)
            hot = jnp.where(sub == labels_ref[micro:micro + 1, :], 1.0, 0.0)
            oh_own[micro] = jnp.where(sub == CPAD - 1, weight, hot).T.astype(BF16)
        for img in range(4):
            @pl.when(home(img) != dp)
            def _():
                oh_copy(img).start()

            @pl.when(home(img) == dp)
            def _():
                pltpu.make_async_copy(oh_src(img), oh_rows(z % 4), oh_recv.at[z % 4]).start()

    @pl.when(jnp.logical_not(has_up))
    def _():
        ext[0:COLS, :] = jnp.zeros((COLS, CH), BF16)

    @pl.when(jnp.logical_not(has_down))
    def _():
        ext[COLS + PIX:, :] = jnp.zeros((COLS, CH), BF16)

    @pl.when(even)
    def _():
        for xx in range(NX):
            for j in range(2 * SECTIONS):
                local_wait(tap_cell(xx, j), tap_recv.at[xx, j])
            tap_pass(xx).start()

    @pl.when(jnp.logical_not(even))
    def _():
        for xx in range(NX):
            local_wait(taps_all.at[xx], pass_recv.at[xx])

    first_rows, last_rows = pl.ds(0, FARROWS), pl.ds(FARROWS, FARROWS)
    half_rows = (first_rows, last_rows)

    def far_copy(way):
        return remote(
            lat_send.at[2, half_rows[way]], lat_far.at[way], lf_send.at[way], lf_recv.at[way],
            right if way == 0 else left, s,
        )

    def near_copy(way, part):
        return remote(
            lat_send.at[way, half_rows[part]], lat_near.at[way, half_rows[part]],
            ln_send.at[way, part], ln_recv.at[way, part], right if way == 0 else left, s,
        )

    lat_send[2] = nn(taps_all[x_far], wl[...]).astype(BF16)
    for way in range(2):
        far_copy(way).start()
    for way in range(2):
        acc[way] = nn(taps_all[x_right if way == 0 else x_left], wl[...])
        rows = half_rows[1 - way]
        lat_send[way, rows] = acc[way, rows].astype(BF16)
        near_copy(way, 1 - way).start()
    acc[2] = nn(taps_all[x], wl[...])
    for way in range(2):
        rows = half_rows[way]
        local_wait(lat_far.at[way], lf_recv.at[way])
        lat_send[way, rows] = (acc[way, rows] + lat_far[way].astype(F32)).astype(BF16)
        near_copy(way, way).start()
    for part in range(2):
        rows = half_rows[part]
        for way in (1 - part, part):
            local_wait(lat_near.at[way, rows], ln_recv.at[way, part])
        lat_nat[rows] = (
            acc[2, rows] + lat_near[0, rows].astype(F32) + lat_near[1, rows].astype(F32)
        ).astype(BF16)

    def band(ref, j):
        return ref.at[pl.ds(pl.multiple_of(j * COLS, COLS), COLS), :]

    def lat_copy(img):
        return remote(band(lat_nat, img), band(lat_img, z % 4), lz_send.at[img], lz_recv.at[z % 4], home(img), s)

    for img in range(4):
        @pl.when(home(img) != dp)
        def _():
            lat_copy(img).start()

        @pl.when(home(img) == dp)
        def _():
            pltpu.make_async_copy(band(lat_nat, img), band(lat_img, z % 4), lz_recv.at[z % 4]).start()

    for r in range(4):
        local_wait(band(lat_img, r), lz_recv.at[r])

    def lat_up():
        return remote(band(lat_img, 0), lat_halo.at[1], lh_send.at[0], lh_recv.at[1], up, s)

    def lat_down():
        return remote(band(lat_img, ROWS - 1), lat_halo.at[0], lh_send.at[1], lh_recv.at[0], down, s)

    @pl.when(jnp.logical_and(has_up, jnp.logical_not(even)))
    def _():
        lat_up().start()

    @pl.when(jnp.logical_and(has_down, jnp.logical_not(even)))
    def _():
        lat_down().start()

    w_copy.wait()

    def lanes(c):
        return pl.ds(c * CK, CK)

    def x_copy(c):
        return pltpu.make_async_remote_copy(
            src_ref=xout.at[:, lanes(c)], dst_ref=xin.at[:, lanes(c)],
            send_sem=x_send.at[c], recv_sem=x_recv.at[c],
            device_id={"dp": dp, "section": s + 1}, device_id_type=MESH,
        )

    def halo_up(c):
        return pltpu.make_async_remote_copy(
            src_ref=ext.at[pl.ds(COLS, COLS), lanes(c)], dst_ref=ext.at[pl.ds(COLS + PIX, COLS), lanes(c)],
            send_sem=halo_send.at[0, c], recv_sem=halo_recv.at[1, c],
            device_id={"dp": up, "section": s}, device_id_type=MESH,
        )

    def halo_down(c):
        return pltpu.make_async_remote_copy(
            src_ref=ext.at[pl.ds(PIX, COLS), lanes(c)], dst_ref=ext.at[pl.ds(0, COLS), lanes(c)],
            send_sem=halo_send.at[1, c], recv_sem=halo_recv.at[0, c],
            device_id={"dp": down, "section": s}, device_id_type=MESH,
        )

    def edge_up(c):
        return remote(
            xout.at[pl.ds(0, COLS), lanes(c)], x_halo.at[1, :, lanes(c)],
            xh_send.at[0, c], xh_recv.at[1, c], up, s + 1,
        )

    def edge_down(c):
        return remote(
            xout.at[pl.ds(PIX - COLS, COLS), lanes(c)], x_halo.at[0, :, lanes(c)],
            xh_send.at[1, c], xh_recv.at[0, c], down, s + 1,
        )

    def take_edges(c):
        cols = slice(c * CK, (c + 1) * CK)
        for side, flag, rows in ((0, has_up, slice(0, COLS)), (1, has_down, slice(COLS + PIX, 2 * COLS + PIX))):
            @pl.when(flag)
            def _():
                local_wait(x_halo.at[side, :, lanes(c)], xh_recv.at[side, c])
                ext[rows, cols] = (
                    x_halo[side, :, cols].astype(F32) + lat_halo[side, :, cols].astype(F32)
                ).astype(BF16)

    def take_x(c):
        cols = slice(c * CK, (c + 1) * CK)

        @pl.when(is_first)
        def _():
            ext[COLS:COLS + PIX, cols] = lat_img[:, cols]

        @pl.when(s > 0)
        def _():
            local_wait(xin.at[:, lanes(c)], x_recv.at[c])
            ext[COLS:COLS + PIX, cols] = (xin[:, cols].astype(F32) + lat_img[:, cols].astype(F32)).astype(BF16)

        @pl.when(jnp.logical_and(has_up, even))
        def _():
            halo_up(c).start()

        @pl.when(jnp.logical_and(has_down, even))
        def _():
            halo_down(c).start()

    def wait_halo(c):
        @pl.when(has_up)
        def _():
            local_wait(ext.at[pl.ds(0, COLS), lanes(c)], halo_recv.at[0, c])

        @pl.when(has_down)
        def _():
            local_wait(ext.at[pl.ds(COLS + PIX, COLS), lanes(c)], halo_recv.at[1, c])

    def conv_part(c, dr, dc, ncols):
        rows = (1 + dr) * COLS
        return nn(
            ext[rows:rows + PIX, c * CK:(c + 1) * CK],
            w[(dr + 1) * 3 + dc + 1, c * CK:(c + 1) * CK, ncols],
        )

    every = slice(0, CH)

    def conv_inner(c, start):
        for dc in (-1, 0, 1):
            term = conv_part(c, 0, dc, every)
            if start:
                acc[dc + 1] = term
            else:
                acc[dc + 1] += term

    def conv_outer(c):
        for dc in (-1, 0, 1):
            acc[dc + 1] += conv_part(c, -1, dc, every) + conv_part(c, 1, dc, every)

    col = lax.broadcasted_iota(jnp.int32, (PIX, CK), 0) % COLS

    def before(v):
        return jnp.where(col == 0, 0.0, pltpu.roll(v, 1, 0))

    def after(v):
        return jnp.where(col == COLS - 1, 0.0, pltpu.roll(v, PIX - 1, 0))

    def conv_finish(n, chunks, direct):
        ncols = slice(n * CK, (n + 1) * CK)
        parts = []
        for dc in (-1, 0, 1):
            part = acc[dc + 1, :, ncols]
            for c in chunks:
                part += conv_part(c, -1, dc, ncols) + conv_part(c, 1, dc, ncols)
            parts.append(part)
        pre = before(parts[0]) + parts[1] + after(parts[2])
        sig = 1.0 / (1.0 + jnp.exp(-pre))
        xout[:, ncols] = (pre * sig).astype(BF16)

        @pl.when(s < SECTIONS - 1)
        def _():
            x_copy(n).start()

        if direct:
            @pl.when(has_up)
            def _():
                edge_up(n).start()

            @pl.when(has_down)
            def _():
                edge_down(n).start()

        dsilu[:, ncols] = sig * (1.0 + pre * (1.0 - sig))

    @pl.when(even)
    def _():
        take_x(0)
        conv_inner(0, True)
        take_x(1)
        conv_inner(1, False)
        wait_halo(0)
        conv_outer(0)
        take_x(2)
        conv_inner(2, False)
        wait_halo(1)
        conv_outer(1)
        wait_halo(2)
        for n in range(NCH):
            conv_finish(n, (2,), True)

    @pl.when(jnp.logical_not(even))
    def _():
        for c in range(NCH):
            take_x(c)
        for c in range(NCH):
            conv_inner(c, c == 0)

        @pl.when(has_up)
        def _():
            local_wait(lat_halo.at[0], lh_recv.at[0])

        @pl.when(has_down)
        def _():
            local_wait(lat_halo.at[1], lh_recv.at[1])

        for c in range(NCH):
            take_edges(c)
        for n in range(NCH):
            conv_finish(n, range(NCH), False)

    def gather_copy(buf, kind, way):
        return remote(
            buf.at[x], buf.at[x], a_send.at[kind, way], a_recv.at[kind, way], right if way == 0 else left, s
        )

    def gather_far(buf, kind, way):
        rows = buf.shape[1] // 2
        block = buf.at[x_left if way == 0 else x_right, pl.ds(way * rows, rows), :]
        return remote(
            block, block, a_send.at[kind, 2 + way], a_recv.at[kind, 2 + way], right if way == 0 else left, s
        )

    def gather_start(buf, kind):
        for way in range(2):
            gather_copy(buf, kind, way).start()

    def gather_forward(buf, kind):
        for way in range(2):
            local_wait(buf.at[x_left if way == 0 else x_right], a_recv.at[kind, way])
            gather_far(buf, kind, way).start()

    def gather_finish(buf, kind):
        rows = buf.shape[1] // 2
        for way in range(2):
            local_wait(buf.at[x_far, pl.ds(way * rows, rows), :], a_recv.at[kind, 2 + way])

    def gather_sent(buf, kind):
        for way in range(2):
            gather_copy(buf, kind, way).wait_send()
            gather_far(buf, kind, way).wait_send()

    def early_start():
        ext_all[x] = ext[...]
        gather_start(ext_all, 2)

    def early_finish():
        gather_finish(ext_all, 2)

        @pl.loop(0, NX)
        def _(src):
            lanes_of = pl.ds(pl.multiple_of(src * PIX, PIX), PIX)
            for dr in range(3):
                cols_t[dr, :, lanes_of] = ext_all[src, dr * COLS:dr * COLS + PIX, :].T
            taps_t[:, lanes_of] = taps_all[src].T

    @pl.when(jnp.logical_and(s < 6, s % 2 == 1))
    def _():
        pl.semaphore_signal(early_sem, inc=1, device_id={"dp": dp, "section": s - 1}, device_id_type=MESH)

    @pl.when(jnp.logical_and(s < 6, s % 2 == 0))
    def _():
        pl.semaphore_wait(early_sem, 1)

    @pl.when(s < 6)
    def _():
        early_start()

    @pl.when(s < 4)
    def _():
        gather_forward(ext_all, 2)
        early_finish()

    @pl.when(is_last)
    def _():
        for r in range(4):
            local_wait(oh_rows(r), oh_recv.at[r])
        logits = nn(xout[...], cls_ref[...])
        spot = lax.broadcasted_iota(jnp.int32, (PIX, CPAD), 1)
        expo = jnp.exp(logits)
        probs = expo / jnp.sum(expo, axis=-1, keepdims=True)
        marks = oh[...].astype(F32)
        weight = jnp.sum(jnp.where(spot == CPAD - 1, marks, 0.0), axis=-1, keepdims=True)
        grad_logits = ((probs - marks[:, :CLASSES]) * weight).astype(BF16)
        gx[...] = nt(grad_logits, cls_ref[...])

    def g_copy(c):
        return pltpu.make_async_remote_copy(
            src_ref=g_out.at[:, lanes(c)], dst_ref=gin.at[:, lanes(c)],
            send_sem=g_send.at[c], recv_sem=g_recv.at[c],
            device_id={"dp": dp, "section": s - 1}, device_id_type=MESH,
        )

    def rim_up(c):
        return pltpu.make_async_remote_copy(
            src_ref=rim_out.at[0, :, lanes(c)], dst_ref=rim_in.at[1, :, lanes(c)],
            send_sem=rim_send.at[0, c], recv_sem=rim_recv.at[1, c],
            device_id={"dp": up, "section": s}, device_id_type=MESH,
        )

    def rim_down(c):
        return pltpu.make_async_remote_copy(
            src_ref=rim_out.at[1, :, lanes(c)], dst_ref=rim_in.at[0, :, lanes(c)],
            send_sem=rim_send.at[1, c], recv_sem=rim_recv.at[0, c],
            device_id={"dp": down, "section": s}, device_id_type=MESH,
        )

    def take_g(c):
        cols = slice(c * CK, (c + 1) * CK)

        @pl.when(s < SECTIONS - 1)
        def _():
            local_wait(gin.at[:, lanes(c)], g_recv.at[c])
            gx[:, cols] = gin[:, cols].astype(F32)

        for side, flag, rows in ((0, has_up, slice(0, COLS)), (1, has_down, slice(PIX - COLS, PIX))):
            @pl.when(jnp.logical_and(flag, even))
            def _():
                local_wait(g_rim.at[side, :, lanes(c)], gr_recv.at[side, c])
                gx[rows, cols] += g_rim[side, :, cols].astype(F32)

        grad_pre = (gx[:, cols] * dsilu[:, cols]).astype(BF16).astype(F32)
        gpv[0, :, cols] = after(grad_pre).astype(BF16)
        gpv[1, :, cols] = grad_pre.astype(BF16)
        gp_all[x, :, cols] = grad_pre.astype(BF16)
        gpv[2, :, cols] = before(grad_pre).astype(BF16)

    def back_part(c, dr, krows):
        total = None
        for dc in (-1, 0, 1):
            term = nt(
                gpv[dc + 1, :, c * CK:(c + 1) * CK],
                w[(dr + 1) * 3 + dc + 1, krows, c * CK:(c + 1) * CK],
            )
            total = term if total is None else total + term
        return total

    def rim_direct_up(c):
        return remote(
            rim_out.at[0, :, lanes(c)], g_rim.at[1, :, lanes(c)], gr_send.at[0, c], gr_recv.at[1, c], up, s - 1
        )

    def rim_direct_down(c):
        return remote(
            rim_out.at[1, :, lanes(c)], g_rim.at[0, :, lanes(c)], gr_send.at[1, c], gr_recv.at[0, c], down, s - 1
        )

    def send_rims(n, upward, downward):
        @pl.when(has_up)
        def _():
            upward(n).start()

        @pl.when(has_down)
        def _():
            downward(n).start()

    def back_rims(n, chunks, start):
        ncols = slice(n * CK, (n + 1) * CK)
        for side, dr in ((0, -1), (2, 1)):
            total = None if start else acc[side, :, ncols]
            for c in chunks:
                term = back_part(c, dr, ncols)
                total = term if total is None else total + term
            acc[side, :, ncols] = total
            if dr < 0:
                rim_out[0, :, ncols] = total[0:COLS].astype(BF16)
            else:
                rim_out[1, :, ncols] = total[PIX - COLS:].astype(BF16)

    def back_inner(n, chunks, start):
        ncols = slice(n * CK, (n + 1) * CK)
        total = None if start else acc[1, :, ncols]
        for c in chunks:
            term = back_part(c, 0, ncols)
            total = term if total is None else total + term
        acc[1, :, ncols] = total
        acc[1, 0:PIX - COLS, ncols] += acc[0, COLS:, ncols]
        acc[1, COLS:, ncols] += acc[2, 0:PIX - COLS, ncols]

    def add_rims(n):
        ncols = slice(n * CK, (n + 1) * CK)

        @pl.when(has_up)
        def _():
            local_wait(rim_in.at[0, :, lanes(n)], rim_recv.at[0, n])
            acc[1, 0:COLS, ncols] += rim_in[0, :, ncols].astype(F32)

        @pl.when(has_down)
        def _():
            local_wait(rim_in.at[1, :, lanes(n)], rim_recv.at[1, n])
            acc[1, PIX - COLS:, ncols] += rim_in[1, :, ncols].astype(F32)

        gs_img[:, ncols] = acc[1, :, ncols].astype(BF16)

    def send_g(n):
        ncols = slice(n * CK, (n + 1) * CK)
        g_out[:, ncols] = acc[1, :, ncols].astype(BF16)
        g_copy(n).start()

    @pl.when(jnp.logical_not(even))
    def _():
        take_g(0)
        for dr in (-1, 0, 1):
            acc[dr + 1] = back_part(0, dr, every)
        take_g(1)
        for dr in (-1, 0, 1):
            acc[dr + 1] += back_part(1, dr, every)
        take_g(2)
        for n in range(NCH):
            back_rims(n, (2,), False)
            send_rims(n, rim_direct_up, rim_direct_down)
            back_inner(n, (2,), False)
            send_g(n)
        for n in range(NCH):
            send_rims(n, rim_up, rim_down)
        for n in range(NCH):
            add_rims(n)

    @pl.when(even)
    def _():
        def finish(n):
            back_inner(n, chunks, True)
            add_rims(n)

            @pl.when(s > 0)
            def _():
                send_g(n)

        for c in range(NCH):
            take_g(c)
        chunks = range(NCH)
        back_rims(0, chunks, True)
        send_rims(0, rim_up, rim_down)
        back_rims(1, chunks, True)
        send_rims(1, rim_up, rim_down)
        finish(0)
        back_rims(2, chunks, True)
        send_rims(2, rim_up, rim_down)
        finish(1)
        finish(2)

    def gz_copy(r):
        return remote(
            band(gs_img, r), band(gs_all.at[x], image), gz_send.at[r], gz_recv.at[image], native(r), s
        )

    for r in range(4):
        @pl.when(native(r) != dp)
        def _():
            gz_copy(r).start()

        @pl.when(native(r) == dp)
        def _():
            pltpu.make_async_copy(band(gs_img, r), band(gs_all.at[x], image), gz_recv.at[image]).start()

    gather_start(gp_all, 0)

    @pl.when(s >= 6)
    def _():
        early_start()

    gather_forward(gp_all, 0)
    for img in range(4):
        local_wait(band(gs_all.at[x], img), gz_recv.at[img])
    gather_start(gs_all, 1)

    @pl.when(s >= 4)
    def _():
        gather_forward(ext_all, 2)

    whole_col = lax.broadcasted_iota(jnp.int32, (PIX, CH), 0) % COLS

    def spread(src):
        rows = pl.ds(pl.multiple_of(src * PIX, PIX), PIX)
        value = gp_all[src].astype(F32)
        gpv_all[0, rows, :] = jnp.where(whole_col == COLS - 1, 0.0, pltpu.roll(value, PIX - 1, 0)).astype(BF16)
        gpv_all[1, rows, :] = gp_all[src]
        gpv_all[2, rows, :] = jnp.where(whole_col == 0, 0.0, pltpu.roll(value, 1, 0)).astype(BF16)

    spread(x)
    spread(x_left)
    spread(x_right)
    gather_finish(gp_all, 0)
    spread(x_far)

    @pl.when(s >= 4)
    def _():
        early_finish()

    @pl.loop(0, 9)
    def _(u):
        unit = 9 * x + u
        o = unit // 4
        chans = pl.ds(pl.multiple_of((unit % 4) * UNIT, UNIT), UNIT)
        part_c[pl.ds(pl.multiple_of(u * UNIT, UNIT), UNIT), :] = nn(cols_t[o // 3, chans, :], gpv_all[o % 3])

    def slice_at(way, t):
        return (z + NZ - 1 - t) % NZ if way == 0 else (z + 1 + t) % NZ

    def own_rows(part, rows, way, t):
        at = pl.ds(pl.multiple_of(slice_at(way, t) * rows, 8), rows)
        return part[at, way * HALF:(way + 1) * HALF]

    def hop(ring, send, recv, way, t):
        return pltpu.make_async_remote_copy(
            src_ref=ring.at[way, t], dst_ref=ring.at[way, t + 1],
            send_sem=send.at[way, t], recv_sem=recv.at[way, t],
            device_id={"dp": z_next if way == 0 else z_prev, "section": s}, device_id_type=MESH,
        )

    conv_ring = (ring_c, rc_send, rc_recv)
    lat_ring = (ring_l, rl_send, rl_recv)
    for way in range(2):
        ring_c[way, 0] = own_rows(part_c, CROWS, way, 0).astype(BF16)
        hop(*conv_ring, way, 0).start()

    gather_forward(gs_all, 1)
    gather_finish(gs_all, 1)
    part_l[...] = nn(taps_t[...], gs_all[...].reshape(WIDE, CH))

    for way in range(2):
        ring_l[way, 0] = own_rows(part_l, KPAD, way, 0).astype(BF16)
        hop(*lat_ring, way, 0).start()

    for t in range(NZ - 1):
        for ring, part, rows, out in ((conv_ring, part_c, CROWS, conv_out), (lat_ring, part_l, KPAD, lat_out)):
            for way in range(2):
                buf = ring[0]
                local_wait(buf.at[way, t + 1], ring[2].at[way, t])
                total = buf[way, t + 1].astype(F32) + own_rows(part, rows, way, t + 1)
                if t < NZ - 2:
                    buf[way, t + 1] = total.astype(BF16)
                    hop(*ring, way, t + 1).start()
                else:
                    out[:, way * HALF:(way + 1) * HALF] = total

    for k in range(8):
        for xx in range(NX):
            @pl.when(elsewhere(k, xx))
            def _():
                tap_copy(k, xx).wait_send()

    @pl.when(even)
    def _():
        for xx in range(NX):
            tap_pass(xx).wait_send()

    for i in range(NZ):
        for way in z_ways(i):
            w_send_z(i, way).wait_send()
    for way in range(2):
        far_copy(way).wait_send()
        for part in range(2):
            near_copy(way, part).wait_send()
    for r in range(4):
        @pl.when(home(r) != dp)
        def _():
            lat_copy(r).wait_send()

    @pl.when(is_last)
    def _():
        for img in range(4):
            @pl.when(home(img) != dp)
            def _():
                oh_copy(img).wait_send()

    for c in range(NCH):
        @pl.when(s < SECTIONS - 1)
        def _():
            x_copy(c).wait_send()

        @pl.when(s > 0)
        def _():
            g_copy(c).wait_send()

        @pl.when(has_up)
        def _():
            rim_up(c).wait_send()

        @pl.when(has_down)
        def _():
            rim_down(c).wait_send()

        @pl.when(jnp.logical_and(has_up, even))
        def _():
            halo_up(c).wait_send()
            edge_up(c).wait_send()

        @pl.when(jnp.logical_and(has_down, even))
        def _():
            halo_down(c).wait_send()
            edge_down(c).wait_send()

        @pl.when(jnp.logical_and(has_up, jnp.logical_not(even)))
        def _():
            rim_direct_up(c).wait_send()

        @pl.when(jnp.logical_and(has_down, jnp.logical_not(even)))
        def _():
            rim_direct_down(c).wait_send()

    @pl.when(jnp.logical_and(has_up, jnp.logical_not(even)))
    def _():
        lat_up().wait_send()

    @pl.when(jnp.logical_and(has_down, jnp.logical_not(even)))
    def _():
        lat_down().wait_send()

    for kind, buf in enumerate((gp_all, gs_all, ext_all)):
        gather_sent(buf, kind)
    for r in range(4):
        @pl.when(native(r) != dp)
        def _():
            gz_copy(r).wait_send()

    for way in range(2):
        for t in range(NZ - 1):
            hop(*conv_ring, way, t).wait_send()
            hop(*lat_ring, way, t).wait_send()


def head_call(taps, lat, w, cls, counts, labels):
    dma = pltpu.SemaphoreType.DMA
    hbm = pl.BlockSpec(memory_space=pl.ANY)
    vmem = pl.BlockSpec(memory_space=pltpu.VMEM)
    smem = pl.BlockSpec(memory_space=pltpu.SMEM)
    return pl.pallas_call(
        head_kernel,
        out_shape=(
            jax.ShapeDtypeStruct((CROWS, CH), F32),
            jax.ShapeDtypeStruct((KPAD, CH), F32),
        ),
        in_specs=[vmem, vmem, hbm, vmem, smem, vmem],
        out_specs=(vmem, vmem),
        scratch_shapes=[
            pltpu.VMEM((8, 16, KW), BF16),
            pltpu.VMEM((XL, CH), BF16),
            pltpu.VMEM((9, CH, CH), BF16),
            pltpu.VMEM((PIX, CH), F32),
            pltpu.VMEM((3, PIX, CH), BF16),
            pltpu.VMEM((2, FARROWS, CH), BF16),
            pltpu.VMEM((2, PIX, CH), BF16),
            pltpu.VMEM((PIX, CH), BF16),
            pltpu.VMEM((PIX, CH), BF16),
            pltpu.VMEM((PIX + 2 * COLS, CH), BF16),
            pltpu.VMEM((PIX, CH), BF16),
            pltpu.VMEM((PIX, CH), BF16),
            pltpu.VMEM((PIX, CH), BF16),
            pltpu.VMEM((PIX, CH), F32),
            pltpu.VMEM((3, PIX, CH), F32),
            pltpu.VMEM((3, PIX, CH), BF16),
            pltpu.VMEM((2, COLS, CH), BF16),
            pltpu.VMEM((2, COLS, CH), BF16),
            pltpu.VMEM((2, 2 * COLS, CPAD), BF16),
            pltpu.VMEM((PIX, CPAD), BF16),
            pltpu.VMEM((2, COLS, CH), BF16),
            pltpu.VMEM((2, COLS, CH), BF16),
            pltpu.VMEM((PIX, CH), BF16),
            pltpu.VMEM((2, COLS, CH), BF16),
            pltpu.VMEM((NX, PIX + 2 * COLS, CH), BF16),
            pltpu.VMEM((NX, PIX, XL), BF16),
            pltpu.VMEM((PIX, CH), BF16),
            pltpu.VMEM((NX, PIX, CH), BF16),
            pltpu.VMEM((NX, PIX, CH), BF16),
            pltpu.VMEM((3, WIDE, CH), BF16),
            pltpu.VMEM((3, CH, WIDE), BF16),
            pltpu.VMEM((XL, WIDE), BF16),
            pltpu.VMEM((XC, CH), F32),
            pltpu.VMEM((XL, CH), F32),
            pltpu.VMEM((2, NZ, CROWS, HALF), BF16),
            pltpu.VMEM((2, NZ, KPAD, HALF), BF16),
            dma((1,)),
            dma((8, NX)),
            dma((NX, 2 * SECTIONS)),
            dma((NX,)),
            dma((NX,)),
            dma((2, NZ)),
            dma((NZ,)),
            dma((2,)),
            dma((2,)),
            dma((2, 2)),
            dma((2, 2)),
            dma((4,)),
            dma((4,)),
            dma((4,)),
            dma((4,)),
            dma((NCH,)),
            dma((NCH,)),
            dma((2, NCH)),
            dma((2, NCH)),
            dma((NCH,)),
            dma((NCH,)),
            dma((2, NCH)),
            dma((2, NCH)),
            dma((2,)),
            dma((2,)),
            dma((2, NCH)),
            dma((2, NCH)),
            dma((2, NCH)),
            dma((2, NCH)),
            pltpu.SemaphoreType.REGULAR,
            dma((4,)),
            dma((4,)),
            dma((3, 4)),
            dma((3, 4)),
            dma((2, NZ - 1)),
            dma((2, NZ - 1)),
            dma((2, NZ - 1)),
            dma((2, NZ - 1)),
        ],
        compiler_params=pltpu.CompilerParams(
            collective_id=0, has_side_effects=True, vmem_limit_bytes=62 << 20
        ),
    )(taps, lat, w, cls, counts, labels)


def on_device(tap_maps, lateral_weight, conv_weight, classifier, tile_counts, labels):
    levels, micros, here, width = tap_maps.shape
    taps = tap_maps.reshape(levels * micros, here, width)
    lat = jnp.pad(lateral_weight[0], ((0, KPAD - KROWS), (0, 0)))
    conv_grad, lateral_grad = head_call(
        taps, lat, conv_weight.reshape(9, CH, CH), classifier, tile_counts, labels
    )
    return (conv_grad[None], lateral_grad[None, :KROWS])


def solution(mesh):
    placed = (
        P(None, None, ("dp", "section"), None),
        P("section", "dp", None),
        P("section", None, None),
        P(),
        P("dp", None),
        P(None, "dp"),
    )
    return jax.shard_map(
        on_device,
        mesh=mesh,
        in_specs=placed,
        out_specs=(P("section", "dp", None), P("section", "dp", None)),
        check_vma=False,
    )
```

```python
import jax
import jax.numpy as jnp
from jax import lax
from jax.experimental import pallas as pl
from jax.experimental.pallas import tpu as pltpu
from jax.sharding import PartitionSpec as P

MESH = pl.DeviceIdType.MESH
F32 = jnp.float32
BF16 = jnp.bfloat16
NZ = 8
NX = 4
COLS = 64
ROWS = 4
PIX = ROWS * COLS
CH = 768
CK = 256
NCH = CH // CK
KROWS = 100
KPAD = 112
GROUPS = NX * NZ
KW = KPAD * GROUPS
SECTIONS = 8
WIDE = NX * PIX
CROWS = 9 * CH // GROUPS
XC, XL = CROWS * NZ, KPAD * NZ
UNIT = XC // 9
HALF = CH // 2
FARROWS = PIX // 2
CLASSES = 150
CPAD = 256


def nt(a, b):
    return lax.dot_general(a, b, (((1,), (1,)), ((), ())), preferred_element_type=F32)


def tn(a, b):
    return lax.dot_general(a, b, (((0,), (0,)), ((), ())), preferred_element_type=F32)


def nn(a, b):
    return jnp.dot(a, b, preferred_element_type=F32)


def head_kernel(
    tap_ref, lat_ref, w_hbm, cls_hbm, counts_ref, labels_ref, conv_out, lat_out,
    cls_ref, tap_pad, wl, w, gx, lat_send, lat_far, lat_near, lat_nat, lat_img,
    ext, xin, xout, gin, dsilu, acc, gpv, rim_out, rim_in, oh_own, oh,
    lat_halo, x_halo, g_out, g_rim,
    ext_all, taps_all, gs_img, gp_all, gs_all, gpv_all, cols_t, taps_t, part_c, part_l, ring_c, ring_l,
    local_sem, tap_send, tap_recv, pass_send, pass_recv, wz_send, w_recv,
    lf_send, lf_recv, ln_send, ln_recv, lz_send, lz_recv, oh_send, oh_recv,
    x_send, x_recv, halo_send, halo_recv, g_send, g_recv, rim_send, rim_recv,
    lh_send, lh_recv, xh_send, xh_recv, gr_send, gr_recv,
    early_sem, gz_send, gz_recv, a_send, a_recv, rc_send, rc_recv, rl_send, rl_recv,
):
    dp = lax.axis_index("dp")
    s = lax.axis_index("section")
    x, z = dp // NZ, dp % NZ
    odd = x % 2
    half = (z % 2 + odd) % 2
    image = z // 2
    has_up = jnp.logical_not(jnp.logical_and(half == 0, x == 0))
    has_down = jnp.logical_not(jnp.logical_and(half == 1, x == NX - 1))
    pair = dp + 1 - 2 * (z % 2)
    up = jnp.where(half == 1, pair, dp - NZ)
    down = jnp.where(half == 0, pair, dp + NZ)
    src_half = z // 4
    is_first, is_last = s == 0, s == SECTIONS - 1
    even = s % 2 == 0
    sibling = s + 1 - 2 * (s % 2)
    z_next, z_prev = x * NZ + (z + 1) % NZ, x * NZ + (z + NZ - 1) % NZ
    x_left, x_right, x_far = (x + NX - 1) % NX, (x + 1) % NX, (x + 2) % NX
    left, right = x_left * NZ + z, x_right * NZ + z

    def home(img):
        return x * NZ + 2 * img + (src_half + odd) % 2

    def remote(src, dst, send, recv, d, sec):
        return pltpu.make_async_remote_copy(
            src_ref=src, dst_ref=dst, send_sem=send, recv_sem=recv,
            device_id={"dp": d, "section": sec}, device_id_type=MESH,
        )

    def local_wait(ref, sem):
        pltpu.make_async_copy(ref, ref, sem).wait()

    w_copy = pltpu.make_async_copy(w_hbm, w, local_sem.at[0])
    w_copy.start()
    cls_copy = pltpu.make_async_copy(cls_hbm, cls_ref, local_sem.at[1])

    @pl.when(is_last)
    def _():
        cls_copy.start()

    barrier = pltpu.get_barrier_semaphore()

    def greet(d, sec):
        pl.semaphore_signal(barrier, inc=1, device_id={"dp": d, "section": sec}, device_id_type=MESH)

    @pl.when(even)
    def _():
        for xx in range(NX):
            for sec in range(SECTIONS):
                @pl.when(jnp.logical_or(xx != x, sec != s))
                def _():
                    greet(xx * NZ + z, sec)

    for d in (left, right, z_next, z_prev):
        greet(d, s)

    @pl.when(has_up)
    def _():
        greet(up, s)
        greet(up, sibling)

    @pl.when(has_down)
    def _():
        greet(down, s)
        greet(down, sibling)

    @pl.when(s > 0)
    def _():
        greet(dp, s - 1)

    @pl.when(s < SECTIONS - 1)
    def _():
        greet(dp, s + 1)

    def native(r):
        return x * NZ + half * 4 + r

    for r in range(4):
        for d in (native(r), home(r)):
            @pl.when(d != dp)
            def _():
                greet(d, s)

    flat = tap_ref[...].reshape(8 * 16, GROUPS * KROWS).astype(F32)
    lane = lax.broadcasted_iota(jnp.int32, (8 * 16, 128), 1)
    for tile in range(KW // 128):
        first = tile * 128
        total = jnp.zeros((8 * 16, 128), F32)
        for g in range(first // KPAD, min((first + 127) // KPAD + 1, GROUPS)):
            lo = first - (KPAD - KROWS) * g
            start = min(max(lo // 128 * 128, 0), GROUPS * KROWS - 256)
            moved = pltpu.roll(flat[:, start:start + 256], (start - lo) % 256, 1)[:, :128]
            inside = jnp.logical_and(lane + first >= KPAD * g, lane + first < KPAD * g + KROWS)
            total = jnp.where(inside, moved, total)
        tap_pad[:, :, first:first + 128] = total.astype(BF16).reshape(8, 16, 128)

    def w_rows(zz):
        return wl.at[pl.ds(pl.multiple_of(zz * KPAD, 16), KPAD), :]

    wl[pl.ds(pl.multiple_of(z * KPAD, 16), KPAD), :] = jnp.concatenate(
        [lat_ref[...].astype(F32), jnp.zeros((KPAD - KROWS, CH), F32)], 0
    ).astype(BF16)

    need = jnp.where(even, 4 + 15, 4 + 16)
    for flag in (has_up, has_down, has_up, has_down, s > 0, s < SECTIONS - 1):
        need += flag.astype(jnp.int32)
    for r in range(4):
        need += (native(r) != dp).astype(jnp.int32) + (home(r) != dp).astype(jnp.int32)
    pl.semaphore_wait(barrier, need)

    def tap_cell(xx, j):
        return taps_all.at[xx, pl.ds(pl.multiple_of(j * 16, 16), 16), :]

    def tap_src(k, xx):
        return tap_pad.at[k, :, pl.ds(xx * XL, XL)]

    def tap_copy(k, xx):
        slot = (k % 2) * SECTIONS + s
        return remote(
            tap_src(k, xx), tap_cell(x, slot), tap_send.at[k, xx], tap_recv.at[x, slot], xx * NZ + z, k // 2 * 2
        )

    def tap_pass(xx):
        return remote(taps_all.at[xx], taps_all.at[xx], pass_send.at[xx], pass_recv.at[xx], dp, s + 1)

    def elsewhere(k, xx):
        return jnp.logical_or(xx != x, k // 2 * 2 != s)

    for k in range(8):
        for xx in range(NX):
            @pl.when(elsewhere(k, xx))
            def _():
                tap_copy(k, xx).start()

            @pl.when(jnp.logical_not(elsewhere(k, xx)))
            def _():
                slot = (k % 2) * SECTIONS + s
                pltpu.make_async_copy(tap_src(k, xx), tap_cell(x, slot), tap_recv.at[x, slot]).start()

    order = (0, -1, 1, -2, 2, -3, 3, -4)

    def ring_z(i):
        return (z + NZ + order[i]) % NZ

    def w_send_z(i, way):
        block = w_rows(ring_z(i))
        return remote(block, block, wz_send.at[way, i], w_recv.at[ring_z(i)], z_next if way == 0 else z_prev, s)

    def z_ways(i):
        ways = []
        if order[i] <= 0 and order[i] > -4:
            ways.append(0)
        if order[i] >= 0 and order[i] < 3:
            ways.append(1)
        return ways

    for i in range(NZ):
        if i > 0:
            local_wait(w_rows(ring_z(i)), w_recv.at[ring_z(i)])
        for way in z_ways(i):
            w_send_z(i, way).start()

    def oh_rows(r):
        return oh.at[pl.ds(pl.multiple_of(r * COLS, COLS), COLS), :]

    def oh_src(img):
        return oh_own.at[img // 2, pl.ds((img % 2) * COLS, COLS), :]

    def oh_copy(img):
        return remote(oh_src(img), oh_rows(z % 4), oh_send.at[img], oh_recv.at[z % 4], home(img), s)

    @pl.when(is_last)
    def _():
        sub = lax.broadcasted_iota(jnp.int32, (CPAD, 2 * COLS), 0)
        tile_of = lax.broadcasted_iota(jnp.int32, (CPAD, 2 * COLS), 1) // COLS
        for micro in range(2):
            count = counts_ref[0, micro]
            share = 1.0 / (count.astype(F32) * (COLS * GROUPS * 2))
            weight = jnp.where(tile_of < count, share, 0.0)
            hot = jnp.where(sub == labels_ref[micro:micro + 1, :], 1.0, 0.0)
            oh_own[micro] = jnp.where(sub == CPAD - 1, weight, hot).T.astype(BF16)
        for img in range(4):
            @pl.when(home(img) != dp)
            def _():
                oh_copy(img).start()

            @pl.when(home(img) == dp)
            def _():
                pltpu.make_async_copy(oh_src(img), oh_rows(z % 4), oh_recv.at[z % 4]).start()

    @pl.when(jnp.logical_not(has_up))
    def _():
        ext[0:COLS, :] = jnp.zeros((COLS, CH), BF16)

    @pl.when(jnp.logical_not(has_down))
    def _():
        ext[COLS + PIX:, :] = jnp.zeros((COLS, CH), BF16)

    @pl.when(even)
    def _():
        for xx in range(NX):
            for j in range(2 * SECTIONS):
                local_wait(tap_cell(xx, j), tap_recv.at[xx, j])
            tap_pass(xx).start()

    @pl.when(jnp.logical_not(even))
    def _():
        for xx in range(NX):
            local_wait(taps_all.at[xx], pass_recv.at[xx])

    first_rows, last_rows = pl.ds(0, FARROWS), pl.ds(FARROWS, FARROWS)
    half_rows = (first_rows, last_rows)

    def far_copy(way):
        return remote(
            lat_send.at[2, half_rows[way]], lat_far.at[way], lf_send.at[way], lf_recv.at[way],
            right if way == 0 else left, s,
        )

    def near_copy(way, part):
        return remote(
            lat_send.at[way, half_rows[part]], lat_near.at[way, half_rows[part]],
            ln_send.at[way, part], ln_recv.at[way, part], right if way == 0 else left, s,
        )

    lat_send[2] = nn(taps_all[x_far], wl[...]).astype(BF16)
    for way in range(2):
        far_copy(way).start()
    for way in range(2):
        acc[way] = nn(taps_all[x_right if way == 0 else x_left], wl[...])
        rows = half_rows[1 - way]
        lat_send[way, rows] = acc[way, rows].astype(BF16)
        near_copy(way, 1 - way).start()
    acc[2] = nn(taps_all[x], wl[...])
    for way in range(2):
        rows = half_rows[way]
        local_wait(lat_far.at[way], lf_recv.at[way])
        lat_send[way, rows] = (acc[way, rows] + lat_far[way].astype(F32)).astype(BF16)
        near_copy(way, way).start()
    for part in range(2):
        rows = half_rows[part]
        for way in (1 - part, part):
            local_wait(lat_near.at[way, rows], ln_recv.at[way, part])
        lat_nat[rows] = (
            acc[2, rows] + lat_near[0, rows].astype(F32) + lat_near[1, rows].astype(F32)
        ).astype(BF16)

    def band(ref, j):
        return ref.at[pl.ds(pl.multiple_of(j * COLS, COLS), COLS), :]

    def lat_copy(img):
        return remote(band(lat_nat, img), band(lat_img, z % 4), lz_send.at[img], lz_recv.at[z % 4], home(img), s)

    for img in range(4):
        @pl.when(home(img) != dp)
        def _():
            lat_copy(img).start()

        @pl.when(home(img) == dp)
        def _():
            pltpu.make_async_copy(band(lat_nat, img), band(lat_img, z % 4), lz_recv.at[z % 4]).start()

    for r in range(4):
        local_wait(band(lat_img, r), lz_recv.at[r])

    def lat_up():
        return remote(band(lat_img, 0), lat_halo.at[1], lh_send.at[0], lh_recv.at[1], up, s)

    def lat_down():
        return remote(band(lat_img, ROWS - 1), lat_halo.at[0], lh_send.at[1], lh_recv.at[0], down, s)

    @pl.when(jnp.logical_and(has_up, jnp.logical_not(even)))
    def _():
        lat_up().start()

    @pl.when(jnp.logical_and(has_down, jnp.logical_not(even)))
    def _():
        lat_down().start()

    w_copy.wait()

    def lanes(c):
        return pl.ds(c * CK, CK)

    def x_copy(c):
        return pltpu.make_async_remote_copy(
            src_ref=xout.at[:, lanes(c)], dst_ref=xin.at[:, lanes(c)],
            send_sem=x_send.at[c], recv_sem=x_recv.at[c],
            device_id={"dp": dp, "section": s + 1}, device_id_type=MESH,
        )

    def halo_up(c):
        return pltpu.make_async_remote_copy(
            src_ref=ext.at[pl.ds(COLS, COLS), lanes(c)], dst_ref=ext.at[pl.ds(COLS + PIX, COLS), lanes(c)],
            send_sem=halo_send.at[0, c], recv_sem=halo_recv.at[1, c],
            device_id={"dp": up, "section": s}, device_id_type=MESH,
        )

    def halo_down(c):
        return pltpu.make_async_remote_copy(
            src_ref=ext.at[pl.ds(PIX, COLS), lanes(c)], dst_ref=ext.at[pl.ds(0, COLS), lanes(c)],
            send_sem=halo_send.at[1, c], recv_sem=halo_recv.at[0, c],
            device_id={"dp": down, "section": s}, device_id_type=MESH,
        )

    def edge_up(c):
        return remote(
            xout.at[pl.ds(0, COLS), lanes(c)], x_halo.at[1, :, lanes(c)],
            xh_send.at[0, c], xh_recv.at[1, c], up, s + 1,
        )

    def edge_down(c):
        return remote(
            xout.at[pl.ds(PIX - COLS, COLS), lanes(c)], x_halo.at[0, :, lanes(c)],
            xh_send.at[1, c], xh_recv.at[0, c], down, s + 1,
        )

    def take_edges(c):
        cols = slice(c * CK, (c + 1) * CK)
        for side, flag, rows in ((0, has_up, slice(0, COLS)), (1, has_down, slice(COLS + PIX, 2 * COLS + PIX))):
            @pl.when(flag)
            def _():
                local_wait(x_halo.at[side, :, lanes(c)], xh_recv.at[side, c])
                ext[rows, cols] = (
                    x_halo[side, :, cols].astype(F32) + lat_halo[side, :, cols].astype(F32)
                ).astype(BF16)

    def take_x(c):
        cols = slice(c * CK, (c + 1) * CK)

        @pl.when(is_first)
        def _():
            ext[COLS:COLS + PIX, cols] = lat_img[:, cols]

        @pl.when(s > 0)
        def _():
            local_wait(xin.at[:, lanes(c)], x_recv.at[c])
            ext[COLS:COLS + PIX, cols] = (xin[:, cols].astype(F32) + lat_img[:, cols].astype(F32)).astype(BF16)

        @pl.when(jnp.logical_and(has_up, even))
        def _():
            halo_up(c).start()

        @pl.when(jnp.logical_and(has_down, even))
        def _():
            halo_down(c).start()

    def wait_halo(c):
        @pl.when(has_up)
        def _():
            local_wait(ext.at[pl.ds(0, COLS), lanes(c)], halo_recv.at[0, c])

        @pl.when(has_down)
        def _():
            local_wait(ext.at[pl.ds(COLS + PIX, COLS), lanes(c)], halo_recv.at[1, c])

    def conv_part(c, dr, dc, ncols):
        rows = (1 + dr) * COLS
        return nn(
            ext[rows:rows + PIX, c * CK:(c + 1) * CK],
            w[(dr + 1) * 3 + dc + 1, c * CK:(c + 1) * CK, ncols],
        )

    every = slice(0, CH)

    def conv_inner(c, start):
        for dc in (-1, 0, 1):
            term = conv_part(c, 0, dc, every)
            if start:
                acc[dc + 1] = term
            else:
                acc[dc + 1] += term

    def conv_outer(c):
        for dc in (-1, 0, 1):
            acc[dc + 1] += conv_part(c, -1, dc, every) + conv_part(c, 1, dc, every)

    col = lax.broadcasted_iota(jnp.int32, (PIX, CK), 0) % COLS

    def before(v):
        return jnp.where(col == 0, 0.0, pltpu.roll(v, 1, 0))

    def after(v):
        return jnp.where(col == COLS - 1, 0.0, pltpu.roll(v, PIX - 1, 0))

    def conv_finish(n, chunks, direct):
        ncols = slice(n * CK, (n + 1) * CK)
        parts = []
        for dc in (-1, 0, 1):
            part = acc[dc + 1, :, ncols]
            for c in chunks:
                part += conv_part(c, -1, dc, ncols) + conv_part(c, 1, dc, ncols)
            parts.append(part)
        pre = before(parts[0]) + parts[1] + after(parts[2])
        sig = 1.0 / (1.0 + jnp.exp(-pre))
        xout[:, ncols] = (pre * sig).astype(BF16)

        @pl.when(s < SECTIONS - 1)
        def _():
            x_copy(n).start()

        if direct:
            @pl.when(has_up)
            def _():
                edge_up(n).start()

            @pl.when(has_down)
            def _():
                edge_down(n).start()

        dsilu[:, ncols] = sig * (1.0 + pre * (1.0 - sig))

    @pl.when(even)
    def _():
        take_x(0)
        conv_inner(0, True)
        take_x(1)
        conv_inner(1, False)
        wait_halo(0)
        conv_outer(0)
        take_x(2)
        conv_inner(2, False)
        wait_halo(1)
        conv_outer(1)
        wait_halo(2)
        for n in range(NCH):
            conv_finish(n, (2,), True)

    @pl.when(jnp.logical_not(even))
    def _():
        for c in range(NCH):
            take_x(c)
        for c in range(NCH):
            conv_inner(c, c == 0)

        @pl.when(has_up)
        def _():
            local_wait(lat_halo.at[0], lh_recv.at[0])

        @pl.when(has_down)
        def _():
            local_wait(lat_halo.at[1], lh_recv.at[1])

        for c in range(NCH):
            take_edges(c)
        for n in range(NCH):
            conv_finish(n, range(NCH), False)

    def gather_copy(buf, kind, way):
        return remote(
            buf.at[x], buf.at[x], a_send.at[kind, way], a_recv.at[kind, way], right if way == 0 else left, s
        )

    def gather_far(buf, kind, way):
        rows = buf.shape[1] // 2
        block = buf.at[x_left if way == 0 else x_right, pl.ds(way * rows, rows), :]
        return remote(
            block, block, a_send.at[kind, 2 + way], a_recv.at[kind, 2 + way], right if way == 0 else left, s
        )

    def gather_start(buf, kind):
        for way in range(2):
            gather_copy(buf, kind, way).start()

    def gather_forward(buf, kind):
        for way in range(2):
            local_wait(buf.at[x_left if way == 0 else x_right], a_recv.at[kind, way])
            gather_far(buf, kind, way).start()

    def gather_finish(buf, kind):
        rows = buf.shape[1] // 2
        for way in range(2):
            local_wait(buf.at[x_far, pl.ds(way * rows, rows), :], a_recv.at[kind, 2 + way])

    def gather_sent(buf, kind):
        for way in range(2):
            gather_copy(buf, kind, way).wait_send()
            gather_far(buf, kind, way).wait_send()

    def early_start():
        ext_all[x] = ext[...]
        gather_start(ext_all, 2)

    def early_finish():
        gather_finish(ext_all, 2)

        @pl.loop(0, NX)
        def _(src):
            lanes_of = pl.ds(pl.multiple_of(src * PIX, PIX), PIX)
            for dr in range(3):
                cols_t[dr, :, lanes_of] = ext_all[src, dr * COLS:dr * COLS + PIX, :].T
            taps_t[:, lanes_of] = taps_all[src].T

    @pl.when(jnp.logical_and(s < 6, s % 2 == 1))
    def _():
        pl.semaphore_signal(early_sem, inc=1, device_id={"dp": dp, "section": s - 1}, device_id_type=MESH)

    @pl.when(jnp.logical_and(s < 6, s % 2 == 0))
    def _():
        pl.semaphore_wait(early_sem, 1)

    @pl.when(s < 6)
    def _():
        early_start()

    @pl.when(s < 4)
    def _():
        gather_forward(ext_all, 2)
        early_finish()

    @pl.when(is_last)
    def _():
        for r in range(4):
            local_wait(oh_rows(r), oh_recv.at[r])
        cls_copy.wait()
        logits = nn(xout[...], cls_ref[...])
        spot = lax.broadcasted_iota(jnp.int32, (PIX, CPAD), 1)
        expo = jnp.exp(logits)
        probs = expo / jnp.sum(expo, axis=-1, keepdims=True)
        marks = oh[...].astype(F32)
        weight = jnp.sum(jnp.where(spot == CPAD - 1, marks, 0.0), axis=-1, keepdims=True)
        grad_logits = ((probs - marks[:, :CLASSES]) * weight).astype(BF16)
        gx[...] = nt(grad_logits, cls_ref[...])

    def g_copy(c):
        return pltpu.make_async_remote_copy(
            src_ref=g_out.at[:, lanes(c)], dst_ref=gin.at[:, lanes(c)],
            send_sem=g_send.at[c], recv_sem=g_recv.at[c],
            device_id={"dp": dp, "section": s - 1}, device_id_type=MESH,
        )

    def rim_up(c):
        return pltpu.make_async_remote_copy(
            src_ref=rim_out.at[0, :, lanes(c)], dst_ref=rim_in.at[1, :, lanes(c)],
            send_sem=rim_send.at[0, c], recv_sem=rim_recv.at[1, c],
            device_id={"dp": up, "section": s}, device_id_type=MESH,
        )

    def rim_down(c):
        return pltpu.make_async_remote_copy(
            src_ref=rim_out.at[1, :, lanes(c)], dst_ref=rim_in.at[0, :, lanes(c)],
            send_sem=rim_send.at[1, c], recv_sem=rim_recv.at[0, c],
            device_id={"dp": down, "section": s}, device_id_type=MESH,
        )

    def take_g(c):
        cols = slice(c * CK, (c + 1) * CK)

        @pl.when(s < SECTIONS - 1)
        def _():
            local_wait(gin.at[:, lanes(c)], g_recv.at[c])
            gx[:, cols] = gin[:, cols].astype(F32)

        for side, flag, rows in ((0, has_up, slice(0, COLS)), (1, has_down, slice(PIX - COLS, PIX))):
            @pl.when(jnp.logical_and(flag, even))
            def _():
                local_wait(g_rim.at[side, :, lanes(c)], gr_recv.at[side, c])
                gx[rows, cols] += g_rim[side, :, cols].astype(F32)

        grad_pre = (gx[:, cols] * dsilu[:, cols]).astype(BF16).astype(F32)
        gpv[0, :, cols] = after(grad_pre).astype(BF16)
        gpv[1, :, cols] = grad_pre.astype(BF16)
        gp_all[x, :, cols] = grad_pre.astype(BF16)
        gpv[2, :, cols] = before(grad_pre).astype(BF16)

    def back_part(c, dr, krows):
        total = None
        for dc in (-1, 0, 1):
            term = nt(
                gpv[dc + 1, :, c * CK:(c + 1) * CK],
                w[(dr + 1) * 3 + dc + 1, krows, c * CK:(c + 1) * CK],
            )
            total = term if total is None else total + term
        return total

    def rim_direct_up(c):
        return remote(
            rim_out.at[0, :, lanes(c)], g_rim.at[1, :, lanes(c)], gr_send.at[0, c], gr_recv.at[1, c], up, s - 1
        )

    def rim_direct_down(c):
        return remote(
            rim_out.at[1, :, lanes(c)], g_rim.at[0, :, lanes(c)], gr_send.at[1, c], gr_recv.at[0, c], down, s - 1
        )

    def send_rims(n, upward, downward):
        @pl.when(has_up)
        def _():
            upward(n).start()

        @pl.when(has_down)
        def _():
            downward(n).start()

    def back_rims(n, chunks, start):
        ncols = slice(n * CK, (n + 1) * CK)
        for side, dr in ((0, -1), (2, 1)):
            total = None if start else acc[side, :, ncols]
            for c in chunks:
                term = back_part(c, dr, ncols)
                total = term if total is None else total + term
            acc[side, :, ncols] = total
            if dr < 0:
                rim_out[0, :, ncols] = total[0:COLS].astype(BF16)
            else:
                rim_out[1, :, ncols] = total[PIX - COLS:].astype(BF16)

    def back_inner(n, chunks, start):
        ncols = slice(n * CK, (n + 1) * CK)
        total = None if start else acc[1, :, ncols]
        for c in chunks:
            term = back_part(c, 0, ncols)
            total = term if total is None else total + term
        acc[1, :, ncols] = total
        acc[1, 0:PIX - COLS, ncols] += acc[0, COLS:, ncols]
        acc[1, COLS:, ncols] += acc[2, 0:PIX - COLS, ncols]

    def add_rims(n):
        ncols = slice(n * CK, (n + 1) * CK)

        @pl.when(has_up)
        def _():
            local_wait(rim_in.at[0, :, lanes(n)], rim_recv.at[0, n])
            acc[1, 0:COLS, ncols] += rim_in[0, :, ncols].astype(F32)

        @pl.when(has_down)
        def _():
            local_wait(rim_in.at[1, :, lanes(n)], rim_recv.at[1, n])
            acc[1, PIX - COLS:, ncols] += rim_in[1, :, ncols].astype(F32)

        gs_img[:, ncols] = acc[1, :, ncols].astype(BF16)

    def send_g(n):
        ncols = slice(n * CK, (n + 1) * CK)
        g_out[:, ncols] = acc[1, :, ncols].astype(BF16)
        g_copy(n).start()

    @pl.when(jnp.logical_not(even))
    def _():
        take_g(0)
        for dr in (-1, 0, 1):
            acc[dr + 1] = back_part(0, dr, every)
        take_g(1)
        for dr in (-1, 0, 1):
            acc[dr + 1] += back_part(1, dr, every)
        take_g(2)
        for n in range(NCH):
            back_rims(n, (2,), False)
            send_rims(n, rim_direct_up, rim_direct_down)
            back_inner(n, (2,), False)
            send_g(n)
        for n in range(NCH):
            send_rims(n, rim_up, rim_down)
        gather_start(gp_all, 0)
        for n in range(NCH):
            add_rims(n)

    @pl.when(even)
    def _():
        def finish(n):
            back_inner(n, chunks, True)
            add_rims(n)

            @pl.when(s > 0)
            def _():
                send_g(n)

        for c in range(NCH):
            take_g(c)

        @pl.when(is_first)
        def _():
            gather_start(gp_all, 0)

        chunks = range(NCH)
        back_rims(0, chunks, True)
        send_rims(0, rim_up, rim_down)
        back_rims(1, chunks, True)
        send_rims(1, rim_up, rim_down)
        finish(0)
        back_rims(2, chunks, True)
        send_rims(2, rim_up, rim_down)
        finish(1)
        finish(2)

    def gz_copy(r):
        return remote(
            band(gs_img, r), band(gs_all.at[x], image), gz_send.at[r], gz_recv.at[image], native(r), s
        )

    for r in range(4):
        @pl.when(native(r) != dp)
        def _():
            gz_copy(r).start()

        @pl.when(native(r) == dp)
        def _():
            pltpu.make_async_copy(band(gs_img, r), band(gs_all.at[x], image), gz_recv.at[image]).start()

    @pl.when(jnp.logical_and(even, s > 0))
    def _():
        gather_start(gp_all, 0)

    @pl.when(s >= 6)
    def _():
        early_start()

    gather_forward(gp_all, 0)

    @pl.when(s >= 4)
    def _():
        gather_forward(ext_all, 2)

    whole_col = lax.broadcasted_iota(jnp.int32, (PIX, CH), 0) % COLS

    def spread(src):
        rows = pl.ds(pl.multiple_of(src * PIX, PIX), PIX)
        value = gp_all[src].astype(F32)
        gpv_all[0, rows, :] = jnp.where(whole_col == COLS - 1, 0.0, pltpu.roll(value, PIX - 1, 0)).astype(BF16)
        gpv_all[1, rows, :] = gp_all[src]
        gpv_all[2, rows, :] = jnp.where(whole_col == 0, 0.0, pltpu.roll(value, 1, 0)).astype(BF16)

    spread(x)
    spread(x_left)
    spread(x_right)
    gather_finish(gp_all, 0)
    for img in range(4):
        local_wait(band(gs_all.at[x], img), gz_recv.at[img])
    gather_start(gs_all, 1)
    spread(x_far)

    @pl.when(s >= 4)
    def _():
        early_finish()

    def conv_unit(u):
        unit = 9 * x + u
        o = unit // 4
        chans = pl.ds(pl.multiple_of((unit % 4) * UNIT, UNIT), UNIT)
        part_c[pl.ds(pl.multiple_of(u * UNIT, UNIT), UNIT), :] = nn(cols_t[o // 3, chans, :], gpv_all[o % 3])

    def conv_slice(zz):
        @pl.loop(0, 2)
        def _(k):
            conv_unit(zz + k)

    def slice_at(way, t):
        return (z + NZ - 1 - t) % NZ if way == 0 else (z + 1 + t) % NZ

    def own_rows(part, rows, way, t):
        at = pl.ds(pl.multiple_of(slice_at(way, t) * rows, 8), rows)
        return part[at, way * HALF:(way + 1) * HALF]

    def hop(ring, send, recv, way, t):
        return pltpu.make_async_remote_copy(
            src_ref=ring.at[way, t], dst_ref=ring.at[way, t + 1],
            send_sem=send.at[way, t], recv_sem=recv.at[way, t],
            device_id={"dp": z_next if way == 0 else z_prev, "section": s}, device_id_type=MESH,
        )

    conv_ring = (ring_c, rc_send, rc_recv)
    lat_ring = (ring_l, rl_send, rl_recv)
    def ring_start(ring, part, rows):
        for way in range(2):
            ring[0][way, 0] = own_rows(part, rows, way, 0).astype(BF16)
            hop(*ring, way, 0).start()

    def ring_step(ring, part, rows, out, t):
        buf = ring[0]
        for way in range(2):
            local_wait(buf.at[way, t + 1], ring[2].at[way, t])
            total = buf[way, t + 1].astype(F32) + own_rows(part, rows, way, t + 1)
            if t < NZ - 2:
                buf[way, t + 1] = total.astype(BF16)
                hop(*ring, way, t + 1).start()
            else:
                out[:, way * HALF:(way + 1) * HALF] = total

    def conv_step(t):
        ring_step(conv_ring, part_c, CROWS, conv_out, t)

    def lat_step(t):
        ring_step(lat_ring, part_l, KPAD, lat_out, t)

    @pl.loop(0, 2)
    def _(k):
        conv_slice((z + 1 + k * (NZ - 2)) % NZ)

    ring_start(conv_ring, part_c, CROWS)

    @pl.loop(0, 2)
    def _(k):
        conv_slice((z + 2 + k * (NZ - 4)) % NZ)

    gather_forward(gs_all, 1)
    conv_step(0)

    @pl.loop(0, 2)
    def _(k):
        conv_slice((z + 3 + k * (NZ - 6)) % NZ)

    gather_finish(gs_all, 1)
    part_l[...] = nn(taps_t[...], gs_all[...].reshape(WIDE, CH))
    ring_start(lat_ring, part_l, KPAD)
    conv_step(1)

    @pl.loop(0, 2)
    def _(k):
        conv_slice((z + 4 * k) % NZ)

    lat_step(0)
    for t in range(2, NZ - 1):
        conv_step(t)
        lat_step(t - 1)
    lat_step(NZ - 2)

    for k in range(8):
        for xx in range(NX):
            @pl.when(elsewhere(k, xx))
            def _():
                tap_copy(k, xx).wait_send()

    @pl.when(even)
    def _():
        for xx in range(NX):
            tap_pass(xx).wait_send()

    for i in range(NZ):
        for way in z_ways(i):
            w_send_z(i, way).wait_send()
    for way in range(2):
        far_copy(way).wait_send()
        for part in range(2):
            near_copy(way, part).wait_send()
    for r in range(4):
        @pl.when(home(r) != dp)
        def _():
            lat_copy(r).wait_send()

    @pl.when(is_last)
    def _():
        for img in range(4):
            @pl.when(home(img) != dp)
            def _():
                oh_copy(img).wait_send()

    for c in range(NCH):
        @pl.when(s < SECTIONS - 1)
        def _():
            x_copy(c).wait_send()

        @pl.when(s > 0)
        def _():
            g_copy(c).wait_send()

        @pl.when(has_up)
        def _():
            rim_up(c).wait_send()

        @pl.when(has_down)
        def _():
            rim_down(c).wait_send()

        @pl.when(jnp.logical_and(has_up, even))
        def _():
            halo_up(c).wait_send()
            edge_up(c).wait_send()

        @pl.when(jnp.logical_and(has_down, even))
        def _():
            halo_down(c).wait_send()
            edge_down(c).wait_send()

        @pl.when(jnp.logical_and(has_up, jnp.logical_not(even)))
        def _():
            rim_direct_up(c).wait_send()

        @pl.when(jnp.logical_and(has_down, jnp.logical_not(even)))
        def _():
            rim_direct_down(c).wait_send()

    @pl.when(jnp.logical_and(has_up, jnp.logical_not(even)))
    def _():
        lat_up().wait_send()

    @pl.when(jnp.logical_and(has_down, jnp.logical_not(even)))
    def _():
        lat_down().wait_send()

    for kind, buf in enumerate((gp_all, gs_all, ext_all)):
        gather_sent(buf, kind)
    for r in range(4):
        @pl.when(native(r) != dp)
        def _():
            gz_copy(r).wait_send()

    for way in range(2):
        for t in range(NZ - 1):
            hop(*conv_ring, way, t).wait_send()
            hop(*lat_ring, way, t).wait_send()


def head_call(taps, lat, w, cls, counts, labels):
    dma = pltpu.SemaphoreType.DMA
    hbm = pl.BlockSpec(memory_space=pl.ANY)
    vmem = pl.BlockSpec(memory_space=pltpu.VMEM)
    smem = pl.BlockSpec(memory_space=pltpu.SMEM)
    return pl.pallas_call(
        head_kernel,
        out_shape=(
            jax.ShapeDtypeStruct((CROWS, CH), F32),
            jax.ShapeDtypeStruct((KPAD, CH), F32),
        ),
        in_specs=[vmem, vmem, hbm, hbm, smem, vmem],
        out_specs=(vmem, vmem),
        scratch_shapes=[
            pltpu.VMEM((CH, CLASSES), BF16),
            pltpu.VMEM((8, 16, KW), BF16),
            pltpu.VMEM((XL, CH), BF16),
            pltpu.VMEM((9, CH, CH), BF16),
            pltpu.VMEM((PIX, CH), F32),
            pltpu.VMEM((3, PIX, CH), BF16),
            pltpu.VMEM((2, FARROWS, CH), BF16),
            pltpu.VMEM((2, PIX, CH), BF16),
            pltpu.VMEM((PIX, CH), BF16),
            pltpu.VMEM((PIX, CH), BF16),
            pltpu.VMEM((PIX + 2 * COLS, CH), BF16),
            pltpu.VMEM((PIX, CH), BF16),
            pltpu.VMEM((PIX, CH), BF16),
            pltpu.VMEM((PIX, CH), BF16),
            pltpu.VMEM((PIX, CH), F32),
            pltpu.VMEM((3, PIX, CH), F32),
            pltpu.VMEM((3, PIX, CH), BF16),
            pltpu.VMEM((2, COLS, CH), BF16),
            pltpu.VMEM((2, COLS, CH), BF16),
            pltpu.VMEM((2, 2 * COLS, CPAD), BF16),
            pltpu.VMEM((PIX, CPAD), BF16),
            pltpu.VMEM((2, COLS, CH), BF16),
            pltpu.VMEM((2, COLS, CH), BF16),
            pltpu.VMEM((PIX, CH), BF16),
            pltpu.VMEM((2, COLS, CH), BF16),
            pltpu.VMEM((NX, PIX + 2 * COLS, CH), BF16),
            pltpu.VMEM((NX, PIX, XL), BF16),
            pltpu.VMEM((PIX, CH), BF16),
            pltpu.VMEM((NX, PIX, CH), BF16),
            pltpu.VMEM((NX, PIX, CH), BF16),
            pltpu.VMEM((3, WIDE, CH), BF16),
            pltpu.VMEM((3, CH, WIDE), BF16),
            pltpu.VMEM((XL, WIDE), BF16),
            pltpu.VMEM((XC, CH), F32),
            pltpu.VMEM((XL, CH), F32),
            pltpu.VMEM((2, NZ, CROWS, HALF), BF16),
            pltpu.VMEM((2, NZ, KPAD, HALF), BF16),
            dma((2,)),
            dma((8, NX)),
            dma((NX, 2 * SECTIONS)),
            dma((NX,)),
            dma((NX,)),
            dma((2, NZ)),
            dma((NZ,)),
            dma((2,)),
            dma((2,)),
            dma((2, 2)),
            dma((2, 2)),
            dma((4,)),
            dma((4,)),
            dma((4,)),
            dma((4,)),
            dma((NCH,)),
            dma((NCH,)),
            dma((2, NCH)),
            dma((2, NCH)),
            dma((NCH,)),
            dma((NCH,)),
            dma((2, NCH)),
            dma((2, NCH)),
            dma((2,)),
            dma((2,)),
            dma((2, NCH)),
            dma((2, NCH)),
            dma((2, NCH)),
            dma((2, NCH)),
            pltpu.SemaphoreType.REGULAR,
            dma((4,)),
            dma((4,)),
            dma((3, 4)),
            dma((3, 4)),
            dma((2, NZ - 1)),
            dma((2, NZ - 1)),
            dma((2, NZ - 1)),
            dma((2, NZ - 1)),
        ],
        compiler_params=pltpu.CompilerParams(
            collective_id=0, has_side_effects=True, vmem_limit_bytes=62 << 20
        ),
    )(taps, lat, w, cls, counts, labels)


def on_device(tap_maps, lateral_weight, conv_weight, classifier, tile_counts, labels):
    levels, micros, here, width = tap_maps.shape
    taps = tap_maps.reshape(levels * micros, here, width)
    conv_grad, lateral_grad = head_call(
        taps, lateral_weight[0], conv_weight.reshape(9, CH, CH), classifier, tile_counts, labels
    )
    return (conv_grad[None], lateral_grad[None, :KROWS])


def solution(mesh):
    placed = (
        P(None, None, ("dp", "section"), None),
        P("section", "dp", None),
        P("section", None, None),
        P(),
        P("dp", None),
        P(None, "dp"),
    )
    return jax.shard_map(
        on_device,
        mesh=mesh,
        in_specs=placed,
        out_specs=(P("section", "dp", None), P("section", "dp", None)),
        check_vma=False,
    )
```

```python
import jax
import jax.numpy as jnp
from jax import lax
from jax.experimental import pallas as pl
from jax.experimental.pallas import tpu as pltpu
from jax.sharding import PartitionSpec as P

MESH = pl.DeviceIdType.MESH
F32 = jnp.float32
BF16 = jnp.bfloat16
NZ = 8
NX = 4
COLS = 64
ROWS = 4
PIX = ROWS * COLS
CH = 768
CK = 256
NCH = CH // CK
KROWS = 100
KPAD = 112
GROUPS = NX * NZ
KW = KPAD * GROUPS
SECTIONS = 8
WIDE = NX * PIX
CROWS = 9 * CH // GROUPS
XC, XL = CROWS * NZ, KPAD * NZ
UNIT = XC // 9
HALF = CH // 2
FARROWS = PIX // 2
CLASSES = 150
CPAD = 256


def nt(a, b):
    return lax.dot_general(a, b, (((1,), (1,)), ((), ())), preferred_element_type=F32)


def tn(a, b):
    return lax.dot_general(a, b, (((0,), (0,)), ((), ())), preferred_element_type=F32)


def nn(a, b):
    return jnp.dot(a, b, preferred_element_type=F32)


def head_kernel(
    tap_ref, lat_ref, w_hbm, cls_hbm, counts_ref, labels_ref, conv_out, lat_out,
    cls_ref, tap_pad, wl, w, gx, lat_send, lat_far, lat_near, lat_nat, lat_img,
    ext, xin, xout, gin, dsilu, acc, gpv, rim_out, rim_in, oh_own, oh,
    lat_halo, x_halo, g_out, g_rim,
    ext_all, taps_all, gs_img, gp_all, gs_all, gpv_all, cols_t, taps_t, part_c, part_l, ring_c, ring_l,
    gate_sem, local_sem, tap_send, tap_recv, pass_send, pass_recv, wz_send, w_recv,
    lf_send, lf_recv, ln_send, ln_recv, lz_send, lz_recv, oh_send, oh_recv,
    x_send, x_recv, halo_send, halo_recv, g_send, g_recv, rim_send, rim_recv,
    lh_send, lh_recv, xh_send, xh_recv, gr_send, gr_recv,
    early_sem, gz_send, gz_recv, a_send, a_recv, rc_send, rc_recv, rl_send, rl_recv,
):
    dp = lax.axis_index("dp")
    s = lax.axis_index("section")
    x, z = dp // NZ, dp % NZ
    odd = x % 2
    half = (z % 2 + odd) % 2
    image = z // 2
    has_up = jnp.logical_not(jnp.logical_and(half == 0, x == 0))
    has_down = jnp.logical_not(jnp.logical_and(half == 1, x == NX - 1))
    pair = dp + 1 - 2 * (z % 2)
    up = jnp.where(half == 1, pair, dp - NZ)
    down = jnp.where(half == 0, pair, dp + NZ)
    src_half = z // 4
    is_first, is_last = s == 0, s == SECTIONS - 1
    even = s % 2 == 0
    sibling = s + 1 - 2 * (s % 2)
    z_next, z_prev = x * NZ + (z + 1) % NZ, x * NZ + (z + NZ - 1) % NZ
    x_left, x_right, x_far = (x + NX - 1) % NX, (x + 1) % NX, (x + 2) % NX
    left, right = x_left * NZ + z, x_right * NZ + z

    def home(img):
        return x * NZ + 2 * img + (src_half + odd) % 2

    def remote(src, dst, send, recv, d, sec):
        return pltpu.make_async_remote_copy(
            src_ref=src, dst_ref=dst, send_sem=send, recv_sem=recv,
            device_id={"dp": d, "section": sec}, device_id_type=MESH,
        )

    def local_wait(ref, sem):
        pltpu.make_async_copy(ref, ref, sem).wait()

    w_copy = pltpu.make_async_copy(w_hbm, w, local_sem.at[0])
    w_copy.start()
    cls_copy = pltpu.make_async_copy(cls_hbm, cls_ref, local_sem.at[1])

    @pl.when(is_last)
    def _():
        cls_copy.start()

    barrier = pltpu.get_barrier_semaphore()

    def greet(d, sec):
        pl.semaphore_signal(barrier, inc=1, device_id={"dp": d, "section": sec}, device_id_type=MESH)

    @pl.when(even)
    def _():
        for xx in range(NX):
            for sec in range(SECTIONS):
                @pl.when(jnp.logical_or(xx != x, sec != s))
                def _():
                    greet(xx * NZ + z, sec)

    for d in (left, right, z_next, z_prev):
        greet(d, s)

    @pl.when(has_up)
    def _():
        greet(up, s)
        greet(up, sibling)

    @pl.when(has_down)
    def _():
        greet(down, s)
        greet(down, sibling)

    @pl.when(s > 0)
    def _():
        greet(dp, s - 1)

    @pl.when(s < SECTIONS - 1)
    def _():
        greet(dp, s + 1)

    def native(r):
        return x * NZ + half * 4 + r

    for r in range(4):
        for d in (native(r), home(r)):
            @pl.when(d != dp)
            def _():
                greet(d, s)

    flat = tap_ref[...].reshape(8 * 16, GROUPS * KROWS).astype(F32)
    lane = lax.broadcasted_iota(jnp.int32, (8 * 16, 128), 1)
    for tile in range(KW // 128):
        first = tile * 128
        total = jnp.zeros((8 * 16, 128), F32)
        for g in range(first // KPAD, min((first + 127) // KPAD + 1, GROUPS)):
            lo = first - (KPAD - KROWS) * g
            start = min(max(lo // 128 * 128, 0), GROUPS * KROWS - 256)
            moved = pltpu.roll(flat[:, start:start + 256], (start - lo) % 256, 1)[:, :128]
            inside = jnp.logical_and(lane + first >= KPAD * g, lane + first < KPAD * g + KROWS)
            total = jnp.where(inside, moved, total)
        tap_pad[:, :, first:first + 128] = total.astype(BF16).reshape(8, 16, 128)

    def w_rows(zz):
        return wl.at[pl.ds(pl.multiple_of(zz * KPAD, 16), KPAD), :]

    wl[pl.ds(pl.multiple_of(z * KPAD, 16), KPAD), :] = jnp.concatenate(
        [lat_ref[...].astype(F32), jnp.zeros((KPAD - KROWS, CH), F32)], 0
    ).astype(BF16)

    need = jnp.where(even, 4 + 15, 4 + 16)
    for flag in (has_up, has_down, has_up, has_down, s > 0, s < SECTIONS - 1):
        need += flag.astype(jnp.int32)
    for r in range(4):
        need += (native(r) != dp).astype(jnp.int32) + (home(r) != dp).astype(jnp.int32)
    pl.semaphore_wait(barrier, need)

    def tap_cell(xx, j):
        return taps_all.at[xx, pl.ds(pl.multiple_of(j * 16, 16), 16), :]

    def tap_src(k, xx):
        return tap_pad.at[k, :, pl.ds(xx * XL, XL)]

    def tap_copy(k, xx):
        slot = (k % 2) * SECTIONS + s
        return remote(
            tap_src(k, xx), tap_cell(x, slot), tap_send.at[k, xx], tap_recv.at[x, slot], xx * NZ + z, k // 2 * 2
        )

    def tap_pass(xx):
        return remote(taps_all.at[xx], taps_all.at[xx], pass_send.at[xx], pass_recv.at[xx], dp, s + 1)

    def elsewhere(k, xx):
        return jnp.logical_or(xx != x, k // 2 * 2 != s)

    order = (0, -1, 1, -2, 2, -3, 3, -4)

    def ring_z(i):
        return (z + NZ + order[i]) % NZ

    def w_send_z(i, way):
        block = w_rows(ring_z(i))
        return remote(block, block, wz_send.at[way, i], w_recv.at[ring_z(i)], z_next if way == 0 else z_prev, s)

    def z_ways(i):
        ways = []
        if order[i] <= 0 and order[i] > -4:
            ways.append(0)
        if order[i] >= 0 and order[i] < 3:
            ways.append(1)
        return ways

    def w_step(i):
        if i > 0:
            local_wait(w_rows(ring_z(i)), w_recv.at[ring_z(i)])
        for way in z_ways(i):
            w_send_z(i, way).start()

    @pl.when(even)
    def _():
        w_step(0)

    for k in range(8):
        for xx in range(NX):
            @pl.when(elsewhere(k, xx))
            def _():
                tap_copy(k, xx).start()

            @pl.when(jnp.logical_not(elsewhere(k, xx)))
            def _():
                slot = (k % 2) * SECTIONS + s
                pltpu.make_async_copy(tap_src(k, xx), tap_cell(x, slot), tap_recv.at[x, slot]).start()

    def pass_turn(k):
        pl.semaphore_signal(gate_sem.at[k], inc=1, device_id={"dp": dp, "section": s + 1}, device_id_type=MESH)

    @pl.when(even)
    def _():
        for i in range(1, NZ):
            w_step(i)
        pass_turn(0)

    @pl.when(jnp.logical_not(even))
    def _():
        pl.semaphore_wait(gate_sem.at[0], 1)
        for i in range(NZ):
            w_step(i)

    def oh_rows(r):
        return oh.at[pl.ds(pl.multiple_of(r * COLS, COLS), COLS), :]

    def oh_src(img):
        return oh_own.at[img // 2, pl.ds((img % 2) * COLS, COLS), :]

    def oh_copy(img):
        return remote(oh_src(img), oh_rows(z % 4), oh_send.at[img], oh_recv.at[z % 4], home(img), s)

    @pl.when(is_last)
    def _():
        sub = lax.broadcasted_iota(jnp.int32, (CPAD, 2 * COLS), 0)
        tile_of = lax.broadcasted_iota(jnp.int32, (CPAD, 2 * COLS), 1) // COLS
        for micro in range(2):
            count = counts_ref[0, micro]
            share = 1.0 / (count.astype(F32) * (COLS * GROUPS * 2))
            weight = jnp.where(tile_of < count, share, 0.0)
            hot = jnp.where(sub == labels_ref[micro:micro + 1, :], 1.0, 0.0)
            oh_own[micro] = jnp.where(sub == CPAD - 1, weight, hot).T.astype(BF16)
        for img in range(4):
            @pl.when(home(img) != dp)
            def _():
                oh_copy(img).start()

            @pl.when(home(img) == dp)
            def _():
                pltpu.make_async_copy(oh_src(img), oh_rows(z % 4), oh_recv.at[z % 4]).start()

    @pl.when(jnp.logical_not(has_up))
    def _():
        ext[0:COLS, :] = jnp.zeros((COLS, CH), BF16)

    @pl.when(jnp.logical_not(has_down))
    def _():
        ext[COLS + PIX:, :] = jnp.zeros((COLS, CH), BF16)

    @pl.when(even)
    def _():
        for xx in range(NX):
            for j in range(2 * SECTIONS):
                local_wait(tap_cell(xx, j), tap_recv.at[xx, j])
            tap_pass(xx).start()

    @pl.when(jnp.logical_not(even))
    def _():
        for xx in range(NX):
            local_wait(taps_all.at[xx], pass_recv.at[xx])

    first_rows, last_rows = pl.ds(0, FARROWS), pl.ds(FARROWS, FARROWS)
    half_rows = (first_rows, last_rows)

    def far_copy(way):
        return remote(
            lat_send.at[2, half_rows[way]], lat_far.at[way], lf_send.at[way], lf_recv.at[way],
            right if way == 0 else left, s,
        )

    def near_copy(way, part):
        return remote(
            lat_send.at[way, half_rows[part]], lat_near.at[way, half_rows[part]],
            ln_send.at[way, part], ln_recv.at[way, part], right if way == 0 else left, s,
        )

    lat_send[2] = nn(taps_all[x_far], wl[...]).astype(BF16)

    @pl.when(jnp.logical_not(even))
    def _():
        pl.semaphore_wait(gate_sem.at[1], 1)

    for way in range(2):
        far_copy(way).start()
    for way in range(2):
        acc[way] = nn(taps_all[x_right if way == 0 else x_left], wl[...])
        rows = half_rows[1 - way]
        lat_send[way, rows] = acc[way, rows].astype(BF16)
        near_copy(way, 1 - way).start()
    acc[2] = nn(taps_all[x], wl[...])
    for way in range(2):
        rows = half_rows[way]
        local_wait(lat_far.at[way], lf_recv.at[way])
        lat_send[way, rows] = (acc[way, rows] + lat_far[way].astype(F32)).astype(BF16)
        near_copy(way, way).start()
    for part in range(2):
        rows = half_rows[part]
        for way in (1 - part, part):
            local_wait(lat_near.at[way, rows], ln_recv.at[way, part])
        lat_nat[rows] = (
            acc[2, rows] + lat_near[0, rows].astype(F32) + lat_near[1, rows].astype(F32)
        ).astype(BF16)

    @pl.when(even)
    def _():
        pass_turn(1)

    def band(ref, j):
        return ref.at[pl.ds(pl.multiple_of(j * COLS, COLS), COLS), :]

    def lat_copy(img):
        return remote(band(lat_nat, img), band(lat_img, z % 4), lz_send.at[img], lz_recv.at[z % 4], home(img), s)

    for img in range(4):
        @pl.when(home(img) != dp)
        def _():
            lat_copy(img).start()

        @pl.when(home(img) == dp)
        def _():
            pltpu.make_async_copy(band(lat_nat, img), band(lat_img, z % 4), lz_recv.at[z % 4]).start()

    for r in range(4):
        local_wait(band(lat_img, r), lz_recv.at[r])

    def lat_up():
        return remote(band(lat_img, 0), lat_halo.at[1], lh_send.at[0], lh_recv.at[1], up, s)

    def lat_down():
        return remote(band(lat_img, ROWS - 1), lat_halo.at[0], lh_send.at[1], lh_recv.at[0], down, s)

    @pl.when(jnp.logical_and(has_up, jnp.logical_not(even)))
    def _():
        lat_up().start()

    @pl.when(jnp.logical_and(has_down, jnp.logical_not(even)))
    def _():
        lat_down().start()

    w_copy.wait()

    def lanes(c):
        return pl.ds(c * CK, CK)

    def x_copy(c):
        return pltpu.make_async_remote_copy(
            src_ref=xout.at[:, lanes(c)], dst_ref=xin.at[:, lanes(c)],
            send_sem=x_send.at[c], recv_sem=x_recv.at[c],
            device_id={"dp": dp, "section": s + 1}, device_id_type=MESH,
        )

    def halo_up(c):
        return pltpu.make_async_remote_copy(
            src_ref=ext.at[pl.ds(COLS, COLS), lanes(c)], dst_ref=ext.at[pl.ds(COLS + PIX, COLS), lanes(c)],
            send_sem=halo_send.at[0, c], recv_sem=halo_recv.at[1, c],
            device_id={"dp": up, "section": s}, device_id_type=MESH,
        )

    def halo_down(c):
        return pltpu.make_async_remote_copy(
            src_ref=ext.at[pl.ds(PIX, COLS), lanes(c)], dst_ref=ext.at[pl.ds(0, COLS), lanes(c)],
            send_sem=halo_send.at[1, c], recv_sem=halo_recv.at[0, c],
            device_id={"dp": down, "section": s}, device_id_type=MESH,
        )

    def edge_up(c):
        return remote(
            xout.at[pl.ds(0, COLS), lanes(c)], x_halo.at[1, :, lanes(c)],
            xh_send.at[0, c], xh_recv.at[1, c], up, s + 1,
        )

    def edge_down(c):
        return remote(
            xout.at[pl.ds(PIX - COLS, COLS), lanes(c)], x_halo.at[0, :, lanes(c)],
            xh_send.at[1, c], xh_recv.at[0, c], down, s + 1,
        )

    def take_edges(c):
        cols = slice(c * CK, (c + 1) * CK)
        for side, flag, rows in ((0, has_up, slice(0, COLS)), (1, has_down, slice(COLS + PIX, 2 * COLS + PIX))):
            @pl.when(flag)
            def _():
                local_wait(x_halo.at[side, :, lanes(c)], xh_recv.at[side, c])
                ext[rows, cols] = (
                    x_halo[side, :, cols].astype(F32) + lat_halo[side, :, cols].astype(F32)
                ).astype(BF16)

    def take_x(c):
        cols = slice(c * CK, (c + 1) * CK)

        @pl.when(is_first)
        def _():
            ext[COLS:COLS + PIX, cols] = lat_img[:, cols]

        @pl.when(s > 0)
        def _():
            local_wait(xin.at[:, lanes(c)], x_recv.at[c])
            ext[COLS:COLS + PIX, cols] = (xin[:, cols].astype(F32) + lat_img[:, cols].astype(F32)).astype(BF16)

        @pl.when(jnp.logical_and(has_up, even))
        def _():
            halo_up(c).start()

        @pl.when(jnp.logical_and(has_down, even))
        def _():
            halo_down(c).start()

    def wait_halo(c):
        @pl.when(has_up)
        def _():
            local_wait(ext.at[pl.ds(0, COLS), lanes(c)], halo_recv.at[0, c])

        @pl.when(has_down)
        def _():
            local_wait(ext.at[pl.ds(COLS + PIX, COLS), lanes(c)], halo_recv.at[1, c])

    def conv_part(c, dr, dc, ncols):
        rows = (1 + dr) * COLS
        return nn(
            ext[rows:rows + PIX, c * CK:(c + 1) * CK],
            w[(dr + 1) * 3 + dc + 1, c * CK:(c + 1) * CK, ncols],
        )

    every = slice(0, CH)

    def conv_inner(c, start):
        for dc in (-1, 0, 1):
            term = conv_part(c, 0, dc, every)
            if start:
                acc[dc + 1] = term
            else:
                acc[dc + 1] += term

    def conv_outer(c):
        for dc in (-1, 0, 1):
            acc[dc + 1] += conv_part(c, -1, dc, every) + conv_part(c, 1, dc, every)

    col = lax.broadcasted_iota(jnp.int32, (PIX, CK), 0) % COLS

    def before(v):
        return jnp.where(col == 0, 0.0, pltpu.roll(v, 1, 0))

    def after(v):
        return jnp.where(col == COLS - 1, 0.0, pltpu.roll(v, PIX - 1, 0))

    def conv_finish(n, chunks, direct):
        ncols = slice(n * CK, (n + 1) * CK)
        parts = []
        for dc in (-1, 0, 1):
            part = acc[dc + 1, :, ncols]
            for c in chunks:
                part += conv_part(c, -1, dc, ncols) + conv_part(c, 1, dc, ncols)
            parts.append(part)
        pre = before(parts[0]) + parts[1] + after(parts[2])
        sig = 1.0 / (1.0 + jnp.exp(-pre))
        xout[:, ncols] = (pre * sig).astype(BF16)

        @pl.when(s < SECTIONS - 1)
        def _():
            x_copy(n).start()

        if direct:
            @pl.when(has_up)
            def _():
                edge_up(n).start()

            @pl.when(has_down)
            def _():
                edge_down(n).start()

        dsilu[:, ncols] = sig * (1.0 + pre * (1.0 - sig))

    @pl.when(even)
    def _():
        take_x(0)
        conv_inner(0, True)
        take_x(1)
        conv_inner(1, False)
        wait_halo(0)
        conv_outer(0)
        take_x(2)
        conv_inner(2, False)
        wait_halo(1)
        conv_outer(1)
        wait_halo(2)
        for n in range(NCH):
            conv_finish(n, (2,), True)

    @pl.when(jnp.logical_not(even))
    def _():
        for c in range(NCH):
            take_x(c)
        for c in range(NCH):
            conv_inner(c, c == 0)

        @pl.when(has_up)
        def _():
            local_wait(lat_halo.at[0], lh_recv.at[0])

        @pl.when(has_down)
        def _():
            local_wait(lat_halo.at[1], lh_recv.at[1])

        for c in range(NCH):
            take_edges(c)
        for n in range(NCH):
            conv_finish(n, range(NCH), False)

    def gather_copy(buf, kind, way):
        return remote(
            buf.at[x], buf.at[x], a_send.at[kind, way], a_recv.at[kind, way], right if way == 0 else left, s
        )

    def gather_far(buf, kind, way):
        rows = buf.shape[1] // 2
        block = buf.at[x_left if way == 0 else x_right, pl.ds(way * rows, rows), :]
        return remote(
            block, block, a_send.at[kind, 2 + way], a_recv.at[kind, 2 + way], right if way == 0 else left, s
        )

    def gather_start(buf, kind):
        for way in range(2):
            gather_copy(buf, kind, way).start()

    def gather_forward(buf, kind):
        for way in range(2):
            local_wait(buf.at[x_left if way == 0 else x_right], a_recv.at[kind, way])
            gather_far(buf, kind, way).start()

    def gather_finish(buf, kind):
        rows = buf.shape[1] // 2
        for way in range(2):
            local_wait(buf.at[x_far, pl.ds(way * rows, rows), :], a_recv.at[kind, 2 + way])

    def gather_sent(buf, kind):
        for way in range(2):
            gather_copy(buf, kind, way).wait_send()
            gather_far(buf, kind, way).wait_send()

    def early_start():
        ext_all[x] = ext[...]
        gather_start(ext_all, 2)

    def early_finish():
        gather_finish(ext_all, 2)

        @pl.loop(0, NX)
        def _(src):
            lanes_of = pl.ds(pl.multiple_of(src * PIX, PIX), PIX)
            for dr in range(3):
                cols_t[dr, :, lanes_of] = ext_all[src, dr * COLS:dr * COLS + PIX, :].T
            taps_t[:, lanes_of] = taps_all[src].T

    @pl.when(jnp.logical_and(s < 6, s % 2 == 1))
    def _():
        pl.semaphore_signal(early_sem, inc=1, device_id={"dp": dp, "section": s - 1}, device_id_type=MESH)

    @pl.when(jnp.logical_and(s < 6, s % 2 == 0))
    def _():
        pl.semaphore_wait(early_sem, 1)

    @pl.when(s < 6)
    def _():
        early_start()

    @pl.when(s < 4)
    def _():
        gather_forward(ext_all, 2)
        early_finish()

    @pl.when(is_last)
    def _():
        for r in range(4):
            local_wait(oh_rows(r), oh_recv.at[r])
        cls_copy.wait()
        logits = nt(xout[...], cls_ref[...])
        spot = lax.broadcasted_iota(jnp.int32, (PIX, CPAD), 1)
        expo = jnp.exp(logits)
        probs = expo / jnp.sum(expo, axis=-1, keepdims=True)
        marks = oh[...].astype(F32)
        weight = jnp.sum(jnp.where(spot == CPAD - 1, marks, 0.0), axis=-1, keepdims=True)
        grad_logits = ((probs - marks[:, :CLASSES]) * weight).astype(BF16)
        gx[...] = nn(grad_logits, cls_ref[...])

    def g_copy(c):
        return pltpu.make_async_remote_copy(
            src_ref=g_out.at[:, lanes(c)], dst_ref=gin.at[:, lanes(c)],
            send_sem=g_send.at[c], recv_sem=g_recv.at[c],
            device_id={"dp": dp, "section": s - 1}, device_id_type=MESH,
        )

    def rim_up(c):
        return pltpu.make_async_remote_copy(
            src_ref=rim_out.at[0, :, lanes(c)], dst_ref=rim_in.at[1, :, lanes(c)],
            send_sem=rim_send.at[0, c], recv_sem=rim_recv.at[1, c],
            device_id={"dp": up, "section": s}, device_id_type=MESH,
        )

    def rim_down(c):
        return pltpu.make_async_remote_copy(
            src_ref=rim_out.at[1, :, lanes(c)], dst_ref=rim_in.at[0, :, lanes(c)],
            send_sem=rim_send.at[1, c], recv_sem=rim_recv.at[0, c],
            device_id={"dp": down, "section": s}, device_id_type=MESH,
        )

    def take_g(c):
        cols = slice(c * CK, (c + 1) * CK)

        @pl.when(s < SECTIONS - 1)
        def _():
            local_wait(gin.at[:, lanes(c)], g_recv.at[c])
            gx[:, cols] = gin[:, cols].astype(F32)

        for side, flag, rows in ((0, has_up, slice(0, COLS)), (1, has_down, slice(PIX - COLS, PIX))):
            @pl.when(jnp.logical_and(flag, even))
            def _():
                local_wait(g_rim.at[side, :, lanes(c)], gr_recv.at[side, c])
                gx[rows, cols] += g_rim[side, :, cols].astype(F32)

        grad_pre = (gx[:, cols] * dsilu[:, cols]).astype(BF16).astype(F32)
        gpv[0, :, cols] = after(grad_pre).astype(BF16)
        gpv[1, :, cols] = grad_pre.astype(BF16)
        gp_all[x, :, cols] = grad_pre.astype(BF16)
        gpv[2, :, cols] = before(grad_pre).astype(BF16)

    def back_part(c, dr, krows):
        total = None
        for dc in (-1, 0, 1):
            term = nt(
                gpv[dc + 1, :, c * CK:(c + 1) * CK],
                w[(dr + 1) * 3 + dc + 1, krows, c * CK:(c + 1) * CK],
            )
            total = term if total is None else total + term
        return total

    def rim_direct_up(c):
        return remote(
            rim_out.at[0, :, lanes(c)], g_rim.at[1, :, lanes(c)], gr_send.at[0, c], gr_recv.at[1, c], up, s - 1
        )

    def rim_direct_down(c):
        return remote(
            rim_out.at[1, :, lanes(c)], g_rim.at[0, :, lanes(c)], gr_send.at[1, c], gr_recv.at[0, c], down, s - 1
        )

    def send_rims(n, upward, downward):
        @pl.when(has_up)
        def _():
            upward(n).start()

        @pl.when(has_down)
        def _():
            downward(n).start()

    def back_rims(n, chunks, start):
        ncols = slice(n * CK, (n + 1) * CK)
        for side, dr in ((0, -1), (2, 1)):
            total = None if start else acc[side, :, ncols]
            for c in chunks:
                term = back_part(c, dr, ncols)
                total = term if total is None else total + term
            acc[side, :, ncols] = total
            if dr < 0:
                rim_out[0, :, ncols] = total[0:COLS].astype(BF16)
            else:
                rim_out[1, :, ncols] = total[PIX - COLS:].astype(BF16)

    def back_inner(n, chunks, start):
        ncols = slice(n * CK, (n + 1) * CK)
        total = None if start else acc[1, :, ncols]
        for c in chunks:
            term = back_part(c, 0, ncols)
            total = term if total is None else total + term
        acc[1, :, ncols] = total
        acc[1, 0:PIX - COLS, ncols] += acc[0, COLS:, ncols]
        acc[1, COLS:, ncols] += acc[2, 0:PIX - COLS, ncols]

    def add_rims(n):
        ncols = slice(n * CK, (n + 1) * CK)

        @pl.when(has_up)
        def _():
            local_wait(rim_in.at[0, :, lanes(n)], rim_recv.at[0, n])
            acc[1, 0:COLS, ncols] += rim_in[0, :, ncols].astype(F32)

        @pl.when(has_down)
        def _():
            local_wait(rim_in.at[1, :, lanes(n)], rim_recv.at[1, n])
            acc[1, PIX - COLS:, ncols] += rim_in[1, :, ncols].astype(F32)

        gs_img[:, ncols] = acc[1, :, ncols].astype(BF16)

    def send_g(n):
        ncols = slice(n * CK, (n + 1) * CK)
        g_out[:, ncols] = acc[1, :, ncols].astype(BF16)
        g_copy(n).start()

    @pl.when(jnp.logical_not(even))
    def _():
        take_g(0)
        for dr in (-1, 0, 1):
            acc[dr + 1] = back_part(0, dr, every)
        take_g(1)
        for dr in (-1, 0, 1):
            acc[dr + 1] += back_part(1, dr, every)
        take_g(2)
        for n in range(NCH):
            back_rims(n, (2,), False)
            send_rims(n, rim_direct_up, rim_direct_down)
            back_inner(n, (2,), False)
            send_g(n)
        for n in range(NCH):
            send_rims(n, rim_up, rim_down)
        gather_start(gp_all, 0)
        for n in range(NCH):
            add_rims(n)

    @pl.when(even)
    def _():
        def finish(n):
            back_inner(n, chunks, True)
            add_rims(n)

            @pl.when(s > 0)
            def _():
                send_g(n)

        for c in range(NCH):
            take_g(c)

        @pl.when(is_first)
        def _():
            gather_start(gp_all, 0)

        chunks = range(NCH)
        back_rims(0, chunks, True)
        send_rims(0, rim_up, rim_down)
        back_rims(1, chunks, True)
        send_rims(1, rim_up, rim_down)
        finish(0)
        back_rims(2, chunks, True)
        send_rims(2, rim_up, rim_down)
        finish(1)
        finish(2)

    def gz_copy(r):
        return remote(
            band(gs_img, r), band(gs_all.at[x], image), gz_send.at[r], gz_recv.at[image], native(r), s
        )

    for r in range(4):
        @pl.when(native(r) != dp)
        def _():
            gz_copy(r).start()

        @pl.when(native(r) == dp)
        def _():
            pltpu.make_async_copy(band(gs_img, r), band(gs_all.at[x], image), gz_recv.at[image]).start()

    @pl.when(jnp.logical_and(even, s > 0))
    def _():
        gather_start(gp_all, 0)

    @pl.when(s >= 6)
    def _():
        early_start()

    gather_forward(gp_all, 0)

    @pl.when(s >= 4)
    def _():
        gather_forward(ext_all, 2)

    whole_col = lax.broadcasted_iota(jnp.int32, (PIX, CH), 0) % COLS

    def spread(src):
        rows = pl.ds(pl.multiple_of(src * PIX, PIX), PIX)
        value = gp_all[src].astype(F32)
        gpv_all[0, rows, :] = jnp.where(whole_col == COLS - 1, 0.0, pltpu.roll(value, PIX - 1, 0)).astype(BF16)
        gpv_all[1, rows, :] = gp_all[src]
        gpv_all[2, rows, :] = jnp.where(whole_col == 0, 0.0, pltpu.roll(value, 1, 0)).astype(BF16)

    spread(x)
    spread(x_left)
    spread(x_right)
    gather_finish(gp_all, 0)
    for img in range(4):
        local_wait(band(gs_all.at[x], img), gz_recv.at[img])
    gather_start(gs_all, 1)
    spread(x_far)

    @pl.when(s >= 4)
    def _():
        early_finish()

    def conv_unit(u):
        unit = 9 * x + u
        o = unit // 4
        chans = pl.ds(pl.multiple_of((unit % 4) * UNIT, UNIT), UNIT)
        part_c[pl.ds(pl.multiple_of(u * UNIT, UNIT), UNIT), :] = nn(cols_t[o // 3, chans, :], gpv_all[o % 3])

    def conv_slice(zz):
        @pl.loop(0, 2)
        def _(k):
            conv_unit(zz + k)

    def slice_at(way, t):
        return (z + NZ - 1 - t) % NZ if way == 0 else (z + 1 + t) % NZ

    def own_rows(part, rows, way, t):
        at = pl.ds(pl.multiple_of(slice_at(way, t) * rows, 8), rows)
        return part[at, way * HALF:(way + 1) * HALF]

    def hop(ring, send, recv, way, t):
        return pltpu.make_async_remote_copy(
            src_ref=ring.at[way, t], dst_ref=ring.at[way, t + 1],
            send_sem=send.at[way, t], recv_sem=recv.at[way, t],
            device_id={"dp": z_next if way == 0 else z_prev, "section": s}, device_id_type=MESH,
        )

    conv_ring = (ring_c, rc_send, rc_recv)
    lat_ring = (ring_l, rl_send, rl_recv)
    def ring_start(ring, part, rows):
        for way in range(2):
            ring[0][way, 0] = own_rows(part, rows, way, 0).astype(BF16)
            hop(*ring, way, 0).start()

    def ring_step(ring, part, rows, out, t):
        buf = ring[0]
        for way in range(2):
            local_wait(buf.at[way, t + 1], ring[2].at[way, t])
            total = buf[way, t + 1].astype(F32) + own_rows(part, rows, way, t + 1)
            if t < NZ - 2:
                buf[way, t + 1] = total.astype(BF16)
                hop(*ring, way, t + 1).start()
            else:
                out[:, way * HALF:(way + 1) * HALF] = total

    def conv_step(t):
        ring_step(conv_ring, part_c, CROWS, conv_out, t)

    def lat_step(t):
        ring_step(lat_ring, part_l, KPAD, lat_out, t)

    @pl.loop(0, 2)
    def _(k):
        conv_slice((z + 1 + k * (NZ - 2)) % NZ)

    ring_start(conv_ring, part_c, CROWS)

    @pl.loop(0, 2)
    def _(k):
        conv_slice((z + 2 + k * (NZ - 4)) % NZ)

    gather_forward(gs_all, 1)
    conv_step(0)

    @pl.loop(0, 2)
    def _(k):
        conv_slice((z + 3 + k * (NZ - 6)) % NZ)

    gather_finish(gs_all, 1)
    part_l[...] = nn(taps_t[...], gs_all[...].reshape(WIDE, CH))
    ring_start(lat_ring, part_l, KPAD)
    conv_step(1)

    @pl.loop(0, 2)
    def _(k):
        conv_slice((z + 4 * k) % NZ)

    lat_step(0)
    for t in range(2, NZ - 1):
        conv_step(t)
        lat_step(t - 1)
    lat_step(NZ - 2)

    for k in range(8):
        for xx in range(NX):
            @pl.when(elsewhere(k, xx))
            def _():
                tap_copy(k, xx).wait_send()

    @pl.when(even)
    def _():
        for xx in range(NX):
            tap_pass(xx).wait_send()

    for i in range(NZ):
        for way in z_ways(i):
            w_send_z(i, way).wait_send()
    for way in range(2):
        far_copy(way).wait_send()
        for part in range(2):
            near_copy(way, part).wait_send()
    for r in range(4):
        @pl.when(home(r) != dp)
        def _():
            lat_copy(r).wait_send()

    @pl.when(is_last)
    def _():
        for img in range(4):
            @pl.when(home(img) != dp)
            def _():
                oh_copy(img).wait_send()

    for c in range(NCH):
        @pl.when(s < SECTIONS - 1)
        def _():
            x_copy(c).wait_send()

        @pl.when(s > 0)
        def _():
            g_copy(c).wait_send()

        @pl.when(has_up)
        def _():
            rim_up(c).wait_send()

        @pl.when(has_down)
        def _():
            rim_down(c).wait_send()

        @pl.when(jnp.logical_and(has_up, even))
        def _():
            halo_up(c).wait_send()
            edge_up(c).wait_send()

        @pl.when(jnp.logical_and(has_down, even))
        def _():
            halo_down(c).wait_send()
            edge_down(c).wait_send()

        @pl.when(jnp.logical_and(has_up, jnp.logical_not(even)))
        def _():
            rim_direct_up(c).wait_send()

        @pl.when(jnp.logical_and(has_down, jnp.logical_not(even)))
        def _():
            rim_direct_down(c).wait_send()

    @pl.when(jnp.logical_and(has_up, jnp.logical_not(even)))
    def _():
        lat_up().wait_send()

    @pl.when(jnp.logical_and(has_down, jnp.logical_not(even)))
    def _():
        lat_down().wait_send()

    for kind, buf in enumerate((gp_all, gs_all, ext_all)):
        gather_sent(buf, kind)
    for r in range(4):
        @pl.when(native(r) != dp)
        def _():
            gz_copy(r).wait_send()

    for way in range(2):
        for t in range(NZ - 1):
            hop(*conv_ring, way, t).wait_send()
            hop(*lat_ring, way, t).wait_send()


def head_call(taps, lat, w, cls, counts, labels):
    dma = pltpu.SemaphoreType.DMA
    hbm = pl.BlockSpec(memory_space=pl.ANY)
    vmem = pl.BlockSpec(memory_space=pltpu.VMEM)
    smem = pl.BlockSpec(memory_space=pltpu.SMEM)
    return pl.pallas_call(
        head_kernel,
        out_shape=(
            jax.ShapeDtypeStruct((CROWS, CH), F32),
            jax.ShapeDtypeStruct((KPAD, CH), F32),
        ),
        in_specs=[vmem, vmem, hbm, hbm, smem, vmem],
        out_specs=(vmem, vmem),
        scratch_shapes=[
            pltpu.VMEM((CLASSES, CH), BF16),
            pltpu.VMEM((8, 16, KW), BF16),
            pltpu.VMEM((XL, CH), BF16),
            pltpu.VMEM((9, CH, CH), BF16),
            pltpu.VMEM((PIX, CH), F32),
            pltpu.VMEM((3, PIX, CH), BF16),
            pltpu.VMEM((2, FARROWS, CH), BF16),
            pltpu.VMEM((2, PIX, CH), BF16),
            pltpu.VMEM((PIX, CH), BF16),
            pltpu.VMEM((PIX, CH), BF16),
            pltpu.VMEM((PIX + 2 * COLS, CH), BF16),
            pltpu.VMEM((PIX, CH), BF16),
            pltpu.VMEM((PIX, CH), BF16),
            pltpu.VMEM((PIX, CH), BF16),
            pltpu.VMEM((PIX, CH), F32),
            pltpu.VMEM((3, PIX, CH), F32),
            pltpu.VMEM((3, PIX, CH), BF16),
            pltpu.VMEM((2, COLS, CH), BF16),
            pltpu.VMEM((2, COLS, CH), BF16),
            pltpu.VMEM((2, 2 * COLS, CPAD), BF16),
            pltpu.VMEM((PIX, CPAD), BF16),
            pltpu.VMEM((2, COLS, CH), BF16),
            pltpu.VMEM((2, COLS, CH), BF16),
            pltpu.VMEM((PIX, CH), BF16),
            pltpu.VMEM((2, COLS, CH), BF16),
            pltpu.VMEM((NX, PIX + 2 * COLS, CH), BF16),
            pltpu.VMEM((NX, PIX, XL), BF16),
            pltpu.VMEM((PIX, CH), BF16),
            pltpu.VMEM((NX, PIX, CH), BF16),
            pltpu.VMEM((NX, PIX, CH), BF16),
            pltpu.VMEM((3, WIDE, CH), BF16),
            pltpu.VMEM((3, CH, WIDE), BF16),
            pltpu.VMEM((XL, WIDE), BF16),
            pltpu.VMEM((XC, CH), F32),
            pltpu.VMEM((XL, CH), F32),
            pltpu.VMEM((2, NZ, CROWS, HALF), BF16),
            pltpu.VMEM((2, NZ, KPAD, HALF), BF16),
            pltpu.SemaphoreType.REGULAR((2,)),
            dma((2,)),
            dma((8, NX)),
            dma((NX, 2 * SECTIONS)),
            dma((NX,)),
            dma((NX,)),
            dma((2, NZ)),
            dma((NZ,)),
            dma((2,)),
            dma((2,)),
            dma((2, 2)),
            dma((2, 2)),
            dma((4,)),
            dma((4,)),
            dma((4,)),
            dma((4,)),
            dma((NCH,)),
            dma((NCH,)),
            dma((2, NCH)),
            dma((2, NCH)),
            dma((NCH,)),
            dma((NCH,)),
            dma((2, NCH)),
            dma((2, NCH)),
            dma((2,)),
            dma((2,)),
            dma((2, NCH)),
            dma((2, NCH)),
            dma((2, NCH)),
            dma((2, NCH)),
            pltpu.SemaphoreType.REGULAR,
            dma((4,)),
            dma((4,)),
            dma((3, 4)),
            dma((3, 4)),
            dma((2, NZ - 1)),
            dma((2, NZ - 1)),
            dma((2, NZ - 1)),
            dma((2, NZ - 1)),
        ],
        compiler_params=pltpu.CompilerParams(
            collective_id=0, has_side_effects=True, vmem_limit_bytes=62 << 20
        ),
    )(taps, lat, w, cls, counts, labels)


def on_device(tap_maps, lateral_weight, conv_weight, classifier, tile_counts, labels):
    levels, micros, here, width = tap_maps.shape
    taps = tap_maps.reshape(levels * micros, here, width)
    conv_grad, lateral_grad = head_call(
        taps, lateral_weight[0], conv_weight.reshape(9, CH, CH), classifier.T, tile_counts, labels
    )
    return (conv_grad[None], lateral_grad[None, :KROWS])


def solution(mesh):
    placed = (
        P(None, None, ("dp", "section"), None),
        P("section", "dp", None),
        P("section", None, None),
        P(),
        P("dp", None),
        P(None, "dp"),
    )
    return jax.shard_map(
        on_device,
        mesh=mesh,
        in_specs=placed,
        out_specs=(P("section", "dp", None), P("section", "dp", None)),
        check_vma=False,
    )
```

```python
import jax
import jax.numpy as jnp
from jax import lax
from jax.experimental import pallas as pl
from jax.experimental.pallas import tpu as pltpu
from jax.sharding import PartitionSpec as P

MESH = pl.DeviceIdType.MESH
F32 = jnp.float32
BF16 = jnp.bfloat16
NZ = 8
NX = 4
COLS = 64
ROWS = 4
PIX = ROWS * COLS
CH = 768
CK = 256
NCH = CH // CK
KROWS = 100
KPAD = 112
GROUPS = NX * NZ
KW = KPAD * GROUPS
SECTIONS = 8
WIDE = NX * PIX
CROWS = 9 * CH // GROUPS
XC, XL = CROWS * NZ, KPAD * NZ
UNIT = XC // 9
HALF = CH // 2
FARROWS = PIX // 2
CLASSES = 150
CPAD = 256


def nt(a, b):
    return lax.dot_general(a, b, (((1,), (1,)), ((), ())), preferred_element_type=F32)


def tn(a, b):
    return lax.dot_general(a, b, (((0,), (0,)), ((), ())), preferred_element_type=F32)


def nn(a, b):
    return jnp.dot(a, b, preferred_element_type=F32)


def head_kernel(
    tap_ref, lat_ref, w_hbm, cls_hbm, counts_ref, labels_ref, conv_out, lat_out,
    cls_ref, tap_pad, wl, w, gx, lat_send, lat_far, lat_near, lat_nat, lat_img,
    ext, xin, xout, gin, dsilu, acc, gpv, rim_out, rim_in, oh_own, oh,
    lat_halo, x_halo, g_out, g_rim,
    ext_all, taps_all, gs_img, gp_all, gs_all, gpv_all, cols_t, taps_t, part_c, part_l, ring_c, ring_l,
    gate_sem, local_sem, tap_send, tap_recv, pass_send, pass_recv, wz_send, w_recv,
    lf_send, lf_recv, ln_send, ln_recv, lz_send, lz_recv, oh_send, oh_recv,
    x_send, x_recv, halo_send, halo_recv, g_send, g_recv, rim_send, rim_recv,
    lh_send, lh_recv, xh_send, xh_recv, gr_send, gr_recv,
    early_sem, gz_send, gz_recv, a_send, a_recv, rc_send, rc_recv, rl_send, rl_recv,
):
    dp = lax.axis_index("dp")
    s = lax.axis_index("section")
    x, z = dp // NZ, dp % NZ
    odd = x % 2
    half = (z % 2 + odd) % 2
    image = z // 2
    has_up = jnp.logical_not(jnp.logical_and(half == 0, x == 0))
    has_down = jnp.logical_not(jnp.logical_and(half == 1, x == NX - 1))
    pair = dp + 1 - 2 * (z % 2)
    up = jnp.where(half == 1, pair, dp - NZ)
    down = jnp.where(half == 0, pair, dp + NZ)
    src_half = z // 4
    is_first, is_last = s == 0, s == SECTIONS - 1
    even = s % 2 == 0
    sibling = s + 1 - 2 * (s % 2)
    z_next, z_prev = x * NZ + (z + 1) % NZ, x * NZ + (z + NZ - 1) % NZ
    x_left, x_right, x_far = (x + NX - 1) % NX, (x + 1) % NX, (x + 2) % NX
    left, right = x_left * NZ + z, x_right * NZ + z

    def home(img):
        return x * NZ + 2 * img + (src_half + odd) % 2

    def remote(src, dst, send, recv, d, sec):
        return pltpu.make_async_remote_copy(
            src_ref=src, dst_ref=dst, send_sem=send, recv_sem=recv,
            device_id={"dp": d, "section": sec}, device_id_type=MESH,
        )

    def local_wait(ref, sem):
        pltpu.make_async_copy(ref, ref, sem).wait()

    w_copy = pltpu.make_async_copy(w_hbm, w, local_sem.at[0])
    w_copy.start()
    cls_copy = pltpu.make_async_copy(cls_hbm, cls_ref, local_sem.at[1])

    @pl.when(is_last)
    def _():
        cls_copy.start()

    barrier = pltpu.get_barrier_semaphore()

    def greet(d, sec):
        pl.semaphore_signal(barrier, inc=1, device_id={"dp": d, "section": sec}, device_id_type=MESH)

    @pl.when(even)
    def _():
        for xx in range(NX):
            for sec in range(SECTIONS):
                @pl.when(jnp.logical_or(xx != x, sec != s))
                def _():
                    greet(xx * NZ + z, sec)

    for d in (left, right, z_next, z_prev):
        greet(d, s)

    @pl.when(has_up)
    def _():
        greet(up, s)
        greet(up, sibling)

    @pl.when(has_down)
    def _():
        greet(down, s)
        greet(down, sibling)

    @pl.when(s > 0)
    def _():
        greet(dp, s - 1)

    @pl.when(s < SECTIONS - 1)
    def _():
        greet(dp, s + 1)

    def native(r):
        return x * NZ + half * 4 + r

    for r in range(4):
        for d in (native(r), home(r)):
            @pl.when(d != dp)
            def _():
                greet(d, s)

    flat = tap_ref[...].reshape(8 * 16, GROUPS * KROWS).astype(F32)
    lane = lax.broadcasted_iota(jnp.int32, (8 * 16, 128), 1)
    for tile in range(KW // 128):
        first = tile * 128
        total = jnp.zeros((8 * 16, 128), F32)
        for g in range(first // KPAD, min((first + 127) // KPAD + 1, GROUPS)):
            lo = first - (KPAD - KROWS) * g
            start = min(max(lo // 128 * 128, 0), GROUPS * KROWS - 256)
            moved = pltpu.roll(flat[:, start:start + 256], (start - lo) % 256, 1)[:, :128]
            inside = jnp.logical_and(lane + first >= KPAD * g, lane + first < KPAD * g + KROWS)
            total = jnp.where(inside, moved, total)
        tap_pad[:, :, first:first + 128] = total.astype(BF16).reshape(8, 16, 128)

    def w_rows(zz):
        return wl.at[pl.ds(pl.multiple_of(zz * KPAD, 16), KPAD), :]

    wl[pl.ds(pl.multiple_of(z * KPAD, 16), KPAD), :] = jnp.concatenate(
        [lat_ref[...].astype(F32), jnp.zeros((KPAD - KROWS, CH), F32)], 0
    ).astype(BF16)

    need = jnp.where(even, 4 + 15, 4 + 16)
    for flag in (has_up, has_down, has_up, has_down, s > 0, s < SECTIONS - 1):
        need += flag.astype(jnp.int32)
    for r in range(4):
        need += (native(r) != dp).astype(jnp.int32) + (home(r) != dp).astype(jnp.int32)
    pl.semaphore_wait(barrier, need)

    def tap_cell(xx, j):
        return taps_all.at[xx, pl.ds(pl.multiple_of(j * 16, 16), 16), :]

    def tap_src(k, xx):
        return tap_pad.at[k, :, pl.ds(xx * XL, XL)]

    def tap_copy(k, xx):
        slot = (k % 2) * SECTIONS + s
        return remote(
            tap_src(k, xx), tap_cell(x, slot), tap_send.at[k, xx], tap_recv.at[x, slot], xx * NZ + z, k // 2 * 2
        )

    def tap_pass(xx):
        return remote(taps_all.at[xx], taps_all.at[xx], pass_send.at[xx], pass_recv.at[xx], dp, s + 1)

    def elsewhere(k, xx):
        return jnp.logical_or(xx != x, k // 2 * 2 != s)

    order = (0, -1, 1, -2, 2, -3, 3, -4)

    def ring_z(i):
        return (z + NZ + order[i]) % NZ

    def w_send_z(i, way):
        block = w_rows(ring_z(i))
        return remote(block, block, wz_send.at[way, i], w_recv.at[ring_z(i)], z_next if way == 0 else z_prev, s)

    def z_ways(i):
        ways = []
        if order[i] <= 0 and order[i] > -4:
            ways.append(0)
        if order[i] >= 0 and order[i] < 3:
            ways.append(1)
        return ways

    def w_step(i):
        if i > 0:
            local_wait(w_rows(ring_z(i)), w_recv.at[ring_z(i)])
        for way in z_ways(i):
            w_send_z(i, way).start()

    @pl.when(even)
    def _():
        w_step(0)

    def send_taps(ks):
        for k in ks:
            for xx in range(NX):
                @pl.when(elsewhere(k, xx))
                def _():
                    tap_copy(k, xx).start()

                @pl.when(jnp.logical_not(elsewhere(k, xx)))
                def _():
                    slot = (k % 2) * SECTIONS + s
                    pltpu.make_async_copy(tap_src(k, xx), tap_cell(x, slot), tap_recv.at[x, slot]).start()

    send_taps(range(2))

    def pass_turn(k):
        pl.semaphore_signal(gate_sem.at[k], inc=1, device_id={"dp": dp, "section": s + 1}, device_id_type=MESH)

    @pl.when(even)
    def _():
        for i in range(1, NZ // 2 + 1):
            w_step(i)
        pass_turn(2)
        send_taps(range(2, 8))
        for i in range(NZ // 2 + 1, NZ):
            w_step(i)
        pass_turn(0)

    @pl.when(jnp.logical_not(even))
    def _():
        pl.semaphore_wait(gate_sem.at[2], 1)
        send_taps(range(2, 8))
        pl.semaphore_wait(gate_sem.at[0], 1)
        for i in range(NZ):
            w_step(i)

    def oh_rows(r):
        return oh.at[pl.ds(pl.multiple_of(r * COLS, COLS), COLS), :]

    def oh_src(img):
        return oh_own.at[img // 2, pl.ds((img % 2) * COLS, COLS), :]

    def oh_copy(img):
        return remote(oh_src(img), oh_rows(z % 4), oh_send.at[img], oh_recv.at[z % 4], home(img), s)

    @pl.when(is_last)
    def _():
        sub = lax.broadcasted_iota(jnp.int32, (CPAD, 2 * COLS), 0)
        tile_of = lax.broadcasted_iota(jnp.int32, (CPAD, 2 * COLS), 1) // COLS
        for micro in range(2):
            count = counts_ref[0, micro]
            share = 1.0 / (count.astype(F32) * (COLS * GROUPS * 2))
            weight = jnp.where(tile_of < count, share, 0.0)
            hot = jnp.where(sub == labels_ref[micro:micro + 1, :], 1.0, 0.0)
            oh_own[micro] = jnp.where(sub == CPAD - 1, weight, hot).T.astype(BF16)
        for img in range(4):
            @pl.when(home(img) != dp)
            def _():
                oh_copy(img).start()

            @pl.when(home(img) == dp)
            def _():
                pltpu.make_async_copy(oh_src(img), oh_rows(z % 4), oh_recv.at[z % 4]).start()

    @pl.when(jnp.logical_not(has_up))
    def _():
        ext[0:COLS, :] = jnp.zeros((COLS, CH), BF16)

    @pl.when(jnp.logical_not(has_down))
    def _():
        ext[COLS + PIX:, :] = jnp.zeros((COLS, CH), BF16)

    @pl.when(even)
    def _():
        for xx in range(NX):
            for j in range(2 * SECTIONS):
                local_wait(tap_cell(xx, j), tap_recv.at[xx, j])
            tap_pass(xx).start()

    @pl.when(jnp.logical_not(even))
    def _():
        for xx in range(NX):
            local_wait(taps_all.at[xx], pass_recv.at[xx])

    first_rows, last_rows = pl.ds(0, FARROWS), pl.ds(FARROWS, FARROWS)
    half_rows = (first_rows, last_rows)

    def far_copy(way):
        return remote(
            lat_send.at[2, half_rows[way]], lat_far.at[way], lf_send.at[way], lf_recv.at[way],
            right if way == 0 else left, s,
        )

    def near_copy(way, part):
        return remote(
            lat_send.at[way, half_rows[part]], lat_near.at[way, half_rows[part]],
            ln_send.at[way, part], ln_recv.at[way, part], right if way == 0 else left, s,
        )

    lat_send[2] = nn(taps_all[x_far], wl[...]).astype(BF16)

    @pl.when(jnp.logical_not(even))
    def _():
        pl.semaphore_wait(gate_sem.at[1], 1)

    for way in range(2):
        far_copy(way).start()
    for way in range(2):
        acc[way] = nn(taps_all[x_right if way == 0 else x_left], wl[...])
        rows = half_rows[1 - way]
        lat_send[way, rows] = acc[way, rows].astype(BF16)
        near_copy(way, 1 - way).start()
    acc[2] = nn(taps_all[x], wl[...])
    for way in range(2):
        rows = half_rows[way]
        local_wait(lat_far.at[way], lf_recv.at[way])
        lat_send[way, rows] = (acc[way, rows] + lat_far[way].astype(F32)).astype(BF16)
        near_copy(way, way).start()
    for part in range(2):
        rows = half_rows[part]
        for way in (1 - part, part):
            local_wait(lat_near.at[way, rows], ln_recv.at[way, part])
        lat_nat[rows] = (
            acc[2, rows] + lat_near[0, rows].astype(F32) + lat_near[1, rows].astype(F32)
        ).astype(BF16)

    @pl.when(even)
    def _():
        pass_turn(1)

    def band(ref, j):
        return ref.at[pl.ds(pl.multiple_of(j * COLS, COLS), COLS), :]

    def lat_copy(img):
        return remote(band(lat_nat, img), band(lat_img, z % 4), lz_send.at[img], lz_recv.at[z % 4], home(img), s)

    for img in range(4):
        @pl.when(home(img) != dp)
        def _():
            lat_copy(img).start()

        @pl.when(home(img) == dp)
        def _():
            pltpu.make_async_copy(band(lat_nat, img), band(lat_img, z % 4), lz_recv.at[z % 4]).start()

    for r in range(4):
        local_wait(band(lat_img, r), lz_recv.at[r])

    def lat_up():
        return remote(band(lat_img, 0), lat_halo.at[1], lh_send.at[0], lh_recv.at[1], up, s)

    def lat_down():
        return remote(band(lat_img, ROWS - 1), lat_halo.at[0], lh_send.at[1], lh_recv.at[0], down, s)

    @pl.when(jnp.logical_and(has_up, jnp.logical_not(even)))
    def _():
        lat_up().start()

    @pl.when(jnp.logical_and(has_down, jnp.logical_not(even)))
    def _():
        lat_down().start()

    w_copy.wait()

    def lanes(c):
        return pl.ds(c * CK, CK)

    def x_copy(c):
        return pltpu.make_async_remote_copy(
            src_ref=xout.at[:, lanes(c)], dst_ref=xin.at[:, lanes(c)],
            send_sem=x_send.at[c], recv_sem=x_recv.at[c],
            device_id={"dp": dp, "section": s + 1}, device_id_type=MESH,
        )

    def halo_up(c):
        return pltpu.make_async_remote_copy(
            src_ref=ext.at[pl.ds(COLS, COLS), lanes(c)], dst_ref=ext.at[pl.ds(COLS + PIX, COLS), lanes(c)],
            send_sem=halo_send.at[0, c], recv_sem=halo_recv.at[1, c],
            device_id={"dp": up, "section": s}, device_id_type=MESH,
        )

    def halo_down(c):
        return pltpu.make_async_remote_copy(
            src_ref=ext.at[pl.ds(PIX, COLS), lanes(c)], dst_ref=ext.at[pl.ds(0, COLS), lanes(c)],
            send_sem=halo_send.at[1, c], recv_sem=halo_recv.at[0, c],
            device_id={"dp": down, "section": s}, device_id_type=MESH,
        )

    def edge_up(c):
        return remote(
            xout.at[pl.ds(0, COLS), lanes(c)], x_halo.at[1, :, lanes(c)],
            xh_send.at[0, c], xh_recv.at[1, c], up, s + 1,
        )

    def edge_down(c):
        return remote(
            xout.at[pl.ds(PIX - COLS, COLS), lanes(c)], x_halo.at[0, :, lanes(c)],
            xh_send.at[1, c], xh_recv.at[0, c], down, s + 1,
        )

    def take_edges(c):
        cols = slice(c * CK, (c + 1) * CK)
        for side, flag, rows in ((0, has_up, slice(0, COLS)), (1, has_down, slice(COLS + PIX, 2 * COLS + PIX))):
            @pl.when(flag)
            def _():
                local_wait(x_halo.at[side, :, lanes(c)], xh_recv.at[side, c])
                ext[rows, cols] = (
                    x_halo[side, :, cols].astype(F32) + lat_halo[side, :, cols].astype(F32)
                ).astype(BF16)

    def take_x(c):
        cols = slice(c * CK, (c + 1) * CK)

        @pl.when(is_first)
        def _():
            ext[COLS:COLS + PIX, cols] = lat_img[:, cols]

        @pl.when(s > 0)
        def _():
            local_wait(xin.at[:, lanes(c)], x_recv.at[c])
            ext[COLS:COLS + PIX, cols] = (xin[:, cols].astype(F32) + lat_img[:, cols].astype(F32)).astype(BF16)

        @pl.when(jnp.logical_and(has_up, even))
        def _():
            halo_up(c).start()

        @pl.when(jnp.logical_and(has_down, even))
        def _():
            halo_down(c).start()

    def wait_halo(c):
        @pl.when(has_up)
        def _():
            local_wait(ext.at[pl.ds(0, COLS), lanes(c)], halo_recv.at[0, c])

        @pl.when(has_down)
        def _():
            local_wait(ext.at[pl.ds(COLS + PIX, COLS), lanes(c)], halo_recv.at[1, c])

    def conv_part(c, dr, dc, ncols):
        rows = (1 + dr) * COLS
        return nn(
            ext[rows:rows + PIX, c * CK:(c + 1) * CK],
            w[(dr + 1) * 3 + dc + 1, c * CK:(c + 1) * CK, ncols],
        )

    every = slice(0, CH)

    def conv_inner(c, start):
        for dc in (-1, 0, 1):
            term = conv_part(c, 0, dc, every)
            if start:
                acc[dc + 1] = term
            else:
                acc[dc + 1] += term

    def conv_outer(c):
        for dc in (-1, 0, 1):
            acc[dc + 1] += conv_part(c, -1, dc, every) + conv_part(c, 1, dc, every)

    col = lax.broadcasted_iota(jnp.int32, (PIX, CK), 0) % COLS

    def before(v):
        return jnp.where(col == 0, 0.0, pltpu.roll(v, 1, 0))

    def after(v):
        return jnp.where(col == COLS - 1, 0.0, pltpu.roll(v, PIX - 1, 0))

    def conv_finish(n, chunks, direct):
        ncols = slice(n * CK, (n + 1) * CK)
        parts = []
        for dc in (-1, 0, 1):
            part = acc[dc + 1, :, ncols]
            for c in chunks:
                part += conv_part(c, -1, dc, ncols) + conv_part(c, 1, dc, ncols)
            parts.append(part)
        pre = before(parts[0]) + parts[1] + after(parts[2])
        sig = 1.0 / (1.0 + jnp.exp(-pre))
        xout[:, ncols] = (pre * sig).astype(BF16)

        @pl.when(s < SECTIONS - 1)
        def _():
            x_copy(n).start()

        if direct:
            @pl.when(has_up)
            def _():
                edge_up(n).start()

            @pl.when(has_down)
            def _():
                edge_down(n).start()

        dsilu[:, ncols] = sig * (1.0 + pre * (1.0 - sig))

    @pl.when(even)
    def _():
        take_x(0)
        conv_inner(0, True)
        take_x(1)
        conv_inner(1, False)
        wait_halo(0)
        conv_outer(0)
        take_x(2)
        conv_inner(2, False)
        wait_halo(1)
        conv_outer(1)
        wait_halo(2)
        for n in range(NCH):
            conv_finish(n, (2,), True)

    @pl.when(jnp.logical_not(even))
    def _():
        for c in range(NCH):
            take_x(c)
        for c in range(NCH):
            conv_inner(c, c == 0)

        @pl.when(has_up)
        def _():
            local_wait(lat_halo.at[0], lh_recv.at[0])

        @pl.when(has_down)
        def _():
            local_wait(lat_halo.at[1], lh_recv.at[1])

        for c in range(NCH):
            take_edges(c)
        for n in range(NCH):
            conv_finish(n, range(NCH), False)

    def gather_copy(buf, kind, way):
        return remote(
            buf.at[x], buf.at[x], a_send.at[kind, way], a_recv.at[kind, way], right if way == 0 else left, s
        )

    def gather_far(buf, kind, way):
        rows = buf.shape[1] // 2
        block = buf.at[x_left if way == 0 else x_right, pl.ds(way * rows, rows), :]
        return remote(
            block, block, a_send.at[kind, 2 + way], a_recv.at[kind, 2 + way], right if way == 0 else left, s
        )

    def gather_start(buf, kind):
        for way in range(2):
            gather_copy(buf, kind, way).start()

    def gather_forward(buf, kind):
        for way in range(2):
            local_wait(buf.at[x_left if way == 0 else x_right], a_recv.at[kind, way])
            gather_far(buf, kind, way).start()

    def gather_finish(buf, kind):
        rows = buf.shape[1] // 2
        for way in range(2):
            local_wait(buf.at[x_far, pl.ds(way * rows, rows), :], a_recv.at[kind, 2 + way])

    def gather_sent(buf, kind):
        for way in range(2):
            gather_copy(buf, kind, way).wait_send()
            gather_far(buf, kind, way).wait_send()

    def early_start():
        ext_all[x] = ext[...]
        gather_start(ext_all, 2)

    def early_finish():
        gather_finish(ext_all, 2)

        @pl.loop(0, NX)
        def _(src):
            lanes_of = pl.ds(pl.multiple_of(src * PIX, PIX), PIX)
            for dr in range(3):
                cols_t[dr, :, lanes_of] = ext_all[src, dr * COLS:dr * COLS + PIX, :].T
            taps_t[:, lanes_of] = taps_all[src].T

    @pl.when(jnp.logical_and(s < 6, s % 2 == 1))
    def _():
        pl.semaphore_signal(early_sem, inc=1, device_id={"dp": dp, "section": s - 1}, device_id_type=MESH)

    @pl.when(jnp.logical_and(s < 6, s % 2 == 0))
    def _():
        pl.semaphore_wait(early_sem, 1)

    @pl.when(s < 6)
    def _():
        early_start()

    @pl.when(s < 4)
    def _():
        gather_forward(ext_all, 2)
        early_finish()

    @pl.when(is_last)
    def _():
        for r in range(4):
            local_wait(oh_rows(r), oh_recv.at[r])
        cls_copy.wait()
        logits = nt(xout[...], cls_ref[...])
        spot = lax.broadcasted_iota(jnp.int32, (PIX, CPAD), 1)
        expo = jnp.exp(logits)
        probs = expo / jnp.sum(expo, axis=-1, keepdims=True)
        marks = oh[...].astype(F32)
        weight = jnp.sum(jnp.where(spot == CPAD - 1, marks, 0.0), axis=-1, keepdims=True)
        grad_logits = ((probs - marks[:, :CLASSES]) * weight).astype(BF16)
        gx[...] = nn(grad_logits, cls_ref[...])

    def g_copy(c):
        return pltpu.make_async_remote_copy(
            src_ref=g_out.at[:, lanes(c)], dst_ref=gin.at[:, lanes(c)],
            send_sem=g_send.at[c], recv_sem=g_recv.at[c],
            device_id={"dp": dp, "section": s - 1}, device_id_type=MESH,
        )

    def rim_up(c):
        return pltpu.make_async_remote_copy(
            src_ref=rim_out.at[0, :, lanes(c)], dst_ref=rim_in.at[1, :, lanes(c)],
            send_sem=rim_send.at[0, c], recv_sem=rim_recv.at[1, c],
            device_id={"dp": up, "section": s}, device_id_type=MESH,
        )

    def rim_down(c):
        return pltpu.make_async_remote_copy(
            src_ref=rim_out.at[1, :, lanes(c)], dst_ref=rim_in.at[0, :, lanes(c)],
            send_sem=rim_send.at[1, c], recv_sem=rim_recv.at[0, c],
            device_id={"dp": down, "section": s}, device_id_type=MESH,
        )

    def take_g(c):
        cols = slice(c * CK, (c + 1) * CK)

        @pl.when(s < SECTIONS - 1)
        def _():
            local_wait(gin.at[:, lanes(c)], g_recv.at[c])
            gx[:, cols] = gin[:, cols].astype(F32)

        for side, flag, rows in ((0, has_up, slice(0, COLS)), (1, has_down, slice(PIX - COLS, PIX))):
            @pl.when(jnp.logical_and(flag, even))
            def _():
                local_wait(g_rim.at[side, :, lanes(c)], gr_recv.at[side, c])
                gx[rows, cols] += g_rim[side, :, cols].astype(F32)

        grad_pre = (gx[:, cols] * dsilu[:, cols]).astype(BF16).astype(F32)
        gpv[0, :, cols] = after(grad_pre).astype(BF16)
        gpv[1, :, cols] = grad_pre.astype(BF16)
        gp_all[x, :, cols] = grad_pre.astype(BF16)
        gpv[2, :, cols] = before(grad_pre).astype(BF16)

    def back_part(c, dr, krows):
        total = None
        for dc in (-1, 0, 1):
            term = nt(
                gpv[dc + 1, :, c * CK:(c + 1) * CK],
                w[(dr + 1) * 3 + dc + 1, krows, c * CK:(c + 1) * CK],
            )
            total = term if total is None else total + term
        return total

    def rim_direct_up(c):
        return remote(
            rim_out.at[0, :, lanes(c)], g_rim.at[1, :, lanes(c)], gr_send.at[0, c], gr_recv.at[1, c], up, s - 1
        )

    def rim_direct_down(c):
        return remote(
            rim_out.at[1, :, lanes(c)], g_rim.at[0, :, lanes(c)], gr_send.at[1, c], gr_recv.at[0, c], down, s - 1
        )

    def send_rims(n, upward, downward):
        @pl.when(has_up)
        def _():
            upward(n).start()

        @pl.when(has_down)
        def _():
            downward(n).start()

    def back_rims(n, chunks, start):
        ncols = slice(n * CK, (n + 1) * CK)
        for side, dr in ((0, -1), (2, 1)):
            total = None if start else acc[side, :, ncols]
            for c in chunks:
                term = back_part(c, dr, ncols)
                total = term if total is None else total + term
            acc[side, :, ncols] = total
            if dr < 0:
                rim_out[0, :, ncols] = total[0:COLS].astype(BF16)
            else:
                rim_out[1, :, ncols] = total[PIX - COLS:].astype(BF16)

    def back_inner(n, chunks, start):
        ncols = slice(n * CK, (n + 1) * CK)
        total = None if start else acc[1, :, ncols]
        for c in chunks:
            term = back_part(c, 0, ncols)
            total = term if total is None else total + term
        acc[1, :, ncols] = total
        acc[1, 0:PIX - COLS, ncols] += acc[0, COLS:, ncols]
        acc[1, COLS:, ncols] += acc[2, 0:PIX - COLS, ncols]

    def add_rims(n):
        ncols = slice(n * CK, (n + 1) * CK)

        @pl.when(has_up)
        def _():
            local_wait(rim_in.at[0, :, lanes(n)], rim_recv.at[0, n])
            acc[1, 0:COLS, ncols] += rim_in[0, :, ncols].astype(F32)

        @pl.when(has_down)
        def _():
            local_wait(rim_in.at[1, :, lanes(n)], rim_recv.at[1, n])
            acc[1, PIX - COLS:, ncols] += rim_in[1, :, ncols].astype(F32)

        gs_img[:, ncols] = acc[1, :, ncols].astype(BF16)

    def send_g(n):
        ncols = slice(n * CK, (n + 1) * CK)
        g_out[:, ncols] = acc[1, :, ncols].astype(BF16)
        g_copy(n).start()

    @pl.when(jnp.logical_not(even))
    def _():
        take_g(0)
        for dr in (-1, 0, 1):
            acc[dr + 1] = back_part(0, dr, every)
        take_g(1)
        for dr in (-1, 0, 1):
            acc[dr + 1] += back_part(1, dr, every)
        take_g(2)
        for n in range(NCH):
            back_rims(n, (2,), False)
            send_rims(n, rim_direct_up, rim_direct_down)
            back_inner(n, (2,), False)
            send_g(n)
        for n in range(NCH):
            send_rims(n, rim_up, rim_down)

        @pl.when(s == 1)
        def _():
            gather_start(gp_all, 0)

        for n in range(NCH):
            add_rims(n)

        @pl.when(s > 1)
        def _():
            pl.semaphore_wait(gate_sem.at[3], 1)
            gather_start(gp_all, 0)

    @pl.when(even)
    def _():
        def finish(n):
            back_inner(n, chunks, True)
            add_rims(n)

            @pl.when(s > 0)
            def _():
                send_g(n)

        for c in range(NCH):
            take_g(c)

        @pl.when(is_first)
        def _():
            gather_start(gp_all, 0)

        chunks = range(NCH)
        back_rims(0, chunks, True)
        send_rims(0, rim_up, rim_down)
        back_rims(1, chunks, True)
        send_rims(1, rim_up, rim_down)
        finish(0)
        back_rims(2, chunks, True)
        send_rims(2, rim_up, rim_down)
        finish(1)
        finish(2)

        @pl.when(s > 0)
        def _():
            pass_turn(3)

    def gz_copy(r):
        return remote(
            band(gs_img, r), band(gs_all.at[x], image), gz_send.at[r], gz_recv.at[image], native(r), s
        )

    for r in range(4):
        @pl.when(native(r) != dp)
        def _():
            gz_copy(r).start()

        @pl.when(native(r) == dp)
        def _():
            pltpu.make_async_copy(band(gs_img, r), band(gs_all.at[x], image), gz_recv.at[image]).start()

    @pl.when(jnp.logical_and(even, s > 0))
    def _():
        gather_start(gp_all, 0)

    @pl.when(s >= 6)
    def _():
        early_start()

    gather_forward(gp_all, 0)

    @pl.when(s >= 4)
    def _():
        gather_forward(ext_all, 2)

    whole_col = lax.broadcasted_iota(jnp.int32, (PIX, CH), 0) % COLS

    def spread(src):
        rows = pl.ds(pl.multiple_of(src * PIX, PIX), PIX)
        value = gp_all[src].astype(F32)
        gpv_all[0, rows, :] = jnp.where(whole_col == COLS - 1, 0.0, pltpu.roll(value, PIX - 1, 0)).astype(BF16)
        gpv_all[1, rows, :] = gp_all[src]
        gpv_all[2, rows, :] = jnp.where(whole_col == 0, 0.0, pltpu.roll(value, 1, 0)).astype(BF16)

    spread(x)
    spread(x_left)
    spread(x_right)
    gather_finish(gp_all, 0)
    for img in range(4):
        local_wait(band(gs_all.at[x], img), gz_recv.at[img])
    gather_start(gs_all, 1)
    spread(x_far)

    @pl.when(s >= 4)
    def _():
        early_finish()

    def conv_unit(u):
        unit = 9 * x + u
        o = unit // 4
        chans = pl.ds(pl.multiple_of((unit % 4) * UNIT, UNIT), UNIT)
        part_c[pl.ds(pl.multiple_of(u * UNIT, UNIT), UNIT), :] = nn(cols_t[o // 3, chans, :], gpv_all[o % 3])

    def conv_slice(zz):
        @pl.loop(0, 2)
        def _(k):
            conv_unit(zz + k)

    def slice_at(way, t):
        return (z + NZ - 1 - t) % NZ if way == 0 else (z + 1 + t) % NZ

    def own_rows(part, rows, way, t):
        at = pl.ds(pl.multiple_of(slice_at(way, t) * rows, 8), rows)
        return part[at, way * HALF:(way + 1) * HALF]

    def hop(ring, send, recv, way, t):
        return pltpu.make_async_remote_copy(
            src_ref=ring.at[way, t], dst_ref=ring.at[way, t + 1],
            send_sem=send.at[way, t], recv_sem=recv.at[way, t],
            device_id={"dp": z_next if way == 0 else z_prev, "section": s}, device_id_type=MESH,
        )

    conv_ring = (ring_c, rc_send, rc_recv)
    lat_ring = (ring_l, rl_send, rl_recv)
    def ring_start(ring, part, rows):
        for way in range(2):
            ring[0][way, 0] = own_rows(part, rows, way, 0).astype(BF16)
            hop(*ring, way, 0).start()

    def ring_step(ring, part, rows, out, t):
        buf = ring[0]
        for way in range(2):
            local_wait(buf.at[way, t + 1], ring[2].at[way, t])
            total = buf[way, t + 1].astype(F32) + own_rows(part, rows, way, t + 1)
            if t < NZ - 2:
                buf[way, t + 1] = total.astype(BF16)
                hop(*ring, way, t + 1).start()
            else:
                out[:, way * HALF:(way + 1) * HALF] = total

    def conv_step(t):
        ring_step(conv_ring, part_c, CROWS, conv_out, t)

    def lat_step(t):
        ring_step(lat_ring, part_l, KPAD, lat_out, t)

    @pl.loop(0, 2)
    def _(k):
        conv_slice((z + 1 + k * (NZ - 2)) % NZ)

    ring_start(conv_ring, part_c, CROWS)

    @pl.loop(0, 2)
    def _(k):
        conv_slice((z + 2 + k * (NZ - 4)) % NZ)

    gather_forward(gs_all, 1)
    conv_step(0)

    @pl.loop(0, 2)
    def _(k):
        conv_slice((z + 3 + k * (NZ - 6)) % NZ)

    gather_finish(gs_all, 1)
    part_l[...] = nn(taps_t[...], gs_all[...].reshape(WIDE, CH))
    ring_start(lat_ring, part_l, KPAD)
    conv_step(1)

    @pl.loop(0, 2)
    def _(k):
        conv_slice((z + 4 * k) % NZ)

    lat_step(0)
    for t in range(2, NZ - 1):
        conv_step(t)
        lat_step(t - 1)
    lat_step(NZ - 2)

    for k in range(8):
        for xx in range(NX):
            @pl.when(elsewhere(k, xx))
            def _():
                tap_copy(k, xx).wait_send()

    @pl.when(even)
    def _():
        for xx in range(NX):
            tap_pass(xx).wait_send()

    for i in range(NZ):
        for way in z_ways(i):
            w_send_z(i, way).wait_send()
    for way in range(2):
        far_copy(way).wait_send()
        for part in range(2):
            near_copy(way, part).wait_send()
    for r in range(4):
        @pl.when(home(r) != dp)
        def _():
            lat_copy(r).wait_send()

    @pl.when(is_last)
    def _():
        for img in range(4):
            @pl.when(home(img) != dp)
            def _():
                oh_copy(img).wait_send()

    for c in range(NCH):
        @pl.when(s < SECTIONS - 1)
        def _():
            x_copy(c).wait_send()

        @pl.when(s > 0)
        def _():
            g_copy(c).wait_send()

        @pl.when(has_up)
        def _():
            rim_up(c).wait_send()

        @pl.when(has_down)
        def _():
            rim_down(c).wait_send()

        @pl.when(jnp.logical_and(has_up, even))
        def _():
            halo_up(c).wait_send()
            edge_up(c).wait_send()

        @pl.when(jnp.logical_and(has_down, even))
        def _():
            halo_down(c).wait_send()
            edge_down(c).wait_send()

        @pl.when(jnp.logical_and(has_up, jnp.logical_not(even)))
        def _():
            rim_direct_up(c).wait_send()

        @pl.when(jnp.logical_and(has_down, jnp.logical_not(even)))
        def _():
            rim_direct_down(c).wait_send()

    @pl.when(jnp.logical_and(has_up, jnp.logical_not(even)))
    def _():
        lat_up().wait_send()

    @pl.when(jnp.logical_and(has_down, jnp.logical_not(even)))
    def _():
        lat_down().wait_send()

    for kind, buf in enumerate((gp_all, gs_all, ext_all)):
        gather_sent(buf, kind)
    for r in range(4):
        @pl.when(native(r) != dp)
        def _():
            gz_copy(r).wait_send()

    for way in range(2):
        for t in range(NZ - 1):
            hop(*conv_ring, way, t).wait_send()
            hop(*lat_ring, way, t).wait_send()


def head_call(taps, lat, w, cls, counts, labels):
    dma = pltpu.SemaphoreType.DMA
    hbm = pl.BlockSpec(memory_space=pl.ANY)
    vmem = pl.BlockSpec(memory_space=pltpu.VMEM)
    smem = pl.BlockSpec(memory_space=pltpu.SMEM)
    return pl.pallas_call(
        head_kernel,
        out_shape=(
            jax.ShapeDtypeStruct((CROWS, CH), F32),
            jax.ShapeDtypeStruct((KPAD, CH), F32),
        ),
        in_specs=[vmem, vmem, hbm, hbm, smem, vmem],
        out_specs=(vmem, vmem),
        scratch_shapes=[
            pltpu.VMEM((CLASSES, CH), BF16),
            pltpu.VMEM((8, 16, KW), BF16),
            pltpu.VMEM((XL, CH), BF16),
            pltpu.VMEM((9, CH, CH), BF16),
            pltpu.VMEM((PIX, CH), F32),
            pltpu.VMEM((3, PIX, CH), BF16),
            pltpu.VMEM((2, FARROWS, CH), BF16),
            pltpu.VMEM((2, PIX, CH), BF16),
            pltpu.VMEM((PIX, CH), BF16),
            pltpu.VMEM((PIX, CH), BF16),
            pltpu.VMEM((PIX + 2 * COLS, CH), BF16),
            pltpu.VMEM((PIX, CH), BF16),
            pltpu.VMEM((PIX, CH), BF16),
            pltpu.VMEM((PIX, CH), BF16),
            pltpu.VMEM((PIX, CH), F32),
            pltpu.VMEM((3, PIX, CH), F32),
            pltpu.VMEM((3, PIX, CH), BF16),
            pltpu.VMEM((2, COLS, CH), BF16),
            pltpu.VMEM((2, COLS, CH), BF16),
            pltpu.VMEM((2, 2 * COLS, CPAD), BF16),
            pltpu.VMEM((PIX, CPAD), BF16),
            pltpu.VMEM((2, COLS, CH), BF16),
            pltpu.VMEM((2, COLS, CH), BF16),
            pltpu.VMEM((PIX, CH), BF16),
            pltpu.VMEM((2, COLS, CH), BF16),
            pltpu.VMEM((NX, PIX + 2 * COLS, CH), BF16),
            pltpu.VMEM((NX, PIX, XL), BF16),
            pltpu.VMEM((PIX, CH), BF16),
            pltpu.VMEM((NX, PIX, CH), BF16),
            pltpu.VMEM((NX, PIX, CH), BF16),
            pltpu.VMEM((3, WIDE, CH), BF16),
            pltpu.VMEM((3, CH, WIDE), BF16),
            pltpu.VMEM((XL, WIDE), BF16),
            pltpu.VMEM((XC, CH), F32),
            pltpu.VMEM((XL, CH), F32),
            pltpu.VMEM((2, NZ, CROWS, HALF), BF16),
            pltpu.VMEM((2, NZ, KPAD, HALF), BF16),
            pltpu.SemaphoreType.REGULAR((4,)),
            dma((2,)),
            dma((8, NX)),
            dma((NX, 2 * SECTIONS)),
            dma((NX,)),
            dma((NX,)),
            dma((2, NZ)),
            dma((NZ,)),
            dma((2,)),
            dma((2,)),
            dma((2, 2)),
            dma((2, 2)),
            dma((4,)),
            dma((4,)),
            dma((4,)),
            dma((4,)),
            dma((NCH,)),
            dma((NCH,)),
            dma((2, NCH)),
            dma((2, NCH)),
            dma((NCH,)),
            dma((NCH,)),
            dma((2, NCH)),
            dma((2, NCH)),
            dma((2,)),
            dma((2,)),
            dma((2, NCH)),
            dma((2, NCH)),
            dma((2, NCH)),
            dma((2, NCH)),
            pltpu.SemaphoreType.REGULAR,
            dma((4,)),
            dma((4,)),
            dma((3, 4)),
            dma((3, 4)),
            dma((2, NZ - 1)),
            dma((2, NZ - 1)),
            dma((2, NZ - 1)),
            dma((2, NZ - 1)),
        ],
        compiler_params=pltpu.CompilerParams(
            collective_id=0, has_side_effects=True, vmem_limit_bytes=62 << 20
        ),
    )(taps, lat, w, cls, counts, labels)


def on_device(tap_maps, lateral_weight, conv_weight, classifier, tile_counts, labels):
    levels, micros, here, width = tap_maps.shape
    taps = tap_maps.reshape(levels * micros, here, width)
    conv_grad, lateral_grad = head_call(
        taps, lateral_weight[0], conv_weight.reshape(9, CH, CH), classifier.T, tile_counts, labels
    )
    return (conv_grad[None], lateral_grad[None, :KROWS])


def solution(mesh):
    placed = (
        P(None, None, ("dp", "section"), None),
        P("section", "dp", None),
        P("section", None, None),
        P(),
        P("dp", None),
        P(None, "dp"),
    )
    return jax.shard_map(
        on_device,
        mesh=mesh,
        in_specs=placed,
        out_specs=(P("section", "dp", None), P("section", "dp", None)),
        check_vma=False,
    )
```

```python
import jax
import jax.numpy as jnp
from jax import lax
from jax.experimental import pallas as pl
from jax.experimental.pallas import tpu as pltpu
from jax.sharding import PartitionSpec as P

MESH = pl.DeviceIdType.MESH
F32 = jnp.float32
BF16 = jnp.bfloat16
NZ = 8
NX = 4
COLS = 64
ROWS = 4
PIX = ROWS * COLS
CH = 768
CK = 256
NCH = CH // CK
KROWS = 100
KPAD = 112
GROUPS = NX * NZ
KW = KPAD * GROUPS
SECTIONS = 8
WIDE = NX * PIX
CROWS = 9 * CH // GROUPS
XC, XL = CROWS * NZ, KPAD * NZ
UNIT = XC // 9
HALF = CH // 2
FARROWS = PIX // 2
CLASSES = 150
CPAD = 256


def nt(a, b):
    return lax.dot_general(a, b, (((1,), (1,)), ((), ())), preferred_element_type=F32)


def tn(a, b):
    return lax.dot_general(a, b, (((0,), (0,)), ((), ())), preferred_element_type=F32)


def nn(a, b):
    return jnp.dot(a, b, preferred_element_type=F32)


def head_kernel(
    tap_ref, lat_ref, w_hbm, cls_hbm, counts_ref, labels_ref, conv_out, lat_out,
    cls_ref, tap_pad, wl, w, gx, lat_send, lat_far, lat_near, lat_nat, lat_img,
    ext, xin, xout, gin, dsilu, acc, gpv, rim_out, rim_in, oh_own, oh,
    lat_halo, x_halo, g_out, g_rim,
    ext_all, taps_all, gs_img, gp_all, gs_all, gpv_all, cols_t, taps_t, part_c, part_l, ring_c, ring_l,
    gate_sem, local_sem, tap_send, tap_recv, pass_send, pass_recv, wz_send, w_recv,
    lf_send, lf_recv, ln_send, ln_recv, lz_send, lz_recv, oh_send, oh_recv,
    x_send, x_recv, halo_send, halo_recv, g_send, g_recv, rim_send, rim_recv,
    lh_send, lh_recv, xh_send, xh_recv, gr_send, gr_recv,
    early_sem, gz_send, gz_recv, a_send, a_recv, rc_send, rc_recv, rl_send, rl_recv,
):
    dp = lax.axis_index("dp")
    s = lax.axis_index("section")
    x, z = dp // NZ, dp % NZ
    odd = x % 2
    half = (z % 2 + odd) % 2
    image = z // 2
    has_up = jnp.logical_not(jnp.logical_and(half == 0, x == 0))
    has_down = jnp.logical_not(jnp.logical_and(half == 1, x == NX - 1))
    pair = dp + 1 - 2 * (z % 2)
    up = jnp.where(half == 1, pair, dp - NZ)
    down = jnp.where(half == 0, pair, dp + NZ)
    src_half = z // 4
    is_first, is_last = s == 0, s == SECTIONS - 1
    even = s % 2 == 0
    sibling = s + 1 - 2 * (s % 2)
    z_next, z_prev = x * NZ + (z + 1) % NZ, x * NZ + (z + NZ - 1) % NZ
    x_left, x_right, x_far = (x + NX - 1) % NX, (x + 1) % NX, (x + 2) % NX
    left, right = x_left * NZ + z, x_right * NZ + z

    def home(img):
        return x * NZ + 2 * img + (src_half + odd) % 2

    def remote(src, dst, send, recv, d, sec):
        return pltpu.make_async_remote_copy(
            src_ref=src, dst_ref=dst, send_sem=send, recv_sem=recv,
            device_id={"dp": d, "section": sec}, device_id_type=MESH,
        )

    def local_wait(ref, sem):
        pltpu.make_async_copy(ref, ref, sem).wait()

    w_copy = pltpu.make_async_copy(w_hbm, w, local_sem.at[0])
    w_copy.start()
    cls_copy = pltpu.make_async_copy(cls_hbm, cls_ref, local_sem.at[1])

    @pl.when(is_last)
    def _():
        cls_copy.start()

    barrier = pltpu.get_barrier_semaphore()

    def greet(d, sec):
        pl.semaphore_signal(barrier, inc=1, device_id={"dp": d, "section": sec}, device_id_type=MESH)

    @pl.when(even)
    def _():
        for xx in range(NX):
            for sec in range(SECTIONS):
                @pl.when(jnp.logical_or(xx != x, sec != s))
                def _():
                    greet(xx * NZ + z, sec)

    for d in (left, right, z_next, z_prev):
        greet(d, s)

    @pl.when(has_up)
    def _():
        greet(up, s)
        greet(up, sibling)

    @pl.when(has_down)
    def _():
        greet(down, s)
        greet(down, sibling)

    @pl.when(s > 0)
    def _():
        greet(dp, s - 1)

    @pl.when(s < SECTIONS - 1)
    def _():
        greet(dp, s + 1)

    def native(r):
        return x * NZ + half * 4 + r

    for r in range(4):
        for d in (native(r), home(r)):
            @pl.when(d != dp)
            def _():
                greet(d, s)

    def pad_taps(k0, k1):
        rows = (k1 - k0) * 16
        flat = tap_ref[k0:k1].reshape(rows, GROUPS * KROWS).astype(F32)
        lane = lax.broadcasted_iota(jnp.int32, (rows, 128), 1)
        for tile in range(KW // 128):
            first = tile * 128
            total = jnp.zeros((rows, 128), F32)
            for g in range(first // KPAD, min((first + 127) // KPAD + 1, GROUPS)):
                lo = first - (KPAD - KROWS) * g
                start = min(max(lo // 128 * 128, 0), GROUPS * KROWS - 256)
                moved = pltpu.roll(flat[:, start:start + 256], (start - lo) % 256, 1)[:, :128]
                inside = jnp.logical_and(lane + first >= KPAD * g, lane + first < KPAD * g + KROWS)
                total = jnp.where(inside, moved, total)
            tap_pad[k0:k1, :, first:first + 128] = total.astype(BF16).reshape(k1 - k0, 16, 128)

    pad_taps(0, 2)

    def w_rows(zz):
        return wl.at[pl.ds(pl.multiple_of(zz * KPAD, 16), KPAD), :]

    wl[pl.ds(pl.multiple_of(z * KPAD, 16), KPAD), :] = jnp.concatenate(
        [lat_ref[...].astype(F32), jnp.zeros((KPAD - KROWS, CH), F32)], 0
    ).astype(BF16)

    need = jnp.where(even, 4 + 15, 4 + 16)
    for flag in (has_up, has_down, has_up, has_down, s > 0, s < SECTIONS - 1):
        need += flag.astype(jnp.int32)
    for r in range(4):
        need += (native(r) != dp).astype(jnp.int32) + (home(r) != dp).astype(jnp.int32)
    pl.semaphore_wait(barrier, need)

    def tap_cell(xx, j):
        return taps_all.at[xx, pl.ds(pl.multiple_of(j * 16, 16), 16), :]

    def tap_src(k, xx):
        return tap_pad.at[k, :, pl.ds(xx * XL, XL)]

    def tap_copy(k, xx):
        slot = (k % 2) * SECTIONS + s
        return remote(
            tap_src(k, xx), tap_cell(x, slot), tap_send.at[k, xx], tap_recv.at[x, slot], xx * NZ + z, k // 2 * 2
        )

    def tap_pass(xx):
        return remote(taps_all.at[xx], taps_all.at[xx], pass_send.at[xx], pass_recv.at[xx], dp, s + 1)

    def elsewhere(k, xx):
        return jnp.logical_or(xx != x, k // 2 * 2 != s)

    order = (0, -1, 1, -2, 2, -3, 3, -4)

    def ring_z(i):
        return (z + NZ + order[i]) % NZ

    def w_send_z(i, way):
        block = w_rows(ring_z(i))
        return remote(block, block, wz_send.at[way, i], w_recv.at[ring_z(i)], z_next if way == 0 else z_prev, s)

    def z_ways(i):
        ways = []
        if order[i] <= 0 and order[i] > -4:
            ways.append(0)
        if order[i] >= 0 and order[i] < 3:
            ways.append(1)
        return ways

    def w_step(i):
        if i > 0:
            local_wait(w_rows(ring_z(i)), w_recv.at[ring_z(i)])
        for way in z_ways(i):
            w_send_z(i, way).start()

    @pl.when(even)
    def _():
        w_step(0)

    def send_taps(ks):
        for k in ks:
            for xx in range(NX):
                @pl.when(elsewhere(k, xx))
                def _():
                    tap_copy(k, xx).start()

                @pl.when(jnp.logical_not(elsewhere(k, xx)))
                def _():
                    slot = (k % 2) * SECTIONS + s
                    pltpu.make_async_copy(tap_src(k, xx), tap_cell(x, slot), tap_recv.at[x, slot]).start()

    send_taps(range(2))
    pad_taps(2, 8)

    def pass_turn(k):
        pl.semaphore_signal(gate_sem.at[k], inc=1, device_id={"dp": dp, "section": s + 1}, device_id_type=MESH)

    @pl.when(even)
    def _():
        for i in range(1, NZ // 2 + 1):
            w_step(i)
        pass_turn(2)
        send_taps(range(2, 8))
        for i in range(NZ // 2 + 1, NZ):
            w_step(i)
        pass_turn(0)

    @pl.when(jnp.logical_not(even))
    def _():
        pl.semaphore_wait(gate_sem.at[2], 1)
        send_taps(range(2, 8))
        pl.semaphore_wait(gate_sem.at[0], 1)
        for i in range(NZ):
            w_step(i)

    def oh_rows(r):
        return oh.at[pl.ds(pl.multiple_of(r * COLS, COLS), COLS), :]

    def oh_src(img):
        return oh_own.at[img // 2, pl.ds((img % 2) * COLS, COLS), :]

    def oh_copy(img):
        return remote(oh_src(img), oh_rows(z % 4), oh_send.at[img], oh_recv.at[z % 4], home(img), s)

    @pl.when(is_last)
    def _():
        sub = lax.broadcasted_iota(jnp.int32, (CPAD, 2 * COLS), 0)
        tile_of = lax.broadcasted_iota(jnp.int32, (CPAD, 2 * COLS), 1) // COLS
        for micro in range(2):
            count = counts_ref[0, micro]
            share = 1.0 / (count.astype(F32) * (COLS * GROUPS * 2))
            weight = jnp.where(tile_of < count, share, 0.0)
            hot = jnp.where(sub == labels_ref[micro:micro + 1, :], 1.0, 0.0)
            oh_own[micro] = jnp.where(sub == CPAD - 1, weight, hot).T.astype(BF16)
        for img in range(4):
            @pl.when(home(img) != dp)
            def _():
                oh_copy(img).start()

            @pl.when(home(img) == dp)
            def _():
                pltpu.make_async_copy(oh_src(img), oh_rows(z % 4), oh_recv.at[z % 4]).start()

    @pl.when(jnp.logical_not(has_up))
    def _():
        ext[0:COLS, :] = jnp.zeros((COLS, CH), BF16)

    @pl.when(jnp.logical_not(has_down))
    def _():
        ext[COLS + PIX:, :] = jnp.zeros((COLS, CH), BF16)

    @pl.when(even)
    def _():
        for xx in range(NX):
            for j in range(2 * SECTIONS):
                local_wait(tap_cell(xx, j), tap_recv.at[xx, j])
            tap_pass(xx).start()

    @pl.when(jnp.logical_not(even))
    def _():
        for xx in range(NX):
            local_wait(taps_all.at[xx], pass_recv.at[xx])

    first_rows, last_rows = pl.ds(0, FARROWS), pl.ds(FARROWS, FARROWS)
    half_rows = (first_rows, last_rows)

    def far_copy(way):
        return remote(
            lat_send.at[2, half_rows[way]], lat_far.at[way], lf_send.at[way], lf_recv.at[way],
            right if way == 0 else left, s,
        )

    def near_copy(way, part):
        return remote(
            lat_send.at[way, half_rows[part]], lat_near.at[way, half_rows[part]],
            ln_send.at[way, part], ln_recv.at[way, part], right if way == 0 else left, s,
        )

    lat_send[2] = nn(taps_all[x_far], wl[...]).astype(BF16)

    @pl.when(jnp.logical_not(even))
    def _():
        pl.semaphore_wait(gate_sem.at[1], 1)

    for way in range(2):
        far_copy(way).start()
    for way in range(2):
        acc[way] = nn(taps_all[x_right if way == 0 else x_left], wl[...])
        rows = half_rows[1 - way]
        lat_send[way, rows] = acc[way, rows].astype(BF16)
        near_copy(way, 1 - way).start()
    acc[2] = nn(taps_all[x], wl[...])
    for way in range(2):
        rows = half_rows[way]
        local_wait(lat_far.at[way], lf_recv.at[way])
        lat_send[way, rows] = (acc[way, rows] + lat_far[way].astype(F32)).astype(BF16)
        near_copy(way, way).start()
    for part in range(2):
        rows = half_rows[part]
        for way in (1 - part, part):
            local_wait(lat_near.at[way, rows], ln_recv.at[way, part])
        lat_nat[rows] = (
            acc[2, rows] + lat_near[0, rows].astype(F32) + lat_near[1, rows].astype(F32)
        ).astype(BF16)

    @pl.when(even)
    def _():
        pass_turn(1)

    def band(ref, j):
        return ref.at[pl.ds(pl.multiple_of(j * COLS, COLS), COLS), :]

    def lat_copy(img):
        return remote(band(lat_nat, img), band(lat_img, z % 4), lz_send.at[img], lz_recv.at[z % 4], home(img), s)

    for img in range(4):
        @pl.when(home(img) != dp)
        def _():
            lat_copy(img).start()

        @pl.when(home(img) == dp)
        def _():
            pltpu.make_async_copy(band(lat_nat, img), band(lat_img, z % 4), lz_recv.at[z % 4]).start()

    for r in range(4):
        local_wait(band(lat_img, r), lz_recv.at[r])

    def lat_up():
        return remote(band(lat_img, 0), lat_halo.at[1], lh_send.at[0], lh_recv.at[1], up, s)

    def lat_down():
        return remote(band(lat_img, ROWS - 1), lat_halo.at[0], lh_send.at[1], lh_recv.at[0], down, s)

    @pl.when(jnp.logical_and(has_up, jnp.logical_not(even)))
    def _():
        lat_up().start()

    @pl.when(jnp.logical_and(has_down, jnp.logical_not(even)))
    def _():
        lat_down().start()

    w_copy.wait()

    def lanes(c):
        return pl.ds(c * CK, CK)

    def x_copy(c):
        return pltpu.make_async_remote_copy(
            src_ref=xout.at[:, lanes(c)], dst_ref=xin.at[:, lanes(c)],
            send_sem=x_send.at[c], recv_sem=x_recv.at[c],
            device_id={"dp": dp, "section": s + 1}, device_id_type=MESH,
        )

    def halo_up(c):
        return pltpu.make_async_remote_copy(
            src_ref=ext.at[pl.ds(COLS, COLS), lanes(c)], dst_ref=ext.at[pl.ds(COLS + PIX, COLS), lanes(c)],
            send_sem=halo_send.at[0, c], recv_sem=halo_recv.at[1, c],
            device_id={"dp": up, "section": s}, device_id_type=MESH,
        )

    def halo_down(c):
        return pltpu.make_async_remote_copy(
            src_ref=ext.at[pl.ds(PIX, COLS), lanes(c)], dst_ref=ext.at[pl.ds(0, COLS), lanes(c)],
            send_sem=halo_send.at[1, c], recv_sem=halo_recv.at[0, c],
            device_id={"dp": down, "section": s}, device_id_type=MESH,
        )

    def edge_up(c):
        return remote(
            xout.at[pl.ds(0, COLS), lanes(c)], x_halo.at[1, :, lanes(c)],
            xh_send.at[0, c], xh_recv.at[1, c], up, s + 1,
        )

    def edge_down(c):
        return remote(
            xout.at[pl.ds(PIX - COLS, COLS), lanes(c)], x_halo.at[0, :, lanes(c)],
            xh_send.at[1, c], xh_recv.at[0, c], down, s + 1,
        )

    def take_edges(c):
        cols = slice(c * CK, (c + 1) * CK)
        for side, flag, rows in ((0, has_up, slice(0, COLS)), (1, has_down, slice(COLS + PIX, 2 * COLS + PIX))):
            @pl.when(flag)
            def _():
                local_wait(x_halo.at[side, :, lanes(c)], xh_recv.at[side, c])
                ext[rows, cols] = (
                    x_halo[side, :, cols].astype(F32) + lat_halo[side, :, cols].astype(F32)
                ).astype(BF16)

    def take_x(c):
        cols = slice(c * CK, (c + 1) * CK)

        @pl.when(is_first)
        def _():
            ext[COLS:COLS + PIX, cols] = lat_img[:, cols]

        @pl.when(s > 0)
        def _():
            local_wait(xin.at[:, lanes(c)], x_recv.at[c])
            ext[COLS:COLS + PIX, cols] = (xin[:, cols].astype(F32) + lat_img[:, cols].astype(F32)).astype(BF16)

        @pl.when(jnp.logical_and(has_up, even))
        def _():
            halo_up(c).start()

        @pl.when(jnp.logical_and(has_down, even))
        def _():
            halo_down(c).start()

    def wait_halo(c):
        @pl.when(has_up)
        def _():
            local_wait(ext.at[pl.ds(0, COLS), lanes(c)], halo_recv.at[0, c])

        @pl.when(has_down)
        def _():
            local_wait(ext.at[pl.ds(COLS + PIX, COLS), lanes(c)], halo_recv.at[1, c])

    def conv_part(c, dr, dc, ncols):
        rows = (1 + dr) * COLS
        return nn(
            ext[rows:rows + PIX, c * CK:(c + 1) * CK],
            w[(dr + 1) * 3 + dc + 1, c * CK:(c + 1) * CK, ncols],
        )

    every = slice(0, CH)

    def conv_inner(c, start):
        for dc in (-1, 0, 1):
            term = conv_part(c, 0, dc, every)
            if start:
                acc[dc + 1] = term
            else:
                acc[dc + 1] += term

    def conv_outer(c):
        for dc in (-1, 0, 1):
            acc[dc + 1] += conv_part(c, -1, dc, every) + conv_part(c, 1, dc, every)

    col = lax.broadcasted_iota(jnp.int32, (PIX, CK), 0) % COLS

    def before(v):
        return jnp.where(col == 0, 0.0, pltpu.roll(v, 1, 0))

    def after(v):
        return jnp.where(col == COLS - 1, 0.0, pltpu.roll(v, PIX - 1, 0))

    def conv_finish(n, chunks, direct):
        ncols = slice(n * CK, (n + 1) * CK)
        parts = []
        for dc in (-1, 0, 1):
            part = acc[dc + 1, :, ncols]
            for c in chunks:
                part += conv_part(c, -1, dc, ncols) + conv_part(c, 1, dc, ncols)
            parts.append(part)
        pre = before(parts[0]) + parts[1] + after(parts[2])
        sig = 1.0 / (1.0 + jnp.exp(-pre))
        xout[:, ncols] = (pre * sig).astype(BF16)

        @pl.when(s < SECTIONS - 1)
        def _():
            x_copy(n).start()

        if direct:
            @pl.when(has_up)
            def _():
                edge_up(n).start()

            @pl.when(has_down)
            def _():
                edge_down(n).start()

        dsilu[:, ncols] = sig * (1.0 + pre * (1.0 - sig))

    @pl.when(even)
    def _():
        take_x(0)
        conv_inner(0, True)
        take_x(1)
        conv_inner(1, False)
        wait_halo(0)
        conv_outer(0)
        take_x(2)
        conv_inner(2, False)
        wait_halo(1)
        conv_outer(1)
        wait_halo(2)
        for n in range(NCH):
            conv_finish(n, (2,), True)

    @pl.when(jnp.logical_not(even))
    def _():
        for c in range(NCH):
            take_x(c)
        for c in range(NCH):
            conv_inner(c, c == 0)

        @pl.when(has_up)
        def _():
            local_wait(lat_halo.at[0], lh_recv.at[0])

        @pl.when(has_down)
        def _():
            local_wait(lat_halo.at[1], lh_recv.at[1])

        for c in range(NCH):
            take_edges(c)
        for n in range(NCH):
            conv_finish(n, range(NCH), False)

    def gather_copy(buf, kind, way):
        return remote(
            buf.at[x], buf.at[x], a_send.at[kind, way], a_recv.at[kind, way], right if way == 0 else left, s
        )

    def gather_far(buf, kind, way):
        rows = buf.shape[1] // 2
        block = buf.at[x_left if way == 0 else x_right, pl.ds(way * rows, rows), :]
        return remote(
            block, block, a_send.at[kind, 2 + way], a_recv.at[kind, 2 + way], right if way == 0 else left, s
        )

    def gather_start(buf, kind):
        for way in range(2):
            gather_copy(buf, kind, way).start()

    def gather_forward(buf, kind):
        for way in range(2):
            local_wait(buf.at[x_left if way == 0 else x_right], a_recv.at[kind, way])
            gather_far(buf, kind, way).start()

    def gather_finish(buf, kind):
        rows = buf.shape[1] // 2
        for way in range(2):
            local_wait(buf.at[x_far, pl.ds(way * rows, rows), :], a_recv.at[kind, 2 + way])

    def gather_sent(buf, kind):
        for way in range(2):
            gather_copy(buf, kind, way).wait_send()
            gather_far(buf, kind, way).wait_send()

    def early_start():
        ext_all[x] = ext[...]
        gather_start(ext_all, 2)

    def early_finish():
        gather_finish(ext_all, 2)

        @pl.loop(0, NX)
        def _(src):
            lanes_of = pl.ds(pl.multiple_of(src * PIX, PIX), PIX)
            for dr in range(3):
                cols_t[dr, :, lanes_of] = ext_all[src, dr * COLS:dr * COLS + PIX, :].T
            taps_t[:, lanes_of] = taps_all[src].T

    @pl.when(jnp.logical_and(s < 6, s % 2 == 1))
    def _():
        pl.semaphore_signal(early_sem, inc=1, device_id={"dp": dp, "section": s - 1}, device_id_type=MESH)

    @pl.when(jnp.logical_and(s < 6, s % 2 == 0))
    def _():
        pl.semaphore_wait(early_sem, 1)

    @pl.when(s < 6)
    def _():
        early_start()

    @pl.when(s < 4)
    def _():
        gather_forward(ext_all, 2)
        early_finish()

    @pl.when(is_last)
    def _():
        for r in range(4):
            local_wait(oh_rows(r), oh_recv.at[r])
        cls_copy.wait()
        logits = nt(xout[...], cls_ref[...])
        spot = lax.broadcasted_iota(jnp.int32, (PIX, CPAD), 1)
        expo = jnp.exp(logits)
        probs = expo / jnp.sum(expo, axis=-1, keepdims=True)
        marks = oh[...].astype(F32)
        weight = jnp.sum(jnp.where(spot == CPAD - 1, marks, 0.0), axis=-1, keepdims=True)
        grad_logits = ((probs - marks[:, :CLASSES]) * weight).astype(BF16)
        gx[...] = nn(grad_logits, cls_ref[...])

    def g_copy(c):
        return pltpu.make_async_remote_copy(
            src_ref=g_out.at[:, lanes(c)], dst_ref=gin.at[:, lanes(c)],
            send_sem=g_send.at[c], recv_sem=g_recv.at[c],
            device_id={"dp": dp, "section": s - 1}, device_id_type=MESH,
        )

    def rim_up(c):
        return pltpu.make_async_remote_copy(
            src_ref=rim_out.at[0, :, lanes(c)], dst_ref=rim_in.at[1, :, lanes(c)],
            send_sem=rim_send.at[0, c], recv_sem=rim_recv.at[1, c],
            device_id={"dp": up, "section": s}, device_id_type=MESH,
        )

    def rim_down(c):
        return pltpu.make_async_remote_copy(
            src_ref=rim_out.at[1, :, lanes(c)], dst_ref=rim_in.at[0, :, lanes(c)],
            send_sem=rim_send.at[1, c], recv_sem=rim_recv.at[0, c],
            device_id={"dp": down, "section": s}, device_id_type=MESH,
        )

    def take_g(c):
        cols = slice(c * CK, (c + 1) * CK)

        @pl.when(s < SECTIONS - 1)
        def _():
            local_wait(gin.at[:, lanes(c)], g_recv.at[c])
            gx[:, cols] = gin[:, cols].astype(F32)

        for side, flag, rows in ((0, has_up, slice(0, COLS)), (1, has_down, slice(PIX - COLS, PIX))):
            @pl.when(jnp.logical_and(flag, even))
            def _():
                local_wait(g_rim.at[side, :, lanes(c)], gr_recv.at[side, c])
                gx[rows, cols] += g_rim[side, :, cols].astype(F32)

        grad_pre = (gx[:, cols] * dsilu[:, cols]).astype(BF16).astype(F32)
        gpv[0, :, cols] = after(grad_pre).astype(BF16)
        gpv[1, :, cols] = grad_pre.astype(BF16)
        gp_all[x, :, cols] = grad_pre.astype(BF16)
        gpv[2, :, cols] = before(grad_pre).astype(BF16)

    def back_part(c, dr, krows):
        total = None
        for dc in (-1, 0, 1):
            term = nt(
                gpv[dc + 1, :, c * CK:(c + 1) * CK],
                w[(dr + 1) * 3 + dc + 1, krows, c * CK:(c + 1) * CK],
            )
            total = term if total is None else total + term
        return total

    def rim_direct_up(c):
        return remote(
            rim_out.at[0, :, lanes(c)], g_rim.at[1, :, lanes(c)], gr_send.at[0, c], gr_recv.at[1, c], up, s - 1
        )

    def rim_direct_down(c):
        return remote(
            rim_out.at[1, :, lanes(c)], g_rim.at[0, :, lanes(c)], gr_send.at[1, c], gr_recv.at[0, c], down, s - 1
        )

    def send_rims(n, upward, downward):
        @pl.when(has_up)
        def _():
            upward(n).start()

        @pl.when(has_down)
        def _():
            downward(n).start()

    def back_rims(n, chunks, start):
        ncols = slice(n * CK, (n + 1) * CK)
        for side, dr in ((0, -1), (2, 1)):
            total = None if start else acc[side, :, ncols]
            for c in chunks:
                term = back_part(c, dr, ncols)
                total = term if total is None else total + term
            acc[side, :, ncols] = total
            if dr < 0:
                rim_out[0, :, ncols] = total[0:COLS].astype(BF16)
            else:
                rim_out[1, :, ncols] = total[PIX - COLS:].astype(BF16)

    def back_inner(n, chunks, start):
        ncols = slice(n * CK, (n + 1) * CK)
        total = None if start else acc[1, :, ncols]
        for c in chunks:
            term = back_part(c, 0, ncols)
            total = term if total is None else total + term
        acc[1, :, ncols] = total
        acc[1, 0:PIX - COLS, ncols] += acc[0, COLS:, ncols]
        acc[1, COLS:, ncols] += acc[2, 0:PIX - COLS, ncols]

    def add_rims(n):
        ncols = slice(n * CK, (n + 1) * CK)

        @pl.when(has_up)
        def _():
            local_wait(rim_in.at[0, :, lanes(n)], rim_recv.at[0, n])
            acc[1, 0:COLS, ncols] += rim_in[0, :, ncols].astype(F32)

        @pl.when(has_down)
        def _():
            local_wait(rim_in.at[1, :, lanes(n)], rim_recv.at[1, n])
            acc[1, PIX - COLS:, ncols] += rim_in[1, :, ncols].astype(F32)

        gs_img[:, ncols] = acc[1, :, ncols].astype(BF16)

    def send_g(n):
        ncols = slice(n * CK, (n + 1) * CK)
        g_out[:, ncols] = acc[1, :, ncols].astype(BF16)
        g_copy(n).start()

    @pl.when(jnp.logical_not(even))
    def _():
        take_g(0)
        for dr in (-1, 0, 1):
            acc[dr + 1] = back_part(0, dr, every)
        take_g(1)
        for dr in (-1, 0, 1):
            acc[dr + 1] += back_part(1, dr, every)
        take_g(2)
        for n in range(NCH):
            back_rims(n, (2,), False)
            send_rims(n, rim_direct_up, rim_direct_down)
            back_inner(n, (2,), False)
            send_g(n)
        for n in range(NCH):
            send_rims(n, rim_up, rim_down)

        @pl.when(s == 1)
        def _():
            gather_start(gp_all, 0)

        for n in range(NCH):
            add_rims(n)

        @pl.when(s > 1)
        def _():
            pl.semaphore_wait(gate_sem.at[3], 1)
            gather_start(gp_all, 0)

    @pl.when(even)
    def _():
        def finish(n):
            back_inner(n, chunks, True)
            add_rims(n)

            @pl.when(s > 0)
            def _():
                send_g(n)

        for c in range(NCH):
            take_g(c)

        @pl.when(is_first)
        def _():
            gather_start(gp_all, 0)

        chunks = range(NCH)
        back_rims(0, chunks, True)
        send_rims(0, rim_up, rim_down)
        back_rims(1, chunks, True)
        send_rims(1, rim_up, rim_down)
        finish(0)
        back_rims(2, chunks, True)
        send_rims(2, rim_up, rim_down)
        finish(1)
        finish(2)

        @pl.when(s > 0)
        def _():
            pass_turn(3)

    def gz_copy(r):
        return remote(
            band(gs_img, r), band(gs_all.at[x], image), gz_send.at[r], gz_recv.at[image], native(r), s
        )

    for r in range(4):
        @pl.when(native(r) != dp)
        def _():
            gz_copy(r).start()

        @pl.when(native(r) == dp)
        def _():
            pltpu.make_async_copy(band(gs_img, r), band(gs_all.at[x], image), gz_recv.at[image]).start()

    @pl.when(jnp.logical_and(even, s > 0))
    def _():
        gather_start(gp_all, 0)

    @pl.when(s >= 6)
    def _():
        early_start()

    gather_forward(gp_all, 0)

    @pl.when(s >= 4)
    def _():
        gather_forward(ext_all, 2)

    whole_col = lax.broadcasted_iota(jnp.int32, (PIX, CH), 0) % COLS

    def spread(src):
        rows = pl.ds(pl.multiple_of(src * PIX, PIX), PIX)
        value = gp_all[src].astype(F32)
        gpv_all[0, rows, :] = jnp.where(whole_col == COLS - 1, 0.0, pltpu.roll(value, PIX - 1, 0)).astype(BF16)
        gpv_all[1, rows, :] = gp_all[src]
        gpv_all[2, rows, :] = jnp.where(whole_col == 0, 0.0, pltpu.roll(value, 1, 0)).astype(BF16)

    spread(x)
    spread(x_left)
    spread(x_right)
    gather_finish(gp_all, 0)
    for img in range(4):
        local_wait(band(gs_all.at[x], img), gz_recv.at[img])
    gather_start(gs_all, 1)
    spread(x_far)

    @pl.when(s >= 4)
    def _():
        early_finish()

    def conv_unit(u):
        unit = 9 * x + u
        o = unit // 4
        chans = pl.ds(pl.multiple_of((unit % 4) * UNIT, UNIT), UNIT)
        part_c[pl.ds(pl.multiple_of(u * UNIT, UNIT), UNIT), :] = nn(cols_t[o // 3, chans, :], gpv_all[o % 3])

    def conv_slice(zz):
        @pl.loop(0, 2)
        def _(k):
            conv_unit(zz + k)

    def slice_at(way, t):
        return (z + NZ - 1 - t) % NZ if way == 0 else (z + 1 + t) % NZ

    def own_rows(part, rows, way, t):
        at = pl.ds(pl.multiple_of(slice_at(way, t) * rows, 8), rows)
        return part[at, way * HALF:(way + 1) * HALF]

    def hop(ring, send, recv, way, t):
        return pltpu.make_async_remote_copy(
            src_ref=ring.at[way, t], dst_ref=ring.at[way, t + 1],
            send_sem=send.at[way, t], recv_sem=recv.at[way, t],
            device_id={"dp": z_next if way == 0 else z_prev, "section": s}, device_id_type=MESH,
        )

    conv_ring = (ring_c, rc_send, rc_recv)
    lat_ring = (ring_l, rl_send, rl_recv)
    def ring_start(ring, part, rows):
        for way in range(2):
            ring[0][way, 0] = own_rows(part, rows, way, 0).astype(BF16)
            hop(*ring, way, 0).start()

    def ring_step(ring, part, rows, out, t):
        buf = ring[0]
        for way in range(2):
            local_wait(buf.at[way, t + 1], ring[2].at[way, t])
            total = buf[way, t + 1].astype(F32) + own_rows(part, rows, way, t + 1)
            if t < NZ - 2:
                buf[way, t + 1] = total.astype(BF16)
                hop(*ring, way, t + 1).start()
            else:
                out[:, way * HALF:(way + 1) * HALF] = total[0:out.shape[0]]

    def conv_step(t):
        ring_step(conv_ring, part_c, CROWS, conv_out, t)

    def lat_step(t):
        ring_step(lat_ring, part_l, KPAD, lat_out, t)

    @pl.loop(0, 2)
    def _(k):
        conv_slice((z + 1 + k * (NZ - 2)) % NZ)

    ring_start(conv_ring, part_c, CROWS)

    @pl.loop(0, 2)
    def _(k):
        conv_slice((z + 2 + k * (NZ - 4)) % NZ)

    gather_forward(gs_all, 1)
    conv_step(0)

    @pl.loop(0, 2)
    def _(k):
        conv_slice((z + 3 + k * (NZ - 6)) % NZ)

    gather_finish(gs_all, 1)
    part_l[...] = nn(taps_t[...], gs_all[...].reshape(WIDE, CH))
    ring_start(lat_ring, part_l, KPAD)
    conv_step(1)

    @pl.loop(0, 2)
    def _(k):
        conv_slice((z + 4 * k) % NZ)

    lat_step(0)
    for t in range(2, NZ - 1):
        conv_step(t)
        lat_step(t - 1)
    lat_step(NZ - 2)

    for k in range(8):
        for xx in range(NX):
            @pl.when(elsewhere(k, xx))
            def _():
                tap_copy(k, xx).wait_send()

    @pl.when(even)
    def _():
        for xx in range(NX):
            tap_pass(xx).wait_send()

    for i in range(NZ):
        for way in z_ways(i):
            w_send_z(i, way).wait_send()
    for way in range(2):
        far_copy(way).wait_send()
        for part in range(2):
            near_copy(way, part).wait_send()
    for r in range(4):
        @pl.when(home(r) != dp)
        def _():
            lat_copy(r).wait_send()

    @pl.when(is_last)
    def _():
        for img in range(4):
            @pl.when(home(img) != dp)
            def _():
                oh_copy(img).wait_send()

    for c in range(NCH):
        @pl.when(s < SECTIONS - 1)
        def _():
            x_copy(c).wait_send()

        @pl.when(s > 0)
        def _():
            g_copy(c).wait_send()

        @pl.when(has_up)
        def _():
            rim_up(c).wait_send()

        @pl.when(has_down)
        def _():
            rim_down(c).wait_send()

        @pl.when(jnp.logical_and(has_up, even))
        def _():
            halo_up(c).wait_send()
            edge_up(c).wait_send()

        @pl.when(jnp.logical_and(has_down, even))
        def _():
            halo_down(c).wait_send()
            edge_down(c).wait_send()

        @pl.when(jnp.logical_and(has_up, jnp.logical_not(even)))
        def _():
            rim_direct_up(c).wait_send()

        @pl.when(jnp.logical_and(has_down, jnp.logical_not(even)))
        def _():
            rim_direct_down(c).wait_send()

    @pl.when(jnp.logical_and(has_up, jnp.logical_not(even)))
    def _():
        lat_up().wait_send()

    @pl.when(jnp.logical_and(has_down, jnp.logical_not(even)))
    def _():
        lat_down().wait_send()

    for kind, buf in enumerate((gp_all, gs_all, ext_all)):
        gather_sent(buf, kind)
    for r in range(4):
        @pl.when(native(r) != dp)
        def _():
            gz_copy(r).wait_send()

    for way in range(2):
        for t in range(NZ - 1):
            hop(*conv_ring, way, t).wait_send()
            hop(*lat_ring, way, t).wait_send()


def head_call(taps, lat, w, cls, counts, labels):
    dma = pltpu.SemaphoreType.DMA
    hbm = pl.BlockSpec(memory_space=pl.ANY)
    vmem = pl.BlockSpec(memory_space=pltpu.VMEM)
    smem = pl.BlockSpec(memory_space=pltpu.SMEM)
    return pl.pallas_call(
        head_kernel,
        out_shape=(
            jax.ShapeDtypeStruct((CROWS, CH), F32),
            jax.ShapeDtypeStruct((KROWS, CH), F32),
        ),
        in_specs=[vmem, vmem, hbm, hbm, smem, vmem],
        out_specs=(vmem, vmem),
        scratch_shapes=[
            pltpu.VMEM((CLASSES, CH), BF16),
            pltpu.VMEM((8, 16, KW), BF16),
            pltpu.VMEM((XL, CH), BF16),
            pltpu.VMEM((9, CH, CH), BF16),
            pltpu.VMEM((PIX, CH), F32),
            pltpu.VMEM((3, PIX, CH), BF16),
            pltpu.VMEM((2, FARROWS, CH), BF16),
            pltpu.VMEM((2, PIX, CH), BF16),
            pltpu.VMEM((PIX, CH), BF16),
            pltpu.VMEM((PIX, CH), BF16),
            pltpu.VMEM((PIX + 2 * COLS, CH), BF16),
            pltpu.VMEM((PIX, CH), BF16),
            pltpu.VMEM((PIX, CH), BF16),
            pltpu.VMEM((PIX, CH), BF16),
            pltpu.VMEM((PIX, CH), F32),
            pltpu.VMEM((3, PIX, CH), F32),
            pltpu.VMEM((3, PIX, CH), BF16),
            pltpu.VMEM((2, COLS, CH), BF16),
            pltpu.VMEM((2, COLS, CH), BF16),
            pltpu.VMEM((2, 2 * COLS, CPAD), BF16),
            pltpu.VMEM((PIX, CPAD), BF16),
            pltpu.VMEM((2, COLS, CH), BF16),
            pltpu.VMEM((2, COLS, CH), BF16),
            pltpu.VMEM((PIX, CH), BF16),
            pltpu.VMEM((2, COLS, CH), BF16),
            pltpu.VMEM((NX, PIX + 2 * COLS, CH), BF16),
            pltpu.VMEM((NX, PIX, XL), BF16),
            pltpu.VMEM((PIX, CH), BF16),
            pltpu.VMEM((NX, PIX, CH), BF16),
            pltpu.VMEM((NX, PIX, CH), BF16),
            pltpu.VMEM((3, WIDE, CH), BF16),
            pltpu.VMEM((3, CH, WIDE), BF16),
            pltpu.VMEM((XL, WIDE), BF16),
            pltpu.VMEM((XC, CH), F32),
            pltpu.VMEM((XL, CH), F32),
            pltpu.VMEM((2, NZ, CROWS, HALF), BF16),
            pltpu.VMEM((2, NZ, KPAD, HALF), BF16),
            pltpu.SemaphoreType.REGULAR((4,)),
            dma((2,)),
            dma((8, NX)),
            dma((NX, 2 * SECTIONS)),
            dma((NX,)),
            dma((NX,)),
            dma((2, NZ)),
            dma((NZ,)),
            dma((2,)),
            dma((2,)),
            dma((2, 2)),
            dma((2, 2)),
            dma((4,)),
            dma((4,)),
            dma((4,)),
            dma((4,)),
            dma((NCH,)),
            dma((NCH,)),
            dma((2, NCH)),
            dma((2, NCH)),
            dma((NCH,)),
            dma((NCH,)),
            dma((2, NCH)),
            dma((2, NCH)),
            dma((2,)),
            dma((2,)),
            dma((2, NCH)),
            dma((2, NCH)),
            dma((2, NCH)),
            dma((2, NCH)),
            pltpu.SemaphoreType.REGULAR,
            dma((4,)),
            dma((4,)),
            dma((3, 4)),
            dma((3, 4)),
            dma((2, NZ - 1)),
            dma((2, NZ - 1)),
            dma((2, NZ - 1)),
            dma((2, NZ - 1)),
        ],
        compiler_params=pltpu.CompilerParams(
            collective_id=0, has_side_effects=True, vmem_limit_bytes=62 << 20
        ),
    )(taps, lat, w, cls, counts, labels)


def on_device(tap_maps, lateral_weight, conv_weight, classifier, tile_counts, labels):
    levels, micros, here, width = tap_maps.shape
    taps = tap_maps.reshape(levels * micros, here, width)
    conv_grad, lateral_grad = head_call(
        taps, lateral_weight[0], conv_weight.reshape(9, CH, CH), classifier.T, tile_counts, labels
    )
    return (conv_grad[None], lateral_grad[None])


def solution(mesh):
    placed = (
        P(None, None, ("dp", "section"), None),
        P("section", "dp", None),
        P("section", None, None),
        P(),
        P("dp", None),
        P(None, "dp"),
    )
    return jax.shard_map(
        on_device,
        mesh=mesh,
        in_specs=placed,
        out_specs=(P("section", "dp", None), P("section", "dp", None)),
        check_vma=False,
    )
```
